32 devices in a mesh: dp: 8 (over y, x, core), tensor: 4 (over z).
Axes of the slice: x: 2, y: 2, z: 4, core: 2. Of those that a mesh axis runs over, the one named last changes fastest.
Arguments:
- inputs: bfloat16 [16384, 768], P(('dp', 'tensor')), may hold values from -6 to 6
- segment_ids: int32 [16, 1024], P('dp'), may hold values from 0 to 15, never falling along the last dimension, each value on 1 to 512 neighbouring positions
- qkv_weight: bfloat16 [768, 2304], P(('dp', 'tensor')), may hold values from -0.21875 to 0.21875
- out_weight: bfloat16 [768, 768], P(('dp', 'tensor')), may hold values from -0.875 to 0.875
- norm_gains: bfloat16 [2, 768], P(None, ('dp', 'tensor')), may hold values from 0.25 to 1.75
- norm_biases: bfloat16 [2, 768], P(None, ('dp', 'tensor')), may hold values from -3 to 3
- gate_weight: bfloat16 [768, 3072], P('dp', 'tensor'), may hold values from -0.21875 to 0.21875
- up_weight: bfloat16 [768, 3072], P('dp', 'tensor'), may hold values from -0.21875 to 0.21875
- down_weight: bfloat16 [3072, 768], P('tensor', 'dp'), may hold values from -0.109375 to 0.109375
- out_grad: bfloat16 [16384, 768], P(('dp', 'tensor')), may hold values from -6 to 6
Outputs:
- outputs: bfloat16 [16384, 768], P(('dp', 'tensor'))
- inputs_grad: float32 [16384, 768], P(('dp', 'tensor'))
- qkv_weight_grad: float32 [768, 2304], P(('dp', 'tensor'))
- out_weight_grad: float32 [768, 768], P(('dp', 'tensor'))
- norm_gains_grad: float32 [2, 768], P(None, ('dp', 'tensor'))
- norm_biases_grad: float32 [2, 768], P(None, ('dp', 'tensor'))
- gate_weight_grad: float32 [768, 3072], P('dp', 'tensor')
- up_weight_grad: float32 [768, 3072], P('dp', 'tensor')
- down_weight_grad: float32 [3072, 768], P('tensor', 'dp')
The draws below stay inside these ranges and needn't reach their ends.
Inputs may be any that keep to these rules, and one draw needn't show every extreme that they name: `segment_ids`: in each row the document numbers never fall; every document of 0 to 15 covers 1 to 512 consecutive tokens, and some row holds one of exactly 512.
All inputs are finite; a program needn't handle non-finite values.
Results may differ from the reference program's by a relative error of at most 0.015.
Values may be sent and summed in bfloat16 or wider, within the bound.
No kernel may reach another device: no remote copies, remote signals or barrier semaphores. Data moves between devices by JAX's collectives and lax.ppermute only.
A program may use at most 256 MiB of HBM per device.

```python
import math
import jax
import jax.numpy as jnp
import numpy as np
from jax import lax

D = 768
H = 12
HD = 64
FF = 3072
SEQ = 1024
DOCS = 16
MOST = 512
QBLK = 512
NROWS = 16
TOKENS = 16384


def level_of(rng, dims, split, least, largest):
    loudness = 1.0
    for dim, parts in split:
        heights = jax.random.uniform(jax.random.fold_in(jax.random.fold_in(rng, 6), dim), (parts,), jnp.float32, least / len(split), largest / len(split))
        loudness = loudness * jnp.repeat(jnp.exp(heights), dims[dim] // parts).reshape((-1,) + (1,) * (len(dims) - 1 - dim))
    return loudness


def length_profile(count, total, most, slope):
    loads = [(1 << 20) // math.isqrt(standing ** slope) + 1 for standing in range(2, count + 1)]
    surplus, given = total - most - (count - 1), [1] * (count - 1)
    while surplus > 0:
        movable = [i for i in range(count - 1) if given[i] < most]
        pool, remaining = sum([loads[i] for i in movable]), surplus
        for i in movable:
            addition = min(most - given[i], max(1, remaining * loads[i] // pool), surplus)
            given[i] = given[i] + addition
            surplus = surplus - addition
    return np.array([most] + given)


def uneven_parts(stream_key, amount, total, bound, lean):
    if amount == 2:
        one = jax.random.randint(stream_key, (), max(1, total - bound), min(bound, total - 1) + 1)
        return jnp.stack([one, total - one])
    sizes = jnp.asarray(length_profile(amount, total, bound, lean), jnp.int32)
    pairs = (amount - 1) // 2
    giver, taker = sizes[1:1 + 2 * pairs:2], sizes[2:2 + 2 * pairs:2]
    slack = jnp.minimum(giver - 1, bound - taker)
    moved = jax.random.randint(jax.random.fold_in(stream_key, 1), (pairs,), 0, 1 << 20) % (slack + 1)
    sizes = sizes.at[1:1 + 2 * pairs:2].set(giver - moved).at[2:2 + 2 * pairs:2].set(taker + moved)
    return sizes[jax.random.permutation(jax.random.fold_in(stream_key, 2), amount)]


def noise(stream_key, dims, width, most, split=(), kind=jnp.bfloat16):
    values = width * jax.random.normal(stream_key, dims, jnp.float32)
    if split:
        values = values * level_of(stream_key, dims, split, -0.22, 0.18)
    return jnp.clip(values, -most, most).astype(kind)


def setup_inputs(seed: int = 0) -> dict:
    key_list = jax.random.split(jax.random.key(seed), 11)
    return {
        "inputs": noise(key_list[0], (TOKENS, D), 1.0, 6.0, ((0, 32),)),
        "segment_ids": jax.vmap(lambda own: jnp.searchsorted(jnp.cumsum(uneven_parts(own, DOCS, SEQ, MOST, 2)), jnp.arange(SEQ), side="right"))(jax.random.split(key_list[1], NROWS)).reshape((NROWS, SEQ)).astype(jnp.int32),
        "qkv_weight": noise(key_list[2], (D, 3 * D), D ** -0.5, 0.21875, ((0, 32),)),
        "out_weight": noise(key_list[3], (D, D), (D // 16) ** -0.5, 0.875, ((0, 32),)),
        "norm_gains": jnp.clip(1.0 + 0.15 * jax.random.normal(key_list[4], (2, D), jnp.float32), 0.25, 1.75).astype(jnp.bfloat16),
        "norm_biases": noise(key_list[5], (2, D), 0.5, 3.0, ((1, 32),)),
        "gate_weight": noise(key_list[6], (D, FF), D ** -0.5, 0.21875, ((0, 8), (1, 4))),
        "up_weight": noise(key_list[7], (D, FF), D ** -0.5, 0.21875, ((0, 8), (1, 4))),
        "down_weight": noise(key_list[8], (FF, D), FF ** -0.5, 0.109375, ((0, 4), (1, 8))),
        "out_grad": noise(key_list[9], (TOKENS, D), 1.0, 6.0, ((0, 32),)),
    }


rope_base = 1000.0
layer_eps = 1e-12

@jax.custom_vjp
def low(v):
    return lax.optimization_barrier(v.astype(jnp.bfloat16)).astype(jnp.float32)

@jax.custom_vjp
def low_back(v):
    return v

def low_keep(v):
    return (low(v), None)

def low_pass(kept, grad):
    return (grad,)

def back_keep(v):
    return (v, None)

def back_low(kept, grad):
    return (low(grad),)
low.defvjp(low_keep, low_pass)
low_back.defvjp(back_keep, back_low)

def rope_tables(segments, head_size):
    length = segments.shape[-1]
    positions = jnp.arange(length, dtype=jnp.int32)
    doc_starts = jnp.concatenate([jnp.ones(segments.shape[:-1] + (1,), jnp.int32), (segments[..., 1:] != segments[..., :-1]).astype(jnp.int32)], axis=-1)
    first_index = lax.cummax(jnp.where(doc_starts > 0, positions, 0), axis=segments.ndim - 1)
    doc_place = (positions - first_index).astype(jnp.float32)
    frequency = rope_base ** (-jnp.arange(head_size // 2, dtype=jnp.float32) * 2.0 / head_size)
    angles = doc_place[..., None] * frequency
    return (jnp.cos(angles), jnp.sin(angles))

def rotate(values_in, cosine, sine_table):
    half_size = values_in.shape[-1] // 2
    first_half = values_in[..., :half_size]
    second_half = values_in[..., half_size:]
    return jnp.concatenate([first_half * cosine - second_half * sine_table, second_half * cosine + first_half * sine_table], axis=-1)

def layer_norm(summed, gain_row, bias_row):
    row_mean = lax.optimization_barrier(jnp.mean(summed, axis=-1, keepdims=True))
    centred = summed - row_mean
    inv_std = lax.rsqrt(lax.optimization_barrier(jnp.mean(centred * centred, axis=-1, keepdims=True)) + layer_eps)
    return centred * inv_std * gain_row + bias_row

def row_attention(row_item):
    queries, keys_all, values_all, segments = row_item
    score_scale = 1.0 / HD ** 0.5

    def one_block(block_start):
        query_block = lax.dynamic_slice_in_dim(queries, block_start, QBLK, 0)
        query_docs = lax.dynamic_slice_in_dim(segments, block_start, QBLK, 0)
        scores = low_back(jnp.einsum('qhd,khd->hqk', query_block, keys_all, precision=lax.Precision.HIGHEST) * score_scale)
        same_doc = (query_docs[:, None] == segments[None, :])[None]
        scores = jnp.where(same_doc, scores, -1e+30)
        row_peak = lax.optimization_barrier(jnp.max(scores, axis=-1, keepdims=True))
        exp_scores = jnp.exp(scores - row_peak)
        probs = low(exp_scores / lax.optimization_barrier(jnp.sum(exp_scores, axis=-1, keepdims=True)))
        return jnp.einsum('hqk,khd->qhd', probs, values_all, precision=lax.Precision.HIGHEST)
    block_starts = jnp.arange(SEQ // QBLK, dtype=jnp.int32) * QBLK
    blocks = lax.map(jax.checkpoint(one_block), block_starts)
    return blocks.reshape(SEQ, H, HD)

def forward(inputs, qkv_weight, out_weight, norm_gains, norm_biases, gate_weight, up_weight, down_weight, segment_ids):
    highest = lax.Precision.HIGHEST
    merged_qkv = low_back(jnp.dot(inputs, qkv_weight, precision=highest))
    merged_qkv = merged_qkv.reshape(NROWS, SEQ, 3, H, HD)
    cosine, sine_table = rope_tables(segment_ids, HD)
    cosine = cosine[:, :, None, :]
    sine_table = sine_table[:, :, None, :]
    queries = low(low_back(rotate(merged_qkv[:, :, 0], cosine, sine_table)))
    keys_all = low(low_back(rotate(merged_qkv[:, :, 1], cosine, sine_table)))
    values_all = low(merged_qkv[:, :, 2])
    attended = lax.map(row_attention, (queries, keys_all, values_all, segment_ids))
    attended = low(low_back(attended.reshape(TOKENS, D)))
    projected = low_back(jnp.dot(attended, out_weight, precision=highest))
    middle = layer_norm(inputs + projected, norm_gains[0], norm_biases[0])
    middle_low = low(middle)
    gate_act = low_back(jnp.dot(middle_low, gate_weight, precision=highest))
    up_act = low_back(jnp.dot(middle_low, up_weight, precision=highest))
    hidden = low(jax.nn.silu(gate_act) * up_act)
    ffn_out = low_back(jnp.dot(hidden, down_weight, precision=highest))
    return layer_norm(middle + ffn_out, norm_gains[1], norm_biases[1])

def reference(inputs, segment_ids, qkv_weight, out_weight, norm_gains, norm_biases, gate_weight, up_weight, down_weight, out_grad):
    floats = [a.astype(jnp.float32) for a in (inputs, qkv_weight, out_weight, norm_gains, norm_biases, gate_weight, up_weight, down_weight)]

    def layer_fn(*weights_in):
        return forward(*weights_in, segment_ids)
    outputs, pull_back = jax.vjp(layer_fn, *floats)
    grads = pull_back(out_grad.astype(jnp.float32))
    return (outputs.astype(jnp.bfloat16), grads[0], grads[1], grads[2], grads[3], grads[4], grads[5], grads[6], grads[7])
```

```python
import jax
import jax.numpy as jnp
import numpy as np
from jax import lax
from jax.experimental import pallas as pl
from jax.experimental.pallas import tpu as pltpu
from jax.sharding import PartitionSpec as P

H = 12
HD = 64
LANES = 128
PAD = 128
NEG = -1e30

rope_base = 1000.0
layer_eps = 1e-12

AXES = ("dp", "tensor")
F32 = jnp.float32
BF16 = jnp.bfloat16
VMEM_BYTES = 60 * 2**20


def params(n_axes=1):
    return pltpu.CompilerParams(
        dimension_semantics=("arbitrary",) * n_axes, vmem_limit_bytes=VMEM_BYTES
    )


def whole_block(shape):
    zeros = (0,) * len(shape)
    return pl.BlockSpec(shape, lambda *_: zeros, pipeline_mode=pl.Buffered(1))


def dot_nn(a, b):
    return lax.dot_general(a, b, (((1,), (0,)), ((), ())), preferred_element_type=F32)


def dot_nt(a, b):
    return lax.dot_general(a, b, (((1,), (1,)), ((), ())), preferred_element_type=F32)


def dot_tn(a, b):
    return lax.dot_general(a, b, (((0,), (0,)), ((), ())), preferred_element_type=F32)


def half_swap(block):
    lane = lax.broadcasted_iota(jnp.int32, block.shape, 1)
    return jnp.where(
        lane % HD < HD // 2, pltpu.roll(block, LANES - HD // 2, 1), pltpu.roll(block, HD // 2, 1)
    )


def normalise(summed):
    mean = jnp.mean(summed, axis=-1, keepdims=True)
    centred = summed - mean
    inv_std = lax.rsqrt(jnp.mean(centred * centred, axis=-1, keepdims=True) + layer_eps)
    return centred * inv_std, inv_std


def norm_back(normed, inv_std, gain, grad):
    scaled = grad * gain
    return inv_std * (
        scaled
        - jnp.mean(scaled, axis=-1, keepdims=True)
        - normed * jnp.mean(scaled * normed, axis=-1, keepdims=True)
    )


def project(x_rel, pieces, offsets, cosine, sine, pos, n_row, k_tile):
    seq, width = x_rel.shape
    rows = seq // n_row
    tile = min(256, rows)
    per_piece = rows // tile
    wide = pieces[0].shape[1]
    block_rows = pieces[0].shape[0]
    n_pieces = len(pieces)

    def true_tile(i, pos_ref):
        return (pos_ref[0] ^ (i // per_piece)) * per_piece + i % per_piece

    def body(pos_ref, offs_ref, x_ref, cos_ref, sin_ref, *rest):
        w_refs = rest[:n_pieces]
        q_ref, k_ref, v_ref, kt_ref, vt_ref, w_ref, norm_ref, w_scr = rest[n_pieces:]

        @pl.when(pl.program_id(0) == 0)
        def _():
            for p, ref in enumerate(w_refs):
                start = pl.multiple_of(offs_ref[p], 8)
                w_scr[pl.ds(start, block_rows), :] = ref[...].astype(F32)
            w_ref[...] = w_scr[...].astype(BF16)
            norm_ref[...] = jnp.transpose(w_scr[:, 4 * width : 4 * width + PAD])[:8, :]

        x = x_ref[...]
        cos = cos_ref[...]
        sin = sin_ref[...]
        merged = dot_nn(x, w_ref[:, : 3 * width])
        for b in range(width // LANES):
            cols = slice(b * LANES, (b + 1) * LANES)
            q = merged[:, b * LANES : (b + 1) * LANES]
            k = merged[:, width + b * LANES : width + (b + 1) * LANES]
            v = merged[:, 2 * width + b * LANES : 2 * width + (b + 1) * LANES]
            q = q * cos + half_swap(q) * sin
            k = k * cos + half_swap(k) * sin
            q_ref[:, cols] = (q * (HD**-0.5)).astype(BF16)
            k_ref[:, cols] = k.astype(BF16)
            v_ref[:, cols] = v.astype(BF16)
            for j in range(tile // k_tile):
                part = slice(j * k_tile, (j + 1) * k_tile)
                kt_ref[j, cols, :] = jnp.transpose(k[part, :]).astype(BF16)
                vt_ref[j, cols, :] = jnp.transpose(v[part, :]).astype(BF16)

    row_block = pl.BlockSpec((tile, width), lambda i, p, o: (true_tile(i, p), 0))
    flip_block = pl.BlockSpec(
        (tile // k_tile, width, k_tile), lambda i, p, o: (true_tile(i, p), 0, 0)
    )
    table_block = pl.BlockSpec((tile, LANES), lambda i, p, o: (true_tile(i, p), 0))
    return pl.pallas_call(
        body,
        grid_spec=pltpu.PrefetchScalarGridSpec(
            num_scalar_prefetch=2,
            grid=(seq // tile,),
            in_specs=[pl.BlockSpec((tile, width), lambda i, p, o: (i, 0)), table_block, table_block]
            + [whole_block(p.shape) for p in pieces],
            out_specs=[row_block] * 3
            + [flip_block] * 2
            + [whole_block((width, wide)), whole_block((8, width))],
            scratch_shapes=[pltpu.VMEM((width, wide), F32)],
        ),
        out_shape=[jax.ShapeDtypeStruct((seq, width), BF16)] * 3
        + [jax.ShapeDtypeStruct((seq // k_tile, width, k_tile), BF16)] * 2
        + [jax.ShapeDtypeStruct((width, wide), BF16), jax.ShapeDtypeStruct((8, width), F32)],
        compiler_params=params(),
        name="project",
    )(pos, offsets, x_rel, cosine, sine, *pieces)


def split_heads(source, target, q_tile):
    lane = lax.broadcasted_iota(jnp.int32, (q_tile, LANES), 1)
    for b in range(H // 2):
        block = source[:, b * LANES : (b + 1) * LANES].astype(F32)
        target[2 * b] = jnp.where(lane < HD, block, 0.0).astype(BF16)
        target[2 * b + 1] = jnp.where(lane < HD, 0.0, block).astype(BF16)


def attend(x_own, q, k, vt, seg_col, seg_row, key_from, key_to, weights, norms, pos, q_tile, k_tile):
    rows, width = x_own.shape
    seq = q.shape[0]
    n_own = rows // q_tile

    def body(pos_ref, from_ref, to_ref, x_ref, q_ref, k_ref, vt_ref, sc_ref, sr_ref, w_ref, norm_ref,
             att_ref, lse_ref, n_ref, istd_ref, mid_ref, qm, peak, total, acc):
        tile_index = pos_ref[0] * n_own + pl.program_id(0)
        split_heads(q_ref, qm, q_tile)
        peak[...] = jnp.full(peak.shape, NEG, F32)
        total[...] = jnp.zeros(total.shape, F32)
        acc[...] = jnp.zeros(acc.shape, F32)
        row_docs = sr_ref[0]

        def step(kt, carry):
            at = pl.multiple_of(kt * k_tile, k_tile)
            mask = sc_ref[pl.ds(at, k_tile), :] == row_docs
            for h in range(H):
                cols = slice(h // 2 * LANES, h // 2 * LANES + LANES)
                heads = slice(h * HD, (h + 1) * HD)
                s = dot_nt(k_ref[pl.ds(at, k_tile), cols], qm[h])
                s = jnp.where(mask, s, NEG)
                old = peak[h : h + 1, :]
                new = jnp.maximum(old, jnp.max(s, axis=0, keepdims=True))
                e = jnp.exp(s - new)
                fade = jnp.exp(old - new)
                peak[h : h + 1, :] = new
                total[h : h + 1, :] = total[h : h + 1, :] * fade + jnp.sum(e, axis=0, keepdims=True)
                acc[heads, :] = acc[heads, :] * fade + dot_nn(vt_ref[kt, heads, :], e.astype(BF16))
            return carry

        lax.fori_loop(from_ref[tile_index], to_ref[tile_index], step, 0)
        lse_ref[...] = peak[...] + jnp.log(total[...])
        for h in range(H):
            heads = slice(h * HD, (h + 1) * HD)
            acc[heads, :] = acc[heads, :] / total[h : h + 1, :]
        attended = jnp.transpose(acc[...]).astype(BF16)
        att_ref[...] = attended
        first_sum = x_ref[...].astype(F32) + dot_nn(attended, w_ref[...])
        normed, inv_std = normalise(first_sum)
        n_ref[...] = normed
        istd_ref[...] = inv_std
        mid_ref[...] = (normed * norm_ref[0:1, :] + norm_ref[2:3, :]).astype(BF16)

    own = pl.BlockSpec((q_tile, width), lambda i, *_: (i, 0))
    return pl.pallas_call(
        body,
        grid_spec=pltpu.PrefetchScalarGridSpec(
            num_scalar_prefetch=3,
            grid=(n_own,),
            in_specs=[
                own,
                pl.BlockSpec((q_tile, width), lambda i, p, *_: (p[0] * n_own + i, 0)),
                whole_block((seq, width)),
                whole_block(vt.shape),
                whole_block((seq, 1)),
                pl.BlockSpec((1, 1, q_tile), lambda i, p, *_: (p[0] * n_own + i, 0, 0)),
                pl.BlockSpec((width, width), lambda *_: (0, 3), pipeline_mode=pl.Buffered(1)),
                whole_block((8, width)),
            ],
            out_specs=[
                own,
                pl.BlockSpec((16, q_tile), lambda i, *_: (0, i)),
                own,
                pl.BlockSpec((q_tile, 1), lambda i, *_: (i, 0)),
                own,
            ],
            scratch_shapes=[
                pltpu.VMEM((H, q_tile, LANES), BF16),
                pltpu.VMEM((16, q_tile), F32),
                pltpu.VMEM((16, q_tile), F32),
                pltpu.VMEM((width, q_tile), F32),
            ],
        ),
        out_shape=[
            jax.ShapeDtypeStruct((rows, width), BF16),
            jax.ShapeDtypeStruct((16, rows), F32),
            jax.ShapeDtypeStruct((rows, width), F32),
            jax.ShapeDtypeStruct((rows, 1), F32),
            jax.ShapeDtypeStruct((rows, width), BF16),
        ],
        compiler_params=params(),
        name="attend",
    )(pos, key_from, key_to, x_own, q, k, vt, seg_col, seg_row, weights, norms)


def feed_forward(mid_own, mid_sib, slots, offsets):
    rows, width = mid_own.shape
    tile = min(256, rows)
    n_own = rows // tile
    n_slots, n_pieces = len(slots), len(slots[0])
    _, block_rows, cols = slots[0][0].shape

    def body(offs_ref, own_ref, sib_ref, *rest):
        w_refs = rest[: n_slots * n_pieces]
        hid_ref, a_ref, b_ref, w_ref, out_own, out_sib = rest[n_slots * n_pieces :]
        i = pl.program_id(0)

        @pl.when(i == 0)
        def _():
            for s in range(n_slots):
                for p in range(n_pieces):
                    start = pl.multiple_of(offs_ref[p], 16)
                    for m in range(3):
                        w_ref[s, m, pl.ds(start, block_rows), :] = w_refs[s * n_pieces + p][m]

        x = jnp.where(i < n_own, own_ref[...].astype(F32), sib_ref[...].astype(F32)).astype(BF16)
        total = None
        for s in range(n_slots):
            gate = dot_nn(x, w_ref[s, 0])
            up = dot_nn(x, w_ref[s, 1])
            sig = 1.0 / (1.0 + jnp.exp(-gate))
            silu = gate * sig
            hidden = (silu * up).astype(BF16)
            hid_ref[s] = hidden
            a_ref[s] = (up * (sig * (1.0 + gate * (1.0 - sig)))).astype(BF16)
            b_ref[s] = silu.astype(BF16)
            part = dot_nt(hidden, w_ref[s, 2])
            total = part if total is None else total + part

        @pl.when(i < n_own)
        def _():
            out_own[...] = total

        @pl.when(i >= n_own)
        def _():
            out_sib[...] = total.astype(BF16)

    own = pl.BlockSpec((tile, width), lambda i, *_: (jnp.minimum(i, n_own - 1), 0))
    sib = pl.BlockSpec((tile, width), lambda i, *_: (jnp.maximum(i - n_own, 0), 0))
    act = pl.BlockSpec((n_slots, tile, cols), lambda i, *_: (0, i, 0))
    act_shape = jax.ShapeDtypeStruct((n_slots, 2 * rows, cols), BF16)
    flat = [p for slot in slots for p in slot]
    return pl.pallas_call(
        body,
        grid_spec=pltpu.PrefetchScalarGridSpec(
            num_scalar_prefetch=1,
            grid=(2 * n_own,),
            in_specs=[own, sib] + [whole_block(p.shape) for p in flat],
            out_specs=[act] * 3 + [whole_block((n_slots, 3, width, cols)), own, sib],
        ),
        out_shape=[act_shape] * 3
        + [
            jax.ShapeDtypeStruct((n_slots, 3, width, cols), BF16),
            jax.ShapeDtypeStruct((rows, width), F32),
            jax.ShapeDtypeStruct((rows, width), BF16),
        ],
        compiler_params=params(),
        name="feed_forward",
    )(offsets, mid_own, mid_sib, *flat)


def second_norm(normed1, part_own, part_sib, out_grad, norms):
    rows, width = normed1.shape
    tile = min(256, rows)

    def body(n_ref, own_ref, sib_ref, g_ref, norm_ref, out_ref, d_ref, dl_ref, ng_ref):
        middle = n_ref[...] * norm_ref[0:1, :] + norm_ref[2:3, :]
        second_sum = middle + (own_ref[...] + sib_ref[...].astype(F32))
        normed, inv_std = normalise(second_sum)
        out_ref[...] = (normed * norm_ref[1:2, :] + norm_ref[3:4, :]).astype(BF16)
        grad = g_ref[...].astype(F32)
        d = norm_back(normed, inv_std, norm_ref[1:2, :], grad)
        d_ref[...] = d
        dl_ref[...] = d.astype(BF16)

        @pl.when(pl.program_id(0) == 0)
        def _():
            ng_ref[...] = jnp.zeros(ng_ref.shape, F32)

        ng_ref[0:1, :] += jnp.sum(grad * normed, axis=0, keepdims=True)
        ng_ref[1:2, :] += jnp.sum(grad, axis=0, keepdims=True)

    block = pl.BlockSpec((tile, width), lambda i: (i, 0))
    return pl.pallas_call(
        body,
        grid=(rows // tile,),
        in_specs=[block] * 4 + [whole_block((8, width))],
        out_specs=[block] * 3 + [whole_block((8, width))],
        out_shape=[
            jax.ShapeDtypeStruct((rows, width), BF16),
            jax.ShapeDtypeStruct((rows, width), F32),
            jax.ShapeDtypeStruct((rows, width), BF16),
            jax.ShapeDtypeStruct((8, width), F32),
        ],
        compiler_params=params(),
        name="second_norm",
    )(normed1, part_own, part_sib, out_grad, norms)


def feed_forward_back(slot, mids, dffs, hidden, fac_a, fac_b, weights, d_mid, offsets, groups, block_rows):
    rows, width = mids[0].shape
    n_slots, _, cols = hidden.shape
    first = d_mid is None

    def body(offs_ref, mo, ms, do, ds, hid_ref, a_ref, b_ref, w_ref, *rest):
        if first:
            prev_ref, rest = None, rest
        else:
            prev_ref, rest = rest[0], rest[1:]
        dm_ref, group_refs, g_scr = rest[0], rest[1 : 1 + len(groups)], rest[-1]
        halves = []
        for t, d_ref in enumerate((do, ds)):
            part = slice(t * rows, (t + 1) * rows)
            dh = dot_nn(d_ref[...], w_ref[0, 2])
            d_gate = (dh * a_ref[0, part, :].astype(F32)).astype(BF16)
            d_up = (dh * b_ref[0, part, :].astype(F32)).astype(BF16)
            dm = dot_nt(d_gate, w_ref[0, 0]) + dot_nt(d_up, w_ref[0, 1])
            dm_ref[part, :] = dm if first else prev_ref[part, :] + dm
            halves.append((d_gate, d_up))
        g_scr[0] = dot_tn(mo[...], halves[0][0]) + dot_tn(ms[...], halves[1][0])
        g_scr[1] = dot_tn(mo[...], halves[0][1]) + dot_tn(ms[...], halves[1][1])
        g_scr[2] = dot_tn(do[...], hid_ref[0, :rows, :]) + dot_tn(ds[...], hid_ref[0, rows:, :])
        for (picks, dtype), ref in zip(groups, group_refs):
            for j, p in enumerate(picks):
                start = pl.multiple_of(offs_ref[p], 8)
                for m in range(3):
                    ref[j, m] = g_scr[m, pl.ds(start, block_rows), :].astype(dtype)

    act = pl.BlockSpec((1, 2 * rows, cols), lambda i, *_: (slot, 0, 0))
    full = whole_block((rows, width))
    acc = whole_block((2 * rows, width))
    group_shapes = [(len(picks), 3, block_rows, cols) for picks, _ in groups]
    extra = [] if first else [d_mid]
    return pl.pallas_call(
        body,
        grid_spec=pltpu.PrefetchScalarGridSpec(
            num_scalar_prefetch=1,
            grid=(1,),
            in_specs=[full] * 4
            + [act] * 3
            + [pl.BlockSpec((1, 3, width, cols), lambda i, *_: (slot, 0, 0, 0))]
            + [acc] * len(extra),
            out_specs=[acc] + [whole_block(s) for s in group_shapes],
            scratch_shapes=[pltpu.VMEM((3, width, cols), F32)],
        ),
        out_shape=[jax.ShapeDtypeStruct((2 * rows, width), F32)]
        + [jax.ShapeDtypeStruct(s, dtype) for s, (_, dtype) in zip(group_shapes, groups)],
        compiler_params=params(),
        name="feed_forward_back",
    )(offsets, *mids, *dffs, hidden, fac_a, fac_b, weights, *extra)


def first_norm_back(normed1, inv_std1, d_second, d_mid, d_mid_sib, norms):
    rows, width = normed1.shape
    tile = min(256, rows)

    def body(n_ref, istd_ref, d2_ref, dm_ref, ds_ref, norm_ref, d_ref, dl_ref, ng_ref):
        grad = d2_ref[...] + dm_ref[...] + ds_ref[...].astype(F32)
        normed = n_ref[...]
        d = norm_back(normed, istd_ref[...], norm_ref[0:1, :], grad)
        d_ref[...] = d
        dl_ref[...] = d.astype(BF16)

        @pl.when(pl.program_id(0) == 0)
        def _():
            ng_ref[...] = jnp.zeros(ng_ref.shape, F32)

        ng_ref[0:1, :] += jnp.sum(grad * normed, axis=0, keepdims=True)
        ng_ref[1:2, :] += jnp.sum(grad, axis=0, keepdims=True)

    block = pl.BlockSpec((tile, width), lambda i: (i, 0))
    column = pl.BlockSpec((tile, 1), lambda i: (i, 0))
    return pl.pallas_call(
        body,
        grid=(rows // tile,),
        in_specs=[block, column, block, block, block, whole_block((8, width))],
        out_specs=[block] * 2 + [whole_block((8, width))],
        out_shape=[
            jax.ShapeDtypeStruct((rows, width), F32),
            jax.ShapeDtypeStruct((rows, width), BF16),
            jax.ShapeDtypeStruct((8, width), F32),
        ],
        compiler_params=params(),
        name="first_norm_back",
    )(normed1, inv_std1, d_second, d_mid, d_mid_sib, norms)


def attend_back(d_rel, att_rel, lse_rel, q, k, v, kt, seg_col, seg_row, key_from, key_to, cosine, sine,
                weights, pos, rows, q_tile, k_tile):
    seq, width = q.shape
    n_own = rows // q_tile
    k_own = rows // k_tile
    n_tiles = seq // q_tile

    def true_tile(i, pos_ref):
        return (pos_ref[0] ^ (i // n_own)) * n_own + i % n_own

    def body(pos_ref, from_ref, to_ref, d_ref, att_ref, lse_ref, q_ref, k_ref, v_ref, kt_ref,
             sc_ref, sr_ref, cosq_ref, sinq_ref, cosk_ref, sink_ref, w_ref, out_ref,
             qm, dom, delta, dq, dk, dv):
        i = pl.program_id(0)
        own_q = i < n_own
        tile_index = true_tile(i, pos_ref)

        @pl.when(i == 0)
        def _():
            dk[...] = jnp.zeros(dk.shape, F32)
            dv[...] = jnp.zeros(dv.shape, F32)

        d_att = dot_nt(d_ref[...], w_ref[...]).astype(BF16)
        flipped = jnp.transpose(d_att.astype(F32) * att_ref[...].astype(F32))
        for h in range(H):
            delta[h : h + 1, :] = jnp.sum(flipped[h * HD : (h + 1) * HD, :], axis=0, keepdims=True)
        split_heads(q_ref, qm, q_tile)
        split_heads(d_att, dom, q_tile)
        row_docs = sr_ref[0]
        low = from_ref[tile_index]
        high = to_ref[tile_index]
        own_low = pos_ref[0] * k_own
        own_high = own_low + k_own
        mine_low = jnp.maximum(low, own_low)
        mine_high = jnp.minimum(high, own_high)

        def step(tile, need_q, need_k):
            at = pl.multiple_of(tile * k_tile, k_tile)
            mask = sc_ref[pl.ds(at, k_tile), :] == row_docs
            for b in range(H // 2):
                cols = slice(b * LANES, (b + 1) * LANES)
                k_block = k_ref[pl.ds(at, k_tile), cols]
                v_block = v_ref[pl.ds(at, k_tile), cols]
                add_k = add_v = None
                for h in (2 * b, 2 * b + 1):
                    heads = slice(h * HD, (h + 1) * HD)
                    s = dot_nt(k_block, qm[h])
                    p = jnp.exp(jnp.where(mask, s, NEG) - lse_ref[h : h + 1, :])
                    dp = dot_nt(v_block, dom[h])
                    ds = (p * (dp - delta[h : h + 1, :])).astype(BF16)
                    if need_q:
                        dq[heads, :] += dot_nn(kt_ref[tile, heads, :], ds)
                    if need_k:
                        pk = dot_nn(ds, qm[h])
                        pv = dot_nn(p.astype(BF16), dom[h])
                        add_k = pk if add_k is None else add_k + pk
                        add_v = pv if add_v is None else add_v + pv
                if need_k:
                    here = pl.ds(pl.multiple_of(at - own_low * k_tile, k_tile), k_tile)
                    dk[here, cols] += add_k
                    dv[here, cols] += add_v

        def both(tile, carry):
            step(tile, True, True)
            return carry

        @pl.when(own_q)
        def _():
            dq[...] = jnp.zeros(dq.shape, F32)
            lax.fori_loop(mine_low, mine_high, both, 0)
            n_left = jnp.maximum(jnp.minimum(high, own_low) - low, 0)
            right = jnp.maximum(low, own_high)
            n_right = jnp.maximum(high - right, 0)

            def outside(j, carry):
                step(jnp.where(j < n_left, low + j, right + j - n_left), True, False)
                return carry

            lax.fori_loop(0, n_left + n_right, outside, 0)
            turned = jnp.transpose(dq[...]) * (HD**-0.5)
            at = pl.ds(pl.multiple_of(i * q_tile, q_tile), q_tile)
            for b in range(width // LANES):
                cols = slice(b * LANES, (b + 1) * LANES)
                g = turned[:, cols].astype(BF16).astype(F32)
                out_ref[at, cols] = (g * cosq_ref[...] - half_swap(g) * sinq_ref[...]).astype(BF16)

        @pl.when(jnp.logical_not(own_q))
        def _():
            def keys_only(tile, carry):
                step(tile, False, True)
                return carry

            lax.fori_loop(mine_low, mine_high, keys_only, 0)

        @pl.when(i == n_tiles - 1)
        def _():
            for b in range(width // LANES):
                cols = slice(b * LANES, (b + 1) * LANES)
                g = dk[:, cols].astype(BF16).astype(F32)
                out_ref[:, width + b * LANES : width + (b + 1) * LANES] = (
                    g * cosk_ref[...] - half_swap(g) * sink_ref[...]
                ).astype(BF16)
            out_ref[:, 2 * width :] = dv[...].astype(BF16)

    rel = pl.BlockSpec((q_tile, width), lambda i, *_: (i, 0))
    q_table = pl.BlockSpec((q_tile, LANES), lambda i, p, *_: (true_tile(i, p), 0))
    k_table = pl.BlockSpec((rows, LANES), lambda i, p, *_: (p[0], 0))
    return pl.pallas_call(
        body,
        grid_spec=pltpu.PrefetchScalarGridSpec(
            num_scalar_prefetch=3,
            grid=(n_tiles,),
            in_specs=[
                rel,
                rel,
                pl.BlockSpec((16, q_tile), lambda i, *_: (0, i)),
                pl.BlockSpec((q_tile, width), lambda i, p, *_: (true_tile(i, p), 0)),
                whole_block((seq, width)),
                whole_block((seq, width)),
                whole_block(kt.shape),
                whole_block((seq, 1)),
                pl.BlockSpec((1, 1, q_tile), lambda i, p, *_: (true_tile(i, p), 0, 0)),
                q_table,
                q_table,
                k_table,
                k_table,
                pl.BlockSpec((width, width), lambda *_: (0, 3), pipeline_mode=pl.Buffered(1)),
            ],
            out_specs=[whole_block((rows, 3 * width))],
            scratch_shapes=[
                pltpu.VMEM((H, q_tile, LANES), BF16),
                pltpu.VMEM((H, q_tile, LANES), BF16),
                pltpu.VMEM((16, q_tile), F32),
                pltpu.VMEM((width, q_tile), F32),
                pltpu.VMEM((rows, width), F32),
                pltpu.VMEM((rows, width), F32),
            ],
        ),
        out_shape=[jax.ShapeDtypeStruct((rows, 3 * width), BF16)],
        compiler_params=params(),
        name="attend_back",
    )(pos, key_from, key_to, d_rel, att_rel, lse_rel, q, k, v, kt, seg_col, seg_row,
      cosine, sine, cosine, sine, weights)[0]


def finish(x_own, d_merged, d_first, d_first_low, attended, weights, norm1, norm2, offsets, groups, block_rows):
    rows, width = x_own.shape
    wide = weights.shape[1]

    def body(offs_ref, x_ref, dm_ref, df_ref, dl_ref, att_ref, w_ref, n1_ref, n2_ref, in_ref, *rest):
        group_refs, g_scr = rest[:-1], rest[-1]
        in_ref[...] = df_ref[...] + dot_nt(dm_ref[...], w_ref[:, : 3 * width])
        for j in range(3):
            cols = slice(j * width, (j + 1) * width)
            g_scr[:, cols] = dot_tn(x_ref[...], dm_ref[:, cols])
        g_scr[:, 3 * width : 4 * width] = dot_tn(att_ref[...], dl_ref[...])
        stacked = jnp.concatenate(
            [n1_ref[0:1, :], n2_ref[0:1, :], n1_ref[1:2, :], n2_ref[1:2, :],
             jnp.zeros((PAD - 4, width), F32)], axis=0)
        g_scr[:, 4 * width :] = jnp.transpose(stacked)
        for (picks, dtype), ref in zip(groups, group_refs):
            for j, p in enumerate(picks):
                start = pl.multiple_of(offs_ref[p], 8)
                ref[j] = g_scr[pl.ds(start, block_rows), :].astype(dtype)

    group_shapes = [(len(picks), block_rows, wide) for picks, _ in groups]
    operands = (x_own, d_merged, d_first, d_first_low, attended, weights, norm1, norm2)
    return pl.pallas_call(
        body,
        grid_spec=pltpu.PrefetchScalarGridSpec(
            num_scalar_prefetch=1,
            grid=(1,),
            in_specs=[whole_block(o.shape) for o in operands],
            out_specs=[whole_block((rows, width))] + [whole_block(s) for s in group_shapes],
            scratch_shapes=[pltpu.VMEM((width, wide), F32)],
        ),
        out_shape=[jax.ShapeDtypeStruct((rows, width), F32)]
        + [jax.ShapeDtypeStruct(s, dtype) for s, (_, dtype) in zip(group_shapes, groups)],
        compiler_params=params(),
        name="finish",
    )(offsets, *operands)


def make_per_device(ndp, nt):
    plane = ndp // 2

    def move(value, chip=0, core=0, ahead=0, flip=0):
        pairs = []
        for d in range(ndp):
            for t in range(nt):
                to_d = ((d // 2) ^ chip) * 2 + ((d % 2) ^ core)
                to_t = ((t + ahead) % nt) ^ flip
                pairs.append((d * nt + t, to_d * nt + to_t))
        return lax.ppermute(value, AXES, pairs)

    def per_device(inputs, segment_ids, qkv_weight, out_weight, norm_gains, norm_biases,
                   gate_weight, up_weight, down_weight, out_grad):
        rows, width = inputs.shape
        seq = segment_ids.shape[1]
        n_row = seq // rows
        q_tile = min(256, rows)
        k_tile = min(256, rows)
        shard = qkv_weight.shape[0]
        ffn_rows, ffn_cols = gate_weight.shape
        half = ffn_cols // 2
        fast = plane == 4 and nt == 4

        d_index = lax.axis_index("dp")
        core = d_index % 2
        chip = d_index // 2
        t_index = lax.axis_index("tensor")
        pos = (t_index % n_row).astype(jnp.int32)

        packed = jnp.concatenate(
            [qkv_weight, out_weight, norm_gains.T, norm_biases.T,
             jnp.zeros((shard, PAD - 4), BF16)], axis=1)
        x_rel = jnp.concatenate(
            [inputs] + [move(inputs, flip=e) for e in range(1, n_row)], axis=0)
        if fast:
            mine = [packed] + [move(packed, ahead=s) for s in range(1, nt)]
            w_pieces, w_offsets = [], []
            for s, piece in enumerate(mine):
                z_from = (t_index - s) % nt
                for dxy in range(4):
                    got = piece if dxy == 0 else move(piece, chip=dxy)
                    base = (chip ^ dxy) * 2
                    for other in range(2):
                        w_pieces.append(got if other == 0 else move(got, core=1))
                        w_offsets.append(((base + (core ^ other)) * nt + z_from) * shard)
        else:
            w_pieces = [lax.all_gather(packed, AXES, axis=0, tiled=True)]
            w_offsets = [0]
        w_offsets = jnp.stack([jnp.asarray(o, jnp.int32) for o in w_offsets])

        ffn = jnp.stack([gate_weight, up_weight, down_weight.T])
        if fast:
            keep = lax.dynamic_slice_in_dim(ffn, core * half, half, 2)
            give = lax.dynamic_slice_in_dim(ffn, (1 - core) * half, half, 2)
            a0, b0 = keep, move(give, core=1)
            slots = []
            for s in range(nt):
                a = a0 if s == 0 else move(a0, ahead=s)
                b = b0 if s == 0 else move(b0, ahead=s)
                ax = move(a, chip=1)
                by = move(b, chip=2)
                slots.append([a, b, ax, move(b, chip=1), move(a, chip=2), by,
                              move(ax, chip=2), move(by, chip=1)])
            f_offsets = jnp.stack(
                [((chip ^ dxy) * 2 + (core ^ other)) * ffn_rows for dxy in range(4) for other in range(2)]
            ).astype(jnp.int32)
        else:
            full = lax.all_gather(ffn, "dp", axis=1, tiled=True)
            full = lax.dynamic_slice_in_dim(full, core * half, half, 2)
            slots = [[lax.all_gather(full, "tensor", axis=2, tiled=True)]]
            f_offsets = jnp.zeros((1,), jnp.int32)

        seg = lax.dynamic_index_in_dim(segment_ids, t_index // n_row, 0, keepdims=False)
        doc_from = jnp.sum((seg[None, :] < seg[:, None]).astype(jnp.int32), axis=1)
        doc_to = jnp.sum((seg[None, :] <= seg[:, None]).astype(jnp.int32), axis=1)
        place = (jnp.arange(seq, dtype=jnp.int32) - doc_from).astype(F32)
        lane = np.arange(LANES)
        frequency = rope_base ** (-jnp.asarray(lane % (HD // 2), F32) * 2.0 / HD)
        angles = place[:, None] * frequency[None, :]
        cosine = jnp.cos(angles)
        sine = jnp.sin(angles) * jnp.asarray(np.where(lane % HD < HD // 2, -1.0, 1.0), F32)[None, :]
        key_from = doc_from[::q_tile] // k_tile
        key_to = (doc_to[q_tile - 1 :: q_tile] + k_tile - 1) // k_tile
        seg_col = seg[:, None]
        seg_row = seg.reshape(seq // q_tile, 1, q_tile)
        pos_arr = pos[None]

        q, k, v, kt, vt, weights, norms = project(
            x_rel, w_pieces, w_offsets, cosine, sine, pos_arr, n_row, k_tile)
        attended, lse, normed1, inv_std1, mid = attend(
            inputs, q, k, vt, seg_col, seg_row, key_from, key_to, weights, norms, pos_arr, q_tile, k_tile)
        mid_sib = move(mid, core=1)
        att_rel = jnp.concatenate(
            [attended] + [move(attended, flip=e) for e in range(1, n_row)], axis=0)
        lse_rel = jnp.concatenate([lse] + [move(lse, flip=e) for e in range(1, n_row)], axis=1)

        hidden, fac_a, fac_b, ffn_w, part_own, part_sib = feed_forward(mid, mid_sib, slots, f_offsets)
        outputs, d_second, d_ffn, norm2 = second_norm(
            normed1, part_own, move(part_sib, core=1), out_grad, norms)
        d_ffn_sib = move(d_ffn, core=1)

        d_mid = None
        reduced = []
        if fast:
            groups = [((4, 6), BF16), ((3, 7), BF16), ((0, 2, 1, 5), F32)]
            block_rows = ffn_rows
        else:
            groups = [((0,), BF16)]
            block_rows = width
        for s in range(len(slots)):
            d_mid, *parts = feed_forward_back(
                s, (mid, mid_sib), (d_ffn, d_ffn_sib), hidden, fac_a, fac_b, ffn_w, d_mid,
                f_offsets, groups, block_rows)
            reduced.append(parts)

        d_mid_sib = move(d_mid[rows:].astype(BF16), core=1)
        d_first, d_first_low, norm1 = first_norm_back(
            normed1, inv_std1, d_second, d_mid, d_mid_sib, norms)
        d_rel = jnp.concatenate(
            [d_first_low] + [move(d_first_low, flip=e) for e in range(1, n_row)], axis=0)
        d_merged = attend_back(
            d_rel, att_rel, lse_rel, q, k, v, kt, seg_col, seg_row, key_from, key_to, cosine, sine,
            weights, pos_arr, rows, q_tile, k_tile)

        if fast:
            q_groups = [((1, 3, 5, 7), BF16), ((0, 2, 4, 6), F32)]
            q_offsets = jnp.stack(
                [((chip ^ dxy) * 2 + (core ^ other)) * (nt * shard) for dxy in range(4) for other in range(2)]
            ).astype(jnp.int32)
            q_rows = nt * shard
        else:
            q_groups = [((0,), F32)]
            q_offsets = jnp.zeros((1,), jnp.int32)
            q_rows = width
        inputs_grad, *q_parts = finish(
            inputs, d_merged, d_first, d_first_low, attended, weights, norm1, norm2,
            q_offsets, q_groups, q_rows)

        if fast:
            total = None
            for s, (to_y, to_x, kept) in enumerate(reduced):
                from_y = move(to_y, chip=2).astype(F32)
                from_x = move(to_x, chip=1).astype(F32)
                own_a = kept[0] + from_y[0] + move((kept[1] + from_y[1]).astype(BF16), chip=1).astype(F32)
                own_b = kept[2] + from_x[0] + move((kept[3] + from_x[1]).astype(BF16), chip=2).astype(F32)
                both = jnp.stack([own_a, own_b])
                if s:
                    both = move(both.astype(BF16), ahead=nt - s).astype(F32)
                total = both if total is None else total + both
            other = move(total[1], core=1)
            mine = total[0]
            ffn_grads = jnp.where(
                core == 0,
                jnp.concatenate([mine, other], axis=2),
                jnp.concatenate([other, mine], axis=2))
            q_sum = q_parts[1] + move(q_parts[0], core=1).astype(F32)
            q_own = q_sum[0]
            for dxy in range(1, 4):
                q_own = q_own + move(q_sum[dxy].astype(BF16), chip=dxy).astype(F32)
            packed_grad = None
            for s in range(nt):
                piece = lax.dynamic_slice_in_dim(q_own, ((t_index - s) % nt) * shard, shard, 0)
                if s:
                    piece = move(piece.astype(BF16), ahead=nt - s).astype(F32)
                packed_grad = piece if packed_grad is None else packed_grad + piece
        else:
            grads = lax.psum_scatter(reduced[0][0][0], "tensor", scatter_dimension=2, tiled=True)
            spread = jnp.zeros(grads.shape[:2] + (2 * half,), BF16)
            spread = lax.dynamic_update_slice_in_dim(spread, grads.astype(BF16), core * half, 2)
            ffn_grads = lax.psum_scatter(spread, "dp", scatter_dimension=1, tiled=True).astype(F32)
            packed_grad = lax.psum_scatter(q_parts[0][0], AXES, scatter_dimension=0, tiled=True)

        return (
            outputs,
            inputs_grad,
            packed_grad[:, : 3 * width],
            packed_grad[:, 3 * width : 4 * width],
            packed_grad[:, 4 * width : 4 * width + 2].T,
            packed_grad[:, 4 * width + 2 : 4 * width + 4].T,
            ffn_grads[0],
            ffn_grads[1],
            ffn_grads[2].T,
        )

    return per_device


def solution(mesh):
    tokens = P(AXES, None)
    both = P("dp", "tensor")
    return jax.shard_map(
        make_per_device(mesh.shape["dp"], mesh.shape["tensor"]),
        mesh=mesh,
        in_specs=(tokens, P("dp", None), tokens, tokens, P(None, AXES), P(None, AXES),
                  both, both, P("tensor", "dp"), tokens),
        out_specs=(tokens, tokens, tokens, tokens, P(None, AXES), P(None, AXES),
                   both, both, P("tensor", "dp")),
        check_vma=False,
    )
```

```python
import jax
import jax.numpy as jnp
import numpy as np
from jax import lax
from jax.experimental import pallas as pl
from jax.experimental.pallas import tpu as pltpu
from jax.sharding import PartitionSpec as P

H = 12
HD = 64
LANES = 128
PAD = 128
NEG = -1e30

rope_base = 1000.0
layer_eps = 1e-12

AXES = ("dp", "tensor")
F32 = jnp.float32
BF16 = jnp.bfloat16
VMEM_BYTES = 60 * 2**20


def params(n_axes=1):
    return pltpu.CompilerParams(
        dimension_semantics=("arbitrary",) * n_axes, vmem_limit_bytes=VMEM_BYTES
    )


def whole_block(shape):
    zeros = (0,) * len(shape)
    return pl.BlockSpec(shape, lambda *_: zeros, pipeline_mode=pl.Buffered(1))


def dot_nn(a, b):
    return lax.dot_general(a, b, (((1,), (0,)), ((), ())), preferred_element_type=F32)


def dot_nt(a, b):
    return lax.dot_general(a, b, (((1,), (1,)), ((), ())), preferred_element_type=F32)


def dot_tn(a, b):
    return lax.dot_general(a, b, (((0,), (0,)), ((), ())), preferred_element_type=F32)


def half_swap(block):
    lane = lax.broadcasted_iota(jnp.int32, block.shape, 1)
    return jnp.where(
        lane % HD < HD // 2, pltpu.roll(block, LANES - HD // 2, 1), pltpu.roll(block, HD // 2, 1)
    )


def normalise(summed):
    mean = jnp.mean(summed, axis=-1, keepdims=True)
    centred = summed - mean
    inv_std = lax.rsqrt(jnp.mean(centred * centred, axis=-1, keepdims=True) + layer_eps)
    return centred * inv_std, inv_std


def norm_back(normed, inv_std, gain, grad):
    scaled = grad * gain
    return inv_std * (
        scaled
        - jnp.mean(scaled, axis=-1, keepdims=True)
        - normed * jnp.mean(scaled * normed, axis=-1, keepdims=True)
    )


class Pieces:
    def __init__(self, slots, width, cols=None):
        self.flat = [p for slot in slots for p in slot]
        self.n_slots = len(slots)
        self.n_pieces = len(slots[0])
        self.blocks = [(p, b) for p in range(self.n_pieces) for b in range(slots[0][p].shape[0])]
        _, self.block_rows, wide = slots[0][0].shape
        self.cols = cols or slice(0, wide)
        self.in_specs = [pl.BlockSpec(memory_space=pl.ANY)] * len(self.flat)
        self.scratch = [
            pltpu.VMEM((self.n_slots, width, self.cols.stop - self.cols.start), BF16),
            pltpu.SemaphoreType.DMA((self.n_slots, len(self.blocks))),
        ]

    def copies(self, slot, refs, offs_ref, scr, sems):
        for j, (p, b) in enumerate(self.blocks):
            start = pl.multiple_of(offs_ref[j], 16)
            yield pltpu.make_async_copy(
                refs[slot * self.n_pieces + p].at[b, :, self.cols],
                scr.at[slot, pl.ds(start, self.block_rows), :],
                sems.at[slot, j],
            )

    def start(self, slot, *args):
        for copy in self.copies(slot, *args):
            copy.start()

    def wait(self, slot, *args):
        for copy in self.copies(slot, *args):
            copy.wait()

    def start_all(self, *args):
        for s in range(self.n_slots):
            self.start(s, *args)

    def wait_for_step(self, step, *args):
        for s in range(self.n_slots):

            @pl.when(step == s)
            def _(s=s):
                self.wait(s, *args)


def head_lanes(block, h, extra):
    lane = lax.broadcasted_iota(jnp.int32, block.shape, 1)
    mine = lane < HD if h % 2 == 0 else lane >= HD
    return jnp.where(mine, block, extra)


def project(x_rel, pieces, offsets, cosine, sine, seg_col, pos, n_row, k_tile):
    seq, width = x_rel.shape
    rows = seq // n_row
    tile = min(256, rows)
    per_piece = rows // tile
    held = Pieces([pieces], width)
    n_in = len(held.flat)

    def true_tile(i, pos_ref):
        return (pos_ref[0] ^ (i // per_piece)) * per_piece + i % per_piece

    def body(pos_ref, offs_ref, x_ref, cos_ref, sin_ref, seg_ref, *rest):
        w_refs, rest = rest[:n_in], rest[n_in:]
        q_ref, k_ref, v_ref, kt_ref, vt_ref, norm_ref, w_scr, sems = rest

        @pl.when(pl.program_id(0) == 0)
        def _():
            held.start(0, w_refs, offs_ref, w_scr, sems)
            held.wait(0, w_refs, offs_ref, w_scr, sems)
            norm_ref[...] = jnp.transpose(w_scr[0, :, 4 * width :].astype(F32))[:8, :]

        x = x_ref[...]
        cos = cos_ref[...]
        sin = sin_ref[...]
        lane = lax.broadcasted_iota(jnp.int32, (tile, LANES), 1)
        same = lane % HD == seg_ref[...]
        key_extra = jnp.where(same, 1.0, 0.0)
        query_extra = jnp.where(same, 0.0, NEG)
        merged = dot_nn(x, w_scr[0, :, : 3 * width])
        for b in range(width // LANES):
            cols = slice(b * LANES, (b + 1) * LANES)
            q = merged[:, b * LANES : (b + 1) * LANES]
            k = merged[:, width + b * LANES : width + (b + 1) * LANES]
            v = merged[:, 2 * width + b * LANES : 2 * width + (b + 1) * LANES]
            q = (q * cos + half_swap(q) * sin) * (HD**-0.5)
            k = k * cos + half_swap(k) * sin
            for h in (2 * b, 2 * b + 1):
                q_ref[h] = head_lanes(q, h, query_extra).astype(BF16)
                k_ref[h] = head_lanes(k, h, key_extra).astype(BF16)
            v_ref[:, cols] = v.astype(BF16)
            vt_ref[cols, :] = jnp.transpose(v).astype(BF16)
            for j in range(tile // k_tile):
                kt_ref[j, cols, :] = jnp.transpose(k[j * k_tile : (j + 1) * k_tile, :]).astype(BF16)

    row_block = pl.BlockSpec((tile, width), lambda i, p, o: (true_tile(i, p), 0))
    head_block = pl.BlockSpec((H, tile, LANES), lambda i, p, o: (0, true_tile(i, p), 0))
    table_block = pl.BlockSpec((tile, LANES), lambda i, p, o: (true_tile(i, p), 0))
    return pl.pallas_call(
        body,
        grid_spec=pltpu.PrefetchScalarGridSpec(
            num_scalar_prefetch=2,
            grid=(seq // tile,),
            in_specs=[
                pl.BlockSpec((tile, width), lambda i, p, o: (i, 0)),
                table_block,
                table_block,
                pl.BlockSpec((tile, 1), lambda i, p, o: (true_tile(i, p), 0)),
            ]
            + held.in_specs,
            out_specs=[
                head_block,
                head_block,
                row_block,
                pl.BlockSpec((tile // k_tile, width, k_tile), lambda i, p, o: (true_tile(i, p), 0, 0)),
                pl.BlockSpec((width, tile), lambda i, p, o: (0, true_tile(i, p))),
                whole_block((8, width)),
            ],
            scratch_shapes=held.scratch,
        ),
        out_shape=[jax.ShapeDtypeStruct((H, seq, LANES), BF16)] * 2
        + [
            jax.ShapeDtypeStruct((seq, width), BF16),
            jax.ShapeDtypeStruct((seq // k_tile, width, k_tile), BF16),
            jax.ShapeDtypeStruct((width, seq), BF16),
            jax.ShapeDtypeStruct((8, width), F32),
        ],
        compiler_params=params(),
        name="project",
    )(pos, offsets, x_rel, cosine, sine, seg_col, *held.flat)


GROUP = 4


def attend(x_own, q, k, vt, pieces, offsets, norms, pos):
    rows, width = x_own.shape
    seq = q.shape[1]
    group_cols = GROUP * HD
    n_steps = H // GROUP
    held = Pieces([pieces], width, slice(3 * width, 4 * width))
    n_in = len(held.flat)

    def body(pos_ref, offs_ref, x_ref, q_ref, k_ref, vt_ref, norm_ref, *rest):
        w_refs, rest = rest[:n_in], rest[n_in:]
        att_ref, lse_ref, n_ref, istd_ref, mid_ref, acc, lse, w_scr, sems = rest
        g = pl.program_id(0)

        @pl.when(g == 0)
        def _():
            held.start(0, w_refs, offs_ref, w_scr, sems)

        for j in range(GROUP):
            s = dot_nt(k_ref[j], q_ref[j])
            peak = jnp.max(s, axis=0, keepdims=True)
            e = jnp.exp(s - peak)
            total = jnp.sum(e, axis=0, keepdims=True)
            out = dot_nn(vt_ref[j * HD : (j + 1) * HD, :], e.astype(BF16))
            acc[g, j * HD : (j + 1) * HD, :] = out / total
            lse[g, j : j + 1, :] = peak + jnp.log(total)

        @pl.when(g == n_steps - 1)
        def _():
            held.wait(0, w_refs, offs_ref, w_scr, sems)
            for i in range(n_steps):
                lse_ref[i] = lse[i]
                att_ref[:, i * group_cols : (i + 1) * group_cols] = jnp.transpose(acc[i]).astype(BF16)
            first_sum = x_ref[...].astype(F32) + dot_nn(att_ref[...], w_scr[0])
            normed, inv_std = normalise(first_sum)
            n_ref[...] = normed
            istd_ref[...] = inv_std
            mid_ref[...] = (normed * norm_ref[0:1, :] + norm_ref[2:3, :]).astype(BF16)

    own = whole_block((rows, width))
    return pl.pallas_call(
        body,
        grid_spec=pltpu.PrefetchScalarGridSpec(
            num_scalar_prefetch=2,
            grid=(n_steps,),
            in_specs=[
                own,
                pl.BlockSpec((GROUP, rows, LANES), lambda g, p, o: (g, p[0], 0)),
                pl.BlockSpec((GROUP, seq, LANES), lambda g, p, o: (g, 0, 0)),
                pl.BlockSpec((group_cols, seq), lambda g, p, o: (g, 0)),
                whole_block((8, width)),
            ]
            + held.in_specs,
            out_specs=[own, whole_block((n_steps, 8, rows)), own, whole_block((rows, 1)), own],
            scratch_shapes=[
                pltpu.VMEM((n_steps, group_cols, rows), F32),
                pltpu.VMEM((n_steps, 8, rows), F32),
            ]
            + held.scratch,
        ),
        out_shape=[
            jax.ShapeDtypeStruct((rows, width), BF16),
            jax.ShapeDtypeStruct((n_steps, 8, rows), F32),
            jax.ShapeDtypeStruct((rows, width), F32),
            jax.ShapeDtypeStruct((rows, 1), F32),
            jax.ShapeDtypeStruct((rows, width), BF16),
        ],
        compiler_params=params(),
        name="attend",
    )(pos, offsets, x_own, q, k, vt, norms, *held.flat)


def feed_forward(mid_own, mid_sib, slots, offsets, before, last):
    rows, width = mid_own.shape
    held = Pieces(slots, width)
    n_slots, cols = held.n_slots, held.cols.stop // 3
    n_in = len(held.flat)

    def body(offs_ref, own_ref, sib_ref, *rest):
        w_refs, rest = rest[:n_in], rest[n_in:]
        if before is not None:
            before_ref, rest = rest[0], rest[1:]
        if last:
            hid_ref, a_ref, b_ref, out_own, out_sib, acc, w_scr, sems = rest
        else:
            hid_ref, a_ref, b_ref, acc, w_scr, sems = rest
        s = pl.program_id(0)

        @pl.when(s == 0)
        def _():
            held.start_all(w_refs, offs_ref, w_scr, sems)
            acc[...] = jnp.zeros(acc.shape, F32) if before is None else before_ref[...]

        held.wait_for_step(s, w_refs, offs_ref, w_scr, sems)
        for i, x_ref in enumerate((own_ref, sib_ref)):
            part = slice(i * rows, (i + 1) * rows)
            both = dot_nn(x_ref[...], w_scr[s, :, : 2 * cols])
            gate, up = both[:, :cols], both[:, cols:]
            sig = 0.5 * jnp.tanh(0.5 * gate) + 0.5
            silu = gate * sig
            hidden = (silu * up).astype(BF16)
            hid_ref[0, part, :] = hidden
            a_ref[0, part, :] = (up * (sig + silu * (1.0 - sig))).astype(BF16)
            b_ref[0, part, :] = silu.astype(BF16)
            acc[part, :] += dot_nt(hidden, w_scr[s, :, 2 * cols :])

        if last:

            @pl.when(s == n_slots - 1)
            def _():
                out_own[...] = acc[:rows, :]
                out_sib[...] = acc[rows:, :].astype(BF16)

    full = whole_block((rows, width))
    both_block = whole_block((2 * rows, width))
    act = pl.BlockSpec((1, 2 * rows, cols), lambda i, *_: (i, 0, 0))
    act_shape = jax.ShapeDtypeStruct((n_slots, 2 * rows, cols), BF16)
    extra = [] if before is None else [before]
    if last:
        acc_specs = [full, full]
        acc_shapes = [jax.ShapeDtypeStruct((rows, width), F32), jax.ShapeDtypeStruct((rows, width), BF16)]
        acc_scratch = [pltpu.VMEM((2 * rows, width), F32)]
    else:
        acc_specs = [both_block]
        acc_shapes = [jax.ShapeDtypeStruct((2 * rows, width), F32)]
        acc_scratch = []
    return pl.pallas_call(
        body,
        grid_spec=pltpu.PrefetchScalarGridSpec(
            num_scalar_prefetch=1,
            grid=(n_slots,),
            in_specs=[full, full] + held.in_specs + [both_block] * len(extra),
            out_specs=[act] * 3 + acc_specs,
            scratch_shapes=acc_scratch + held.scratch,
        ),
        out_shape=[act_shape] * 3 + acc_shapes,
        compiler_params=params(),
        name="feed_forward",
    )(offsets, mid_own, mid_sib, *held.flat, *extra)


def second_norm(normed1, part_own, part_sib, out_grad, norms):
    rows, width = normed1.shape
    tile = min(256, rows)

    def body(n_ref, own_ref, sib_ref, g_ref, norm_ref, out_ref, d_ref, dl_ref, ng_ref):
        middle = n_ref[...] * norm_ref[0:1, :] + norm_ref[2:3, :]
        second_sum = middle + (own_ref[...] + sib_ref[...].astype(F32))
        normed, inv_std = normalise(second_sum)
        out_ref[...] = (normed * norm_ref[1:2, :] + norm_ref[3:4, :]).astype(BF16)
        grad = g_ref[...].astype(F32)
        d = norm_back(normed, inv_std, norm_ref[1:2, :], grad)
        d_ref[...] = d
        dl_ref[...] = d.astype(BF16)

        @pl.when(pl.program_id(0) == 0)
        def _():
            ng_ref[...] = jnp.zeros(ng_ref.shape, F32)

        ng_ref[0:1, :] += jnp.sum(grad * normed, axis=0, keepdims=True)
        ng_ref[1:2, :] += jnp.sum(grad, axis=0, keepdims=True)

    block = pl.BlockSpec((tile, width), lambda i: (i, 0))
    return pl.pallas_call(
        body,
        grid=(rows // tile,),
        in_specs=[block] * 4 + [whole_block((8, width))],
        out_specs=[block] * 3 + [whole_block((8, width))],
        out_shape=[
            jax.ShapeDtypeStruct((rows, width), BF16),
            jax.ShapeDtypeStruct((rows, width), F32),
            jax.ShapeDtypeStruct((rows, width), BF16),
            jax.ShapeDtypeStruct((8, width), F32),
        ],
        compiler_params=params(),
        name="second_norm",
    )(normed1, part_own, part_sib, out_grad, norms)


def hidden_back(dffs, factors, slots, offsets):
    rows, width = dffs[0].shape
    held = Pieces(slots, width)
    n_slots, cols = held.n_slots, held.cols.stop // 3
    n_in = len(held.flat)
    per_call = factors[0][0].shape[0]
    n_fac = len(factors)

    def body(offs_ref, do_ref, ds_ref, *rest):
        fac_refs, rest = rest[: 2 * n_fac], rest[2 * n_fac :]
        w_refs, rest = rest[:n_in], rest[n_in:]
        d_ref, out_own, out_sib, acc, w_scr, sems = rest
        s = pl.program_id(0)

        @pl.when(s == 0)
        def _():
            held.start_all(w_refs, offs_ref, w_scr, sems)
            acc[...] = jnp.zeros(acc.shape, F32)

        held.wait_for_step(s, w_refs, offs_ref, w_scr, sems)

        def work(a_ref, b_ref):
            for i, x_ref in enumerate((do_ref, ds_ref)):
                part = slice(i * rows, (i + 1) * rows)
                dh = dot_nn(x_ref[...], w_scr[s, :, 2 * cols :])
                d_ref[0, part, :cols] = (dh * a_ref[0, part, :].astype(F32)).astype(BF16)
                d_ref[0, part, cols:] = (dh * b_ref[0, part, :].astype(F32)).astype(BF16)
                acc[part, :] += dot_nt(d_ref[0, part, :], w_scr[s, :, : 2 * cols])

        for f in range(n_fac):

            @pl.when(s // per_call == f)
            def _(f=f):
                work(fac_refs[2 * f], fac_refs[2 * f + 1])

        @pl.when(s == n_slots - 1)
        def _():
            out_own[...] = acc[:rows, :]
            out_sib[...] = acc[rows:, :].astype(BF16)

    full = whole_block((rows, width))

    def fac_spec(f):
        return pl.BlockSpec(
            (1, 2 * rows, cols), lambda i, *_: (jnp.clip(i - f * per_call, 0, per_call - 1), 0, 0)
        )

    return pl.pallas_call(
        body,
        grid_spec=pltpu.PrefetchScalarGridSpec(
            num_scalar_prefetch=1,
            grid=(n_slots,),
            in_specs=[full, full]
            + [fac_spec(f) for f in range(n_fac) for _ in range(2)]
            + held.in_specs,
            out_specs=[pl.BlockSpec((1, 2 * rows, 2 * cols), lambda i, *_: (i, 0, 0)), full, full],
            scratch_shapes=[pltpu.VMEM((2 * rows, width), F32)] + held.scratch,
        ),
        out_shape=[
            jax.ShapeDtypeStruct((n_slots, 2 * rows, 2 * cols), BF16),
            jax.ShapeDtypeStruct((rows, width), F32),
            jax.ShapeDtypeStruct((rows, width), BF16),
        ],
        compiler_params=params(),
        name="hidden_back",
    )(offsets, *dffs, *[x for pair in factors for x in pair], *held.flat)


def store_groups(groups, group_refs, offs_ref, n_blocks, block_rows, source):
    for (picks, dtype), ref in zip(groups, group_refs):
        for j, p in enumerate(picks):
            for b in range(n_blocks):
                start = pl.multiple_of(offs_ref[p * n_blocks + b], 8)
                ref[j, b] = source[pl.ds(start, block_rows), :].astype(dtype)


def ffn_grads(first, mids, dffs, hidden, d_both, offsets, groups, n_blocks, block_rows):
    rows, width = mids[0].shape
    n_slots, _, cols = hidden.shape
    shapes = [[(len(picks), n_blocks, block_rows, 3 * cols) for picks, _ in gs] for gs in groups]
    n_out = [len(gs) for gs in groups]

    def body(offs_ref, mo, ms, do, ds, hid_ref, d_ref, *rest):
        outs, rest = rest[: sum(n_out)], rest[sum(n_out) :]
        stages, (mid_t, dff_t, g_scr, sems) = rest[: sum(n_out)], rest[sum(n_out) :]
        s = pl.program_id(0)

        @pl.when(s == 0)
        def _():
            for i, (m_ref, x_ref) in enumerate(((mo, do), (ms, ds))):
                part = slice(i * rows, (i + 1) * rows)
                mid_t[:, part] = jnp.transpose(m_ref[...])
                dff_t[:, part] = jnp.transpose(x_ref[...])

        g_scr[:, : 2 * cols] = dot_nn(mid_t[...], d_ref[0])
        g_scr[:, 2 * cols :] = dot_nn(dff_t[...], hid_ref[0])
        for j in range(n_slots):
            at = sum(n_out[:j])

            @pl.when(s == j)
            def _(j=j, at=at):
                store_groups(groups[j], stages[at : at + n_out[j]], offs_ref, n_blocks, block_rows, g_scr)
                for o in range(at, at + n_out[j]):
                    pltpu.make_async_copy(stages[o], outs[o], sems.at[o]).start()

        @pl.when(s == n_slots - 1)
        def _():
            for o in range(sum(n_out)):
                pltpu.make_async_copy(stages[o], outs[o], sems.at[o]).wait()

    flat = [(shape, dtype) for ss, gs in zip(shapes, groups) for shape, (_, dtype) in zip(ss, gs)]
    full = whole_block((rows, width))
    results = pl.pallas_call(
        body,
        grid_spec=pltpu.PrefetchScalarGridSpec(
            num_scalar_prefetch=1,
            grid=(n_slots,),
            in_specs=[full] * 4
            + [
                pl.BlockSpec((1, 2 * rows, cols), lambda i, *_: (i, 0, 0)),
                pl.BlockSpec((1, 2 * rows, 2 * cols), lambda i, *_: (first + i, 0, 0)),
            ],
            out_specs=[pl.BlockSpec(memory_space=pl.ANY)] * len(flat),
            scratch_shapes=[pltpu.VMEM(shape, dtype) for shape, dtype in flat]
            + [
                pltpu.VMEM((width, 2 * rows), BF16),
                pltpu.VMEM((width, 2 * rows), BF16),
                pltpu.VMEM((width, 3 * cols), F32),
                pltpu.SemaphoreType.DMA((len(flat),)),
            ],
        ),
        out_shape=[jax.ShapeDtypeStruct(shape, dtype) for shape, dtype in flat],
        compiler_params=params(),
        name="ffn_grads",
    )(offsets, *mids, *dffs, hidden, d_both)
    return [results[sum(n_out[:j]) : sum(n_out[: j + 1])] for j in range(n_slots)]


def first_norm_back(normed1, inv_std1, d_second, d_mid, d_mid_sib, norms):
    rows, width = normed1.shape
    tile = min(256, rows)

    def body(n_ref, istd_ref, d2_ref, dm_ref, ds_ref, norm_ref, d_ref, dl_ref, ng_ref):
        grad = d2_ref[...] + dm_ref[...] + ds_ref[...].astype(F32)
        normed = n_ref[...]
        d = norm_back(normed, istd_ref[...], norm_ref[0:1, :], grad)
        d_ref[...] = d
        dl_ref[...] = d.astype(BF16)

        @pl.when(pl.program_id(0) == 0)
        def _():
            ng_ref[...] = jnp.zeros(ng_ref.shape, F32)

        ng_ref[0:1, :] += jnp.sum(grad * normed, axis=0, keepdims=True)
        ng_ref[1:2, :] += jnp.sum(grad, axis=0, keepdims=True)

    block = pl.BlockSpec((tile, width), lambda i: (i, 0))
    column = pl.BlockSpec((tile, 1), lambda i: (i, 0))
    return pl.pallas_call(
        body,
        grid=(rows // tile,),
        in_specs=[block, column, block, block, block, whole_block((8, width))],
        out_specs=[block] * 2 + [whole_block((8, width))],
        out_shape=[
            jax.ShapeDtypeStruct((rows, width), F32),
            jax.ShapeDtypeStruct((rows, width), BF16),
            jax.ShapeDtypeStruct((8, width), F32),
        ],
        compiler_params=params(),
        name="first_norm_back",
    )(normed1, inv_std1, d_second, d_mid, d_mid_sib, norms)


def out_grads(attended, d_first_low, norm1, norm2):
    rows, width = attended.shape

    def body(att_ref, dl_ref, n1_ref, n2_ref, out_ref):
        out_ref[:, :width] = dot_tn(att_ref[...], dl_ref[...]).astype(BF16)
        stacked = jnp.concatenate(
            [n1_ref[0:1, :], n2_ref[0:1, :], n1_ref[1:2, :], n2_ref[1:2, :],
             jnp.zeros((PAD - 4, width), F32)], axis=0)
        out_ref[:, width:] = jnp.transpose(stacked).astype(BF16)

    operands = (attended, d_first_low, norm1, norm2)
    return pl.pallas_call(
        body,
        grid=(1,),
        in_specs=[whole_block(o.shape) for o in operands],
        out_specs=whole_block((width, width + PAD)),
        out_shape=jax.ShapeDtypeStruct((width, width + PAD), BF16),
        compiler_params=params(),
        name="out_grads",
    )(*operands)


def unrotated(g, cos, sin):
    g = g.astype(BF16).astype(F32)
    return (g * cos - half_swap(g) * sin).astype(BF16)


def prepare_heads(d_att, att, dom, delta, at):
    n = d_att.shape[0]
    flipped = jnp.transpose(d_att.astype(F32) * att.astype(F32))
    for j in range(GROUP):
        delta[j : j + 1, at : at + n] = jnp.sum(flipped[j * HD : (j + 1) * HD, :], axis=0, keepdims=True)
        block = d_att[:, j // 2 * LANES : j // 2 * LANES + LANES].astype(F32)
        dom[j, at : at + n, :] = head_lanes(block, j, 0.0).astype(BF16)


def pair_up(even, odd):
    return head_lanes(even, 0, odd)


def attend_back_own(d_first, attended, lse, q, k, v, kt, key_from, key_to, cosine, sine, pieces, offsets, pos,
                    k_tile):
    rows, width = d_first.shape
    seq = q.shape[1]
    n_own = rows // k_tile
    group_cols = GROUP * HD
    held = Pieces([pieces], width, slice(3 * width, 4 * width))
    n_in = len(held.flat)
    n_q = key_from.shape[0] * rows // seq

    def body(pos_ref, offs_ref, from_ref, to_ref, d_ref, att_ref, lse_ref, q_ref, k_ref, v_ref, kt_ref,
             cos_ref, sin_ref, *rest):
        w_refs, rest = rest[:n_in], rest[n_in:]
        dq_ref, dk_ref, dv_ref, dom, delta, dq, w_scr, sems = rest
        g = pl.program_id(0)

        @pl.when(g == 0)
        def _():
            held.start(0, w_refs, offs_ref, w_scr, sems)
            held.wait(0, w_refs, offs_ref, w_scr, sems)

        w_rows = w_scr[0, pl.ds(pl.multiple_of(g * group_cols, group_cols), group_cols), :]
        d_att = dot_nt(d_ref[...], w_rows).astype(BF16)
        prepare_heads(d_att, att_ref[...], dom, delta, 0)
        own_low = pos_ref[0] * n_own

        def weights_of(j, at, n):
            cols = slice(j // 2 * LANES, j // 2 * LANES + LANES)
            s = dot_nt(k_ref[j, pl.ds(at, n), :], q_ref[j])
            p = jnp.exp(s - lse_ref[0, j : j + 1, :])
            dp = dot_nt(v_ref[pl.ds(at, n), cols], dom[j])
            return p, (p * (dp - delta[j : j + 1, :])).astype(BF16)

        base = pl.multiple_of(pos_ref[0] * rows, rows)
        for b in range(GROUP // 2):
            dks, dvs = [], []
            for j in (2 * b, 2 * b + 1):
                p, ds = weights_of(j, base, rows)
                dvs.append(dot_nn(p.astype(BF16), dom[j]))
                dks.append(dot_nn(ds, q_ref[j]))
                heads = slice(j * HD, (j + 1) * HD)
                total = None
                for t in range(n_own):
                    part = dot_nn(kt_ref[own_low + t, heads, :], ds[t * k_tile : (t + 1) * k_tile, :])
                    total = part if total is None else total + part
                dq[heads, :] = total
            cols = slice(b * LANES, (b + 1) * LANES)
            dk_ref[:, cols] = pair_up(*dks)
            dv_ref[:, cols] = dvs[0] + dvs[1]

        first_tile = pos_ref[0] * n_q
        low = from_ref[first_tile]
        high = to_ref[first_tile + n_q - 1]
        n_left = jnp.maximum(own_low - low, 0)
        n_right = jnp.maximum(high - own_low - n_own, 0)

        def outside(i, carry):
            tile = jnp.where(i < n_left, low + i, own_low + n_own + i - n_left)
            at = pl.multiple_of(tile * k_tile, k_tile)
            for j in range(GROUP):
                heads = slice(j * HD, (j + 1) * HD)
                _, ds = weights_of(j, at, k_tile)
                dq[heads, :] += dot_nn(kt_ref[tile, heads, :], ds)
            return carry

        lax.fori_loop(0, n_left + n_right, outside, 0)
        turned = jnp.transpose(dq[...]) * (HD**-0.5)
        for b in range(GROUP // 2):
            cols = slice(b * LANES, (b + 1) * LANES)
            dq_ref[:, cols] = unrotated(turned[:, cols], cos_ref[...], sin_ref[...])

    def col_block(n):
        return pl.BlockSpec((n, group_cols), lambda g, *_: (0, g))

    table = pl.BlockSpec((rows, LANES), lambda g, p, *_: (p[0], 0))
    sum_shape = jax.ShapeDtypeStruct((rows, width), F32)
    return pl.pallas_call(
        body,
        grid_spec=pltpu.PrefetchScalarGridSpec(
            num_scalar_prefetch=4,
            grid=(H // GROUP,),
            in_specs=[
                whole_block((rows, width)),
                col_block(rows),
                pl.BlockSpec((1, 8, rows), lambda g, *_: (g, 0, 0)),
                pl.BlockSpec((GROUP, rows, LANES), lambda g, p, *_: (g, p[0], 0)),
                pl.BlockSpec((GROUP, seq, LANES), lambda g, *_: (g, 0, 0)),
                col_block(seq),
                pl.BlockSpec((seq // k_tile, group_cols, k_tile), lambda g, *_: (0, g, 0)),
                table,
                table,
            ]
            + held.in_specs,
            out_specs=[col_block(rows)] * 3,
            scratch_shapes=[
                pltpu.VMEM((GROUP, rows, LANES), BF16),
                pltpu.VMEM((8, rows), F32),
                pltpu.VMEM((group_cols, rows), F32),
            ]
            + held.scratch,
        ),
        out_shape=[jax.ShapeDtypeStruct((rows, width), BF16), sum_shape, sum_shape],
        compiler_params=params(),
        name="attend_back_own",
    )(pos, offsets, key_from, key_to, d_first, attended, lse, q, k, v, kt, cosine, sine, *held.flat)


def attend_back_others(d_others, att_others, lse_others, sums, q, k, v, key_from, key_to, cosine, sine, pieces,
                       offsets, pos, q_tile, k_tile):
    rows, width = sums[0].shape
    seq = q.shape[1]
    n_q = rows // q_tile
    n_own = rows // k_tile
    n_tiles = d_others.shape[0] // q_tile
    group_cols = GROUP * HD
    held = Pieces([pieces], width, slice(3 * width, 4 * width))
    n_in = len(held.flat)

    def body(pos_ref, offs_ref, from_ref, to_ref, d_ref, att_ref, lse_ref, q_ref, k_ref, v_ref, dk_in, dv_in,
             cos_ref, sin_ref, *rest):
        w_refs, rest = rest[:n_in], rest[n_in:]
        dk_ref, dv_ref, dom, delta, dk, dv, w_scr, sems = rest
        g = pl.program_id(0)

        @pl.when(g == 0)
        def _():
            held.start(0, w_refs, offs_ref, w_scr, sems)
            held.wait(0, w_refs, offs_ref, w_scr, sems)

        dk[...] = dk_in[...]
        dv[...] = dv_in[...]
        own_low = pos_ref[0] * n_own

        for i in range(n_tiles):
            true_tile = (pos_ref[0] ^ (1 + i // n_q)) * n_q + i % n_q
            low = jnp.maximum(from_ref[true_tile], own_low)
            high = jnp.minimum(to_ref[true_tile], own_low + n_own)
            here = slice(i * q_tile, (i + 1) * q_tile)

            @pl.when(high > low)
            def _(i=i, true_tile=true_tile, low=low, high=high, here=here):
                w_rows = w_scr[0, pl.ds(pl.multiple_of(g * group_cols, group_cols), group_cols), :]
                d_att = dot_nt(d_ref[here, :], w_rows).astype(BF16)
                prepare_heads(d_att, att_ref[here, :], dom, delta, 0)
                q_at = pl.multiple_of(true_tile * q_tile, q_tile)

                def one(tile, carry):
                    at = pl.ds(pl.multiple_of((tile - own_low) * k_tile, k_tile), k_tile)
                    for b in range(GROUP // 2):
                        cols = slice(b * LANES, (b + 1) * LANES)
                        dks, dvs = [], []
                        for j in (2 * b, 2 * b + 1):
                            q_head = q_ref[j, pl.ds(q_at, q_tile), :]
                            s = dot_nt(k_ref[j, at, :], q_head)
                            p = jnp.exp(s - lse_ref[0, j : j + 1, here])
                            dp = dot_nt(v_ref[at, cols], dom[j])
                            ds = (p * (dp - delta[j : j + 1, :])).astype(BF16)
                            dvs.append(dot_nn(p.astype(BF16), dom[j]))
                            dks.append(dot_nn(ds, q_head))
                        dk[at, cols] += pair_up(*dks)
                        dv[at, cols] += dvs[0] + dvs[1]
                    return carry

                lax.fori_loop(low, high, one, 0)

        for b in range(GROUP // 2):
            cols = slice(b * LANES, (b + 1) * LANES)
            dk_ref[:, cols] = unrotated(dk[:, cols], cos_ref[...], sin_ref[...])
        dv_ref[...] = dv[...].astype(BF16)

    def col_block(n):
        return pl.BlockSpec((n, group_cols), lambda g, *_: (0, g))

    table = pl.BlockSpec((rows, LANES), lambda g, p, *_: (p[0], 0))
    return pl.pallas_call(
        body,
        grid_spec=pltpu.PrefetchScalarGridSpec(
            num_scalar_prefetch=4,
            grid=(H // GROUP,),
            in_specs=[
                whole_block(d_others.shape),
                col_block(d_others.shape[0]),
                pl.BlockSpec((1, 8, d_others.shape[0]), lambda g, *_: (g, 0, 0)),
                pl.BlockSpec((GROUP, seq, LANES), lambda g, *_: (g, 0, 0)),
                pl.BlockSpec((GROUP, rows, LANES), lambda g, p, *_: (g, p[0], 0)),
                pl.BlockSpec((rows, group_cols), lambda g, p, *_: (p[0], g)),
                col_block(rows),
                col_block(rows),
                table,
                table,
            ]
            + held.in_specs,
            out_specs=[col_block(rows)] * 2,
            scratch_shapes=[
                pltpu.VMEM((GROUP, q_tile, LANES), BF16),
                pltpu.VMEM((8, q_tile), F32),
                pltpu.VMEM((rows, group_cols), F32),
                pltpu.VMEM((rows, group_cols), F32),
            ]
            + held.scratch,
        ),
        out_shape=[jax.ShapeDtypeStruct((rows, width), BF16)] * 2,
        compiler_params=params(),
        name="attend_back_others",
    )(pos, offsets, key_from, key_to, d_others, att_others, lse_others, q, k, v, *sums, cosine, sine, *held.flat)


def qkv_grads(x_own, merged, out_part, offsets, groups, n_blocks, block_rows):
    rows, width = x_own.shape
    wide = 3 * width + out_part.shape[1]

    def body(offs_ref, x_ref, dq_ref, dk_ref, dv_ref, out_ref, *rest):
        group_refs, g_scr = rest[:-1], rest[-1]
        x_t = jnp.transpose(x_ref[...])
        for j, ref in enumerate((dq_ref, dk_ref, dv_ref)):
            g_scr[:, j * width : (j + 1) * width] = dot_nn(x_t, ref[...])
        g_scr[:, 3 * width :] = out_ref[...].astype(F32)
        store_groups(groups, group_refs, offs_ref, n_blocks, block_rows, g_scr)

    group_shapes = [(len(picks), n_blocks, block_rows, wide) for picks, _ in groups]
    return pl.pallas_call(
        body,
        grid_spec=pltpu.PrefetchScalarGridSpec(
            num_scalar_prefetch=1,
            grid=(1,),
            in_specs=[whole_block((rows, width))] * 4 + [whole_block(out_part.shape)],
            out_specs=[whole_block(s) for s in group_shapes],
            scratch_shapes=[pltpu.VMEM((width, wide), F32)],
        ),
        out_shape=[jax.ShapeDtypeStruct(s, dtype) for s, (_, dtype) in zip(group_shapes, groups)],
        compiler_params=params(),
        name="qkv_grads",
    )(offsets, x_own, *merged, out_part)


def input_grads(merged, d_first, pieces, offsets):
    rows, width = d_first.shape
    tile = min(256, rows)
    held = Pieces([pieces], width, slice(0, 3 * width))
    n_in = len(held.flat)

    def body(offs_ref, dq_ref, dk_ref, dv_ref, df_ref, *rest):
        w_refs, (out_ref, w_scr, sems) = rest[:n_in], rest[n_in:]

        @pl.when(pl.program_id(0) == 0)
        def _():
            held.start(0, w_refs, offs_ref, w_scr, sems)
            held.wait(0, w_refs, offs_ref, w_scr, sems)

        total = df_ref[...]
        for j, ref in enumerate((dq_ref, dk_ref, dv_ref)):
            total = total + dot_nt(ref[...], w_scr[0, :, j * width : (j + 1) * width])
        out_ref[...] = total

    block = pl.BlockSpec((tile, width), lambda i, o: (i, 0))
    return pl.pallas_call(
        body,
        grid_spec=pltpu.PrefetchScalarGridSpec(
            num_scalar_prefetch=1,
            grid=(rows // tile,),
            in_specs=[block] * 4 + held.in_specs,
            out_specs=block,
            scratch_shapes=held.scratch,
        ),
        out_shape=jax.ShapeDtypeStruct((rows, width), F32),
        compiler_params=params(),
        name="input_grads",
    )(offsets, *merged, d_first, *held.flat)


def combine(kept, got):
    _, n_blocks, block_rows, wide = kept.shape

    def body(kept_ref, got_ref, own_ref, on_ref):
        own_ref[...] = kept_ref[0] + got_ref[0].astype(F32)
        on_ref[...] = (kept_ref[1] + got_ref[1].astype(F32)).astype(BF16)

    two = pl.BlockSpec((2, 1, block_rows, wide), lambda i: (0, i, 0, 0))
    one = pl.BlockSpec((1, block_rows, wide), lambda i: (i, 0, 0))
    shape = (n_blocks, block_rows, wide)
    return pl.pallas_call(
        body,
        grid=(n_blocks,),
        in_specs=[two, two],
        out_specs=[one, one],
        out_shape=[jax.ShapeDtypeStruct(shape, F32), jax.ShapeDtypeStruct(shape, BF16)],
        compiler_params=params(),
        name="combine",
    )(kept, got)


def make_per_device(ndp, nt):
    plane = ndp // 2

    def move(value, chip=0, core=0, flip=0):
        pairs = []
        for d in range(ndp):
            for t in range(nt):
                to_d = ((d // 2) ^ chip) * 2 + ((d % 2) ^ core)
                pairs.append((d * nt + t, to_d * nt + (t ^ flip)))
        return lax.ppermute(value, AXES, pairs)

    def after(value, *others):
        return lax.optimization_barrier((value, *others))[0]

    def per_device(inputs, segment_ids, qkv_weight, out_weight, norm_gains, norm_biases,
                   gate_weight, up_weight, down_weight, out_grad):
        rows, width = inputs.shape
        seq = segment_ids.shape[1]
        n_row = seq // rows
        q_tile = min(256, rows)
        k_tile = min(256, rows)
        shard = qkv_weight.shape[0]
        ffn_rows, ffn_cols = gate_weight.shape
        half = ffn_cols // 2
        fast = plane == 4 and nt == 4 and n_row == 2

        d_index = lax.axis_index("dp")
        core = d_index % 2
        chip = d_index // 2
        t_index = lax.axis_index("tensor")
        pos = (t_index % n_row).astype(jnp.int32)
        block_at = [((chip ^ dxy) * 2 + (core ^ other)) for dxy in range(4) for other in range(2)]

        packed = jnp.concatenate(
            [qkv_weight, out_weight, norm_gains.T, norm_biases.T,
             jnp.zeros((shard, PAD - 4), BF16)], axis=1)
        seg = lax.dynamic_index_in_dim(segment_ids, t_index // n_row, 0, keepdims=False)
        doc_from = jnp.sum((seg[None, :] < seg[:, None]).astype(jnp.int32), axis=1)
        doc_to = jnp.sum((seg[None, :] <= seg[:, None]).astype(jnp.int32), axis=1)
        place = (jnp.arange(seq, dtype=jnp.int32) - doc_from).astype(F32)
        lane = np.arange(LANES)
        frequency = rope_base ** (-jnp.asarray(lane % (HD // 2), F32) * 2.0 / HD)
        angles = place[:, None] * frequency[None, :]
        cosine = jnp.cos(angles)
        sine = jnp.sin(angles) * jnp.asarray(np.where(lane % HD < HD // 2, -1.0, 1.0), F32)[None, :]
        key_from = doc_from[::q_tile] // k_tile
        key_to = (doc_to[q_tile - 1 :: q_tile] + k_tile - 1) // k_tile
        seg_col = seg[:, None]
        seg_row = seg.reshape(seq // q_tile, 1, q_tile)
        pos_arr = pos[None]

        ffn = (gate_weight, up_weight, down_weight.T)
        mine, given = [
            jnp.concatenate([lax.dynamic_slice_in_dim(w, c * half, half, 1) for w in ffn], axis=1)
            for c in (core, 1 - core)
        ]
        if fast:
            pair = jnp.stack([mine, move(given, core=1)])
            slots = [[pair, move(pair, chip=1), move(pair, chip=2)]]
            x_others = [move(inputs, flip=1)]
            slots += [[move(pair, flip=s)] for s in (1, 2, 3)]

            def spread(s, *others):
                one = after(slots[s][0], *others)
                slots[s] += [move(one, chip=1), move(one, chip=2)]

            def spread_on(s, *others):
                side, chip_step = (1, 2) if s % 2 == 0 else (2, 1)
                slots[s].append(move(after(slots[s][side], *others), chip=chip_step))

            by_flip = [packed] + [move(packed, flip=e) for e in range(1, nt)]
            near = jnp.concatenate(
                [lax.select_n(t_index, *[by_flip[j ^ t] for t in range(nt)]) for j in range(nt)], axis=0)[None]
            far = [move(near, chip=dxy) for dxy in range(1, 4)]
            near_sib = move(near, core=1)
            far_sib = move(
                after(jnp.concatenate(far, axis=0), slots[1][0], *x_others, cosine, sine, key_from, key_to),
                core=1)
            spread_on(0, *far)
            spread(1, *far)
            x_rel = after(jnp.concatenate([inputs] + x_others, axis=0), *slots[1][1:])
            w_pieces = [near, *far, near_sib, far_sib]
            w_offsets = jnp.stack(
                [((chip ^ dxy) * 2 + (core ^ other)) * (nt * shard) for other in range(2) for dxy in range(4)]
            ).astype(jnp.int32)
            f_offsets = jnp.stack([b * ffn_rows for b in block_at]).astype(jnp.int32)
            n_blocks, block_rows = 2, ffn_rows
        else:
            x_others = [move(inputs, flip=e) for e in range(1, n_row)]
            x_rel = jnp.concatenate([inputs] + x_others, axis=0)
            w_pieces = [lax.all_gather(packed, AXES, axis=0, tiled=True)[None]]
            w_offsets = jnp.zeros((1,), jnp.int32)
            full = lax.all_gather(mine, "dp", axis=0, tiled=True).reshape(width, 3, half)
            full = lax.all_gather(full, "tensor", axis=2, tiled=True)
            slots = [[full.reshape(1, width, 3 * half * nt)]]
            f_offsets = jnp.zeros((1,), jnp.int32)
            n_blocks, block_rows = 1, width

        q, k, v, kt, vt, norms = project(
            x_rel, w_pieces, w_offsets, cosine, sine, seg_col, pos_arr, n_row, k_tile)
        if fast:
            spread_on(1, q)
        attended, lse, normed1, inv_std1, mid = attend(
            inputs, q, k, vt, w_pieces, w_offsets, norms, pos_arr)
        if fast:
            spread(2, mid)
            spread(3, mid)
            spread_on(2, mid)
            spread_on(3, mid)
        mid_sib = move(mid, core=1)

        calls = [slots[:2], slots[2:]] if fast else [slots]
        acts, partial = [], None
        for j, some in enumerate(calls):
            hid, fac_a, fac_b, *partial = feed_forward(
                mid, mid_sib, some, f_offsets, partial[0] if j else None, j == len(calls) - 1)
            acts.append((hid, fac_a, fac_b))
        part_own, part_sib = partial
        att_others = [move(attended, flip=e) for e in range(1, n_row)]
        lse_others = [move(lse, flip=e) for e in range(1, n_row)]
        part_sib = move(after(part_sib, *att_others, *lse_others), core=1)
        outputs, d_second, d_ffn, norm2 = second_norm(normed1, part_own, part_sib, out_grad, norms)
        d_ffn_sib = move(d_ffn, core=1)
        d_both, d_mid, d_mid_give = hidden_back(
            (d_ffn, d_ffn_sib), [a[1:] for a in acts], slots, f_offsets)
        d_mid_sib = move(d_mid_give, core=1)

        def groups_of(s):
            if not fast:
                return [((0,), BF16)]
            if s % 2 == 0:
                return [((2, 3), BF16), ((0, 1), F32)]
            return [((1, 3), BF16), ((0, 2), F32)]

        def weight_grads(j, d_both):
            first = sum(len(c) for c in calls[:j])
            return ffn_grads(
                first, (mid, mid_sib), (d_ffn, d_ffn_sib), acts[j][0], d_both, f_offsets,
                [groups_of(first + i) for i in range(len(calls[j]))], n_blocks, block_rows)

        d_first, d_first_low, norm1 = first_norm_back(
            normed1, inv_std1, d_second, d_mid, d_mid_sib, norms)
        d_others = [move(d_first_low, flip=e) for e in range(1, n_row)]
        d_both = after(d_both, d_first_low)
        reduced = [r for j in range(len(calls)) for r in weight_grads(j, d_both)]

        def turn(s):
            return (2, 1) if s % 2 == 0 else (1, 2)

        arrived, owned = {}, {}
        if fast:
            arrived = {s: move(reduced[s][0], chip=turn(s)[0]) for s in range(nt)}

        def combine_on(s):
            own, on = combine(reduced[s][1], arrived[s])
            owned[s] = (own, move(on, chip=turn(s)[1]))

        def owned_sum(s, *others):
            own, on = owned[s]
            mine = own + after(on, *others).astype(F32)
            return mine.astype(BF16) if s else mine

        dq, *sums = attend_back_own(
            after(d_first_low, *[r[-1] for r in reduced]), attended, lse, q, k, v, kt, key_from, key_to,
            cosine, sine, w_pieces, w_offsets, pos_arr, k_tile)
        if fast:
            arrived[0], arrived[1] = after(arrived[0], dq), after(arrived[1], dq)
            combine_on(0)
            combine_on(1)
            sums[0] = after(sums[0], owned[0][0], owned[1][0])
        dk, dv = attend_back_others(
            jnp.concatenate(d_others, axis=0), jnp.concatenate(att_others, axis=0),
            jnp.concatenate(lse_others, axis=2), sums, q, k, v, key_from, key_to, cosine, sine,
            w_pieces, w_offsets, pos_arr, q_tile, k_tile)
        out_part = out_grads(attended, d_first_low, norm1, norm2)
        if fast:
            sent = {s: owned_sum(s, dk) for s in (0, 1)}
            arrived[2], arrived[3] = after(arrived[2], dk), after(arrived[3], dk)
            combine_on(2)
            combine_on(3)
            dv = after(dv, owned[2][0], owned[3][0], sent[1])
        merged = (dq, dk, dv)

        if fast:
            q_groups = [((1, 3, 5, 7), BF16), ((0, 2, 4, 6), F32)]
            q_offsets = jnp.stack([b * (nt * shard) for b in block_at]).astype(jnp.int32)
            q_rows = nt * shard
        else:
            q_groups = [((0,), F32)]
            q_offsets = jnp.zeros((1,), jnp.int32)
            q_rows = width
        q_parts = qkv_grads(inputs, merged, out_part, q_offsets, q_groups, 1, q_rows)
        inputs_grad = input_grads(merged, d_first, w_pieces, w_offsets)

        if fast:
            sent.update({s: owned_sum(s, q_parts[0]) for s in (2, 3)})
            back = [move(sent[s], flip=s) for s in range(1, nt)]
            q_other = after(move(q_parts[0], core=1), inputs_grad)
            q_sum = q_parts[1][:, 0] + q_other[:, 0].astype(F32)
            q_own = q_sum[0]
            for dxy in range(1, 4):
                q_own = q_own + move(q_sum[dxy].astype(BF16), chip=dxy).astype(F32)
            back = lax.optimization_barrier((*back, q_own))[:-1]
            total = sent[0] + sum(b.astype(F32) for b in back)
            packed_grad = None
            for e in range(nt):
                piece = lax.dynamic_slice_in_dim(q_own, (t_index ^ e) * shard, shard, 0)
                if e:
                    piece = move(piece.astype(BF16), flip=e).astype(F32)
                packed_grad = piece if packed_grad is None else packed_grad + piece
            other = move(total[1], core=1)
            mine = total[0]
            grads = []
            for m in range(3):
                part = slice(m * half, (m + 1) * half)
                grads.append(jnp.where(
                    core == 0,
                    jnp.concatenate([mine[:, part], other[:, part]], axis=1),
                    jnp.concatenate([other[:, part], mine[:, part]], axis=1)))
        else:
            summed = lax.psum_scatter(
                reduced[0][0][0, 0].reshape(width, 3, half * nt), "tensor", scatter_dimension=2, tiled=True)
            spread = jnp.zeros((width, 3, 2 * half), BF16)
            spread = lax.dynamic_update_slice_in_dim(spread, summed.astype(BF16), core * half, 2)
            spread = lax.psum_scatter(spread, "dp", scatter_dimension=0, tiled=True).astype(F32)
            grads = [spread[:, m] for m in range(3)]
            packed_grad = lax.psum_scatter(q_parts[0][0, 0], AXES, scatter_dimension=0, tiled=True)

        return (
            outputs,
            inputs_grad,
            packed_grad[:, : 3 * width],
            packed_grad[:, 3 * width : 4 * width],
            packed_grad[:, 4 * width : 4 * width + 2].T,
            packed_grad[:, 4 * width + 2 : 4 * width + 4].T,
            grads[0],
            grads[1],
            grads[2].T,
        )

    return per_device


def solution(mesh):
    tokens = P(AXES, None)
    both = P("dp", "tensor")
    return jax.shard_map(
        make_per_device(mesh.shape["dp"], mesh.shape["tensor"]),
        mesh=mesh,
        in_specs=(tokens, P("dp", None), tokens, tokens, P(None, AXES), P(None, AXES),
                  both, both, P("tensor", "dp"), tokens),
        out_specs=(tokens, tokens, tokens, tokens, P(None, AXES), P(None, AXES),
                   both, both, P("tensor", "dp")),
        check_vma=False,
    )
```

```python
import jax
import jax.numpy as jnp
import numpy as np
from jax import lax
from jax.experimental import pallas as pl
from jax.experimental.pallas import tpu as pltpu
from jax.sharding import PartitionSpec as P

H = 12
HD = 64
LANES = 128
PAD = 128
NEG = -1e30

rope_base = 1000.0
layer_eps = 1e-12

AXES = ("dp", "tensor")
F32 = jnp.float32
BF16 = jnp.bfloat16


def params(mebibytes):
    return pltpu.CompilerParams(
        dimension_semantics=("arbitrary",), vmem_limit_bytes=mebibytes * 2**20
    )


def whole_block(shape):
    zeros = (0,) * len(shape)
    return pl.BlockSpec(shape, lambda *_: zeros, pipeline_mode=pl.Buffered(1))


def dot_nn(a, b):
    return lax.dot_general(a, b, (((1,), (0,)), ((), ())), preferred_element_type=F32)


def dot_nt(a, b):
    return lax.dot_general(a, b, (((1,), (1,)), ((), ())), preferred_element_type=F32)


def dot_tn(a, b):
    return lax.dot_general(a, b, (((0,), (0,)), ((), ())), preferred_element_type=F32)


def half_swap(block):
    lane = lax.broadcasted_iota(jnp.int32, block.shape, 1)
    return jnp.where(
        lane % HD < HD // 2, pltpu.roll(block, LANES - HD // 2, 1), pltpu.roll(block, HD // 2, 1)
    )


def normalise(summed):
    mean = jnp.mean(summed, axis=-1, keepdims=True)
    centred = summed - mean
    inv_std = lax.rsqrt(jnp.mean(centred * centred, axis=-1, keepdims=True) + layer_eps)
    return centred * inv_std, inv_std


def norm_back(normed, inv_std, gain, grad):
    scaled = grad * gain
    return inv_std * (
        scaled
        - jnp.mean(scaled, axis=-1, keepdims=True)
        - normed * jnp.mean(scaled * normed, axis=-1, keepdims=True)
    )


def in_hbm(x):
    return pltpu.with_memory_space_constraint(x, pltpu.HBM)


class Pieces:
    def __init__(self, slots, width, cols=None):
        self.flat = [in_hbm(p) for slot in slots for p in slot]
        self.n_slots = len(slots)
        self.n_pieces = len(slots[0])
        self.blocks = [(p, b) for p in range(self.n_pieces) for b in range(slots[0][p].shape[0])]
        _, self.block_rows, wide = slots[0][0].shape
        self.cols = cols or slice(0, wide)
        self.in_specs = [pl.BlockSpec(memory_space=pl.ANY)] * len(self.flat)
        self.scratch = [
            pltpu.VMEM((self.n_slots, width, self.cols.stop - self.cols.start), BF16),
            pltpu.SemaphoreType.DMA((self.n_slots, len(self.blocks))),
        ]

    def copies(self, slot, refs, offs_ref, scr, sems):
        for j, (p, b) in enumerate(self.blocks):
            start = pl.multiple_of(offs_ref[j], 16)
            yield pltpu.make_async_copy(
                refs[slot * self.n_pieces + p].at[b, :, self.cols],
                scr.at[slot, pl.ds(start, self.block_rows), :],
                sems.at[slot, j],
            )

    def start(self, slot, *args):
        for copy in self.copies(slot, *args):
            copy.start()

    def wait(self, slot, *args):
        for copy in self.copies(slot, *args):
            copy.wait()

    def start_all(self, *args):
        for s in range(self.n_slots):
            self.start(s, *args)

    def wait_for_step(self, step, *args):
        for s in range(self.n_slots):

            @pl.when(step == s)
            def _(s=s):
                self.wait(s, *args)


def head_lanes(block, h, extra):
    lane = lax.broadcasted_iota(jnp.int32, block.shape, 1)
    mine = lane < HD if h % 2 == 0 else lane >= HD
    return jnp.where(mine, block, extra)


def project(x_rel, pieces, offsets, cosine, sine, seg_col, pos, n_row, k_tile):
    seq, width = x_rel.shape
    rows = seq // n_row
    tile = min(256, rows)
    per_piece = rows // tile
    held = Pieces([pieces], width)
    n_in = len(held.flat)

    def true_tile(i, pos_ref):
        return (pos_ref[0] ^ (i // per_piece)) * per_piece + i % per_piece

    def body(pos_ref, offs_ref, x_ref, cos_ref, sin_ref, seg_ref, *rest):
        w_refs, rest = rest[:n_in], rest[n_in:]
        q_ref, k_ref, v_ref, kt_ref, vt_ref, norm_ref, w_scr, sems = rest

        @pl.when(pl.program_id(0) == 0)
        def _():
            held.start(0, w_refs, offs_ref, w_scr, sems)
            held.wait(0, w_refs, offs_ref, w_scr, sems)
            norm_ref[...] = jnp.transpose(w_scr[0, :, 4 * width :].astype(F32))[:8, :]

        x = x_ref[...]
        cos = cos_ref[...]
        sin = sin_ref[...]
        lane = lax.broadcasted_iota(jnp.int32, (tile, LANES), 1)
        same = lane % HD == seg_ref[...]
        key_extra = jnp.where(same, 1.0, 0.0)
        query_extra = jnp.where(same, 0.0, NEG)
        merged = dot_nn(x, w_scr[0, :, : 3 * width])
        for b in range(width // LANES):
            cols = slice(b * LANES, (b + 1) * LANES)
            q = merged[:, b * LANES : (b + 1) * LANES]
            k = merged[:, width + b * LANES : width + (b + 1) * LANES]
            v = merged[:, 2 * width + b * LANES : 2 * width + (b + 1) * LANES]
            q = (q * cos + half_swap(q) * sin) * (HD**-0.5)
            k = k * cos + half_swap(k) * sin
            for h in (2 * b, 2 * b + 1):
                q_ref[h] = head_lanes(q, h, query_extra).astype(BF16)
                k_ref[h] = head_lanes(k, h, key_extra).astype(BF16)
            v_ref[:, cols] = v.astype(BF16)
            vt_ref[cols, :] = jnp.transpose(v).astype(BF16)
            for j in range(tile // k_tile):
                kt_ref[j, cols, :] = jnp.transpose(k[j * k_tile : (j + 1) * k_tile, :]).astype(BF16)

    row_block = pl.BlockSpec((tile, width), lambda i, p, o: (true_tile(i, p), 0))
    head_block = pl.BlockSpec((H, tile, LANES), lambda i, p, o: (0, true_tile(i, p), 0))
    table_block = pl.BlockSpec((tile, LANES), lambda i, p, o: (true_tile(i, p), 0))
    return pl.pallas_call(
        body,
        grid_spec=pltpu.PrefetchScalarGridSpec(
            num_scalar_prefetch=2,
            grid=(seq // tile,),
            in_specs=[
                pl.BlockSpec((tile, width), lambda i, p, o: (i, 0)),
                table_block,
                table_block,
                pl.BlockSpec((tile, 1), lambda i, p, o: (true_tile(i, p), 0)),
            ]
            + held.in_specs,
            out_specs=[
                head_block,
                head_block,
                row_block,
                pl.BlockSpec((tile // k_tile, width, k_tile), lambda i, p, o: (true_tile(i, p), 0, 0)),
                pl.BlockSpec((width, tile), lambda i, p, o: (0, true_tile(i, p))),
                whole_block((8, width)),
            ],
            scratch_shapes=held.scratch,
        ),
        out_shape=[jax.ShapeDtypeStruct((H, seq, LANES), BF16)] * 2
        + [
            jax.ShapeDtypeStruct((seq, width), BF16),
            jax.ShapeDtypeStruct((seq // k_tile, width, k_tile), BF16),
            jax.ShapeDtypeStruct((width, seq), BF16),
            jax.ShapeDtypeStruct((8, width), F32),
        ],
        compiler_params=params(20),
        name="project",
    )(pos, offsets, x_rel, cosine, sine, seg_col, *held.flat)


GROUP = 4


def attend(x_own, q, k, vt, pieces, offsets, norms, pos):
    rows, width = x_own.shape
    seq = q.shape[1]
    group_cols = GROUP * HD
    n_steps = H // GROUP
    held = Pieces([pieces], width, slice(3 * width, 4 * width))
    n_in = len(held.flat)

    def body(pos_ref, offs_ref, x_ref, q_ref, k_ref, vt_ref, norm_ref, *rest):
        w_refs, rest = rest[:n_in], rest[n_in:]
        att_ref, lse_ref, n_ref, istd_ref, mid_ref, acc, lse, w_scr, sems = rest
        g = pl.program_id(0)

        @pl.when(g == 0)
        def _():
            held.start(0, w_refs, offs_ref, w_scr, sems)

        for j in range(GROUP):
            s = dot_nt(k_ref[j], q_ref[j])
            peak = jnp.max(s, axis=0, keepdims=True)
            e = jnp.exp(s - peak)
            total = jnp.sum(e, axis=0, keepdims=True)
            out = dot_nn(vt_ref[j * HD : (j + 1) * HD, :], e.astype(BF16))
            acc[g, j * HD : (j + 1) * HD, :] = out / total
            lse[g, j : j + 1, :] = peak + jnp.log(total)

        @pl.when(g == n_steps - 1)
        def _():
            held.wait(0, w_refs, offs_ref, w_scr, sems)
            for i in range(n_steps):
                lse_ref[i] = lse[i]
                att_ref[:, i * group_cols : (i + 1) * group_cols] = jnp.transpose(acc[i]).astype(BF16)
            first_sum = x_ref[...].astype(F32) + dot_nn(att_ref[...], w_scr[0])
            normed, inv_std = normalise(first_sum)
            n_ref[...] = normed
            istd_ref[...] = inv_std
            mid_ref[...] = (normed * norm_ref[0:1, :] + norm_ref[2:3, :]).astype(BF16)

    own = whole_block((rows, width))
    return pl.pallas_call(
        body,
        grid_spec=pltpu.PrefetchScalarGridSpec(
            num_scalar_prefetch=2,
            grid=(n_steps,),
            in_specs=[
                own,
                pl.BlockSpec((GROUP, rows, LANES), lambda g, p, o: (g, p[0], 0)),
                pl.BlockSpec((GROUP, seq, LANES), lambda g, p, o: (g, 0, 0)),
                pl.BlockSpec((group_cols, seq), lambda g, p, o: (g, 0)),
                whole_block((8, width)),
            ]
            + held.in_specs,
            out_specs=[own, whole_block((n_steps, 8, rows)), own, whole_block((rows, 1)), own],
            scratch_shapes=[
                pltpu.VMEM((n_steps, group_cols, rows), F32),
                pltpu.VMEM((n_steps, 8, rows), F32),
            ]
            + held.scratch,
        ),
        out_shape=[
            jax.ShapeDtypeStruct((rows, width), BF16),
            jax.ShapeDtypeStruct((n_steps, 8, rows), F32),
            jax.ShapeDtypeStruct((rows, width), F32),
            jax.ShapeDtypeStruct((rows, 1), F32),
            jax.ShapeDtypeStruct((rows, width), BF16),
        ],
        compiler_params=params(18),
        name="attend",
    )(pos, offsets, x_own, q, k, vt, norms, *held.flat)


def feed_forward(mid_own, mid_sib, slots, offsets, before, last):
    rows, width = mid_own.shape
    held = Pieces(slots, width)
    n_slots, cols = held.n_slots, held.cols.stop // 3
    n_in = len(held.flat)

    def body(offs_ref, own_ref, sib_ref, *rest):
        w_refs, rest = rest[:n_in], rest[n_in:]
        if before is not None:
            before_ref, rest = rest[0], rest[1:]
        if last:
            hid_ref, a_ref, b_ref, out_own, out_sib, acc, w_scr, sems = rest
        else:
            hid_ref, a_ref, b_ref, acc, w_scr, sems = rest
        s = pl.program_id(0)

        @pl.when(s == 0)
        def _():
            held.start_all(w_refs, offs_ref, w_scr, sems)
            acc[...] = jnp.zeros(acc.shape, F32) if before is None else before_ref[...]

        held.wait_for_step(s, w_refs, offs_ref, w_scr, sems)
        for i, x_ref in enumerate((own_ref, sib_ref)):
            part = slice(i * rows, (i + 1) * rows)
            both = dot_nn(x_ref[...], w_scr[s, :, : 2 * cols])
            gate, up = both[:, :cols], both[:, cols:]
            sig = 0.5 * jnp.tanh(0.5 * gate) + 0.5
            silu = gate * sig
            hidden = (silu * up).astype(BF16)
            hid_ref[0, part, :] = hidden
            a_ref[0, part, :] = (up * (sig + silu * (1.0 - sig))).astype(BF16)
            b_ref[0, part, :] = silu.astype(BF16)
            acc[part, :] += dot_nt(hidden, w_scr[s, :, 2 * cols :])

        if last:

            @pl.when(s == n_slots - 1)
            def _():
                out_own[...] = acc[:rows, :]
                out_sib[...] = acc[rows:, :].astype(BF16)

    full = whole_block((rows, width))
    both_block = whole_block((2 * rows, width))
    act = pl.BlockSpec((1, 2 * rows, cols), lambda i, *_: (i, 0, 0))
    act_shape = jax.ShapeDtypeStruct((n_slots, 2 * rows, cols), BF16)
    extra = [] if before is None else [before]
    if last:
        acc_specs = [full, full]
        acc_shapes = [jax.ShapeDtypeStruct((rows, width), F32), jax.ShapeDtypeStruct((rows, width), BF16)]
        acc_scratch = [pltpu.VMEM((2 * rows, width), F32)]
    else:
        acc_specs = [both_block]
        acc_shapes = [jax.ShapeDtypeStruct((2 * rows, width), F32)]
        acc_scratch = []
    return pl.pallas_call(
        body,
        grid_spec=pltpu.PrefetchScalarGridSpec(
            num_scalar_prefetch=1,
            grid=(n_slots,),
            in_specs=[full, full] + held.in_specs + [both_block] * len(extra),
            out_specs=[act] * 3 + acc_specs,
            scratch_shapes=acc_scratch + held.scratch,
        ),
        out_shape=[act_shape] * 3 + acc_shapes,
        compiler_params=params(18),
        name="feed_forward",
    )(offsets, mid_own, mid_sib, *held.flat, *extra)


def second_norm(normed1, part_own, part_sib, out_grad, norms):
    rows, width = normed1.shape
    tile = min(256, rows)

    def body(n_ref, own_ref, sib_ref, g_ref, norm_ref, out_ref, d_ref, dl_ref, ng_ref):
        middle = n_ref[...] * norm_ref[0:1, :] + norm_ref[2:3, :]
        second_sum = middle + (own_ref[...] + sib_ref[...].astype(F32))
        normed, inv_std = normalise(second_sum)
        out_ref[...] = (normed * norm_ref[1:2, :] + norm_ref[3:4, :]).astype(BF16)
        grad = g_ref[...].astype(F32)
        d = norm_back(normed, inv_std, norm_ref[1:2, :], grad)
        d_ref[...] = d
        dl_ref[...] = d.astype(BF16)

        @pl.when(pl.program_id(0) == 0)
        def _():
            ng_ref[...] = jnp.zeros(ng_ref.shape, F32)

        ng_ref[0:1, :] += jnp.sum(grad * normed, axis=0, keepdims=True)
        ng_ref[1:2, :] += jnp.sum(grad, axis=0, keepdims=True)

    block = pl.BlockSpec((tile, width), lambda i: (i, 0))
    return pl.pallas_call(
        body,
        grid=(rows // tile,),
        in_specs=[block] * 4 + [whole_block((8, width))],
        out_specs=[block] * 3 + [whole_block((8, width))],
        out_shape=[
            jax.ShapeDtypeStruct((rows, width), BF16),
            jax.ShapeDtypeStruct((rows, width), F32),
            jax.ShapeDtypeStruct((rows, width), BF16),
            jax.ShapeDtypeStruct((8, width), F32),
        ],
        compiler_params=params(10),
        name="second_norm",
    )(normed1, part_own, part_sib, out_grad, norms)


def hidden_back(dffs, factors, slots, offsets):
    rows, width = dffs[0].shape
    held = Pieces(slots, width)
    n_slots, cols = held.n_slots, held.cols.stop // 3
    n_in = len(held.flat)
    per_call = factors[0][0].shape[0]
    n_fac = len(factors)

    def body(offs_ref, do_ref, ds_ref, *rest):
        fac_refs, rest = rest[: 2 * n_fac], rest[2 * n_fac :]
        w_refs, rest = rest[:n_in], rest[n_in:]
        d_ref, out_own, out_sib, acc, w_scr, sems = rest
        s = pl.program_id(0)

        @pl.when(s == 0)
        def _():
            held.start_all(w_refs, offs_ref, w_scr, sems)
            acc[...] = jnp.zeros(acc.shape, F32)

        held.wait_for_step(s, w_refs, offs_ref, w_scr, sems)

        def work(a_ref, b_ref):
            for i, x_ref in enumerate((do_ref, ds_ref)):
                part = slice(i * rows, (i + 1) * rows)
                dh = dot_nn(x_ref[...], w_scr[s, :, 2 * cols :])
                d_ref[0, part, :cols] = (dh * a_ref[0, part, :].astype(F32)).astype(BF16)
                d_ref[0, part, cols:] = (dh * b_ref[0, part, :].astype(F32)).astype(BF16)
                acc[part, :] += dot_nt(d_ref[0, part, :], w_scr[s, :, : 2 * cols])

        for f in range(n_fac):

            @pl.when(s // per_call == f)
            def _(f=f):
                work(fac_refs[2 * f], fac_refs[2 * f + 1])

        @pl.when(s == n_slots - 1)
        def _():
            out_own[...] = acc[:rows, :]
            out_sib[...] = acc[rows:, :].astype(BF16)

    full = whole_block((rows, width))

    def fac_spec(f):
        return pl.BlockSpec(
            (1, 2 * rows, cols), lambda i, *_: (jnp.clip(i - f * per_call, 0, per_call - 1), 0, 0)
        )

    return pl.pallas_call(
        body,
        grid_spec=pltpu.PrefetchScalarGridSpec(
            num_scalar_prefetch=1,
            grid=(n_slots,),
            in_specs=[full, full]
            + [fac_spec(f) for f in range(n_fac) for _ in range(2)]
            + held.in_specs,
            out_specs=[pl.BlockSpec((1, 2 * rows, 2 * cols), lambda i, *_: (i, 0, 0)), full, full],
            scratch_shapes=[pltpu.VMEM((2 * rows, width), F32)] + held.scratch,
        ),
        out_shape=[
            jax.ShapeDtypeStruct((n_slots, 2 * rows, 2 * cols), BF16),
            jax.ShapeDtypeStruct((rows, width), F32),
            jax.ShapeDtypeStruct((rows, width), BF16),
        ],
        compiler_params=params(22),
        name="hidden_back",
    )(offsets, *dffs, *[x for pair in factors for x in pair], *held.flat)


def store_groups(groups, group_refs, offs_ref, n_blocks, block_rows, source):
    for (picks, dtype), ref in zip(groups, group_refs):
        for j, p in enumerate(picks):
            for b in range(n_blocks):
                start = pl.multiple_of(offs_ref[p * n_blocks + b], 8)
                ref[j, b] = source[pl.ds(start, block_rows), :].astype(dtype)


def ffn_grads(first, mids, dffs, hidden, d_both, offsets, groups, n_blocks, block_rows):
    rows, width = mids[0].shape
    n_slots, _, cols = hidden.shape
    shapes = [[(len(picks), n_blocks, block_rows, 3 * cols) for picks, _ in gs] for gs in groups]
    n_out = [len(gs) for gs in groups]

    def body(offs_ref, mo, ms, do, ds, hid_ref, d_ref, *rest):
        outs, rest = rest[: sum(n_out)], rest[sum(n_out) :]
        stages, (mid_t, dff_t, g_scr, sems) = rest[: sum(n_out)], rest[sum(n_out) :]
        s = pl.program_id(0)

        @pl.when(s == 0)
        def _():
            for i, (m_ref, x_ref) in enumerate(((mo, do), (ms, ds))):
                part = slice(i * rows, (i + 1) * rows)
                mid_t[:, part] = jnp.transpose(m_ref[...])
                dff_t[:, part] = jnp.transpose(x_ref[...])

        g_scr[:, : 2 * cols] = dot_nn(mid_t[...], d_ref[0])
        g_scr[:, 2 * cols :] = dot_nn(dff_t[...], hid_ref[0])
        for j in range(n_slots):
            at = sum(n_out[:j])

            @pl.when(s == j)
            def _(j=j, at=at):
                store_groups(groups[j], stages[at : at + n_out[j]], offs_ref, n_blocks, block_rows, g_scr)
                for o in range(at, at + n_out[j]):
                    pltpu.make_async_copy(stages[o], outs[o], sems.at[o]).start()

        @pl.when(s == n_slots - 1)
        def _():
            for o in range(sum(n_out)):
                pltpu.make_async_copy(stages[o], outs[o], sems.at[o]).wait()

    flat = [(shape, dtype) for ss, gs in zip(shapes, groups) for shape, (_, dtype) in zip(ss, gs)]
    full = whole_block((rows, width))
    results = pl.pallas_call(
        body,
        grid_spec=pltpu.PrefetchScalarGridSpec(
            num_scalar_prefetch=1,
            grid=(n_slots,),
            in_specs=[full] * 4
            + [
                pl.BlockSpec((1, 2 * rows, cols), lambda i, *_: (i, 0, 0)),
                pl.BlockSpec((1, 2 * rows, 2 * cols), lambda i, *_: (first + i, 0, 0)),
            ],
            out_specs=[pl.BlockSpec(memory_space=pl.ANY)] * len(flat),
            scratch_shapes=[pltpu.VMEM(shape, dtype) for shape, dtype in flat]
            + [
                pltpu.VMEM((width, 2 * rows), BF16),
                pltpu.VMEM((width, 2 * rows), BF16),
                pltpu.VMEM((width, 3 * cols), F32),
                pltpu.SemaphoreType.DMA((len(flat),)),
            ],
        ),
        out_shape=[jax.ShapeDtypeStruct(shape, dtype) for shape, dtype in flat],
        compiler_params=params(22),
        name="ffn_grads",
    )(offsets, *mids, *dffs, hidden, d_both)
    return [results[sum(n_out[:j]) : sum(n_out[: j + 1])] for j in range(n_slots)]


def first_norm_back(normed1, inv_std1, d_second, d_mid, d_mid_sib, norms):
    rows, width = normed1.shape
    tile = min(256, rows)

    def body(n_ref, istd_ref, d2_ref, dm_ref, ds_ref, norm_ref, d_ref, dl_ref, ng_ref):
        grad = d2_ref[...] + dm_ref[...] + ds_ref[...].astype(F32)
        normed = n_ref[...]
        d = norm_back(normed, istd_ref[...], norm_ref[0:1, :], grad)
        d_ref[...] = d
        dl_ref[...] = d.astype(BF16)

        @pl.when(pl.program_id(0) == 0)
        def _():
            ng_ref[...] = jnp.zeros(ng_ref.shape, F32)

        ng_ref[0:1, :] += jnp.sum(grad * normed, axis=0, keepdims=True)
        ng_ref[1:2, :] += jnp.sum(grad, axis=0, keepdims=True)

    block = pl.BlockSpec((tile, width), lambda i: (i, 0))
    column = pl.BlockSpec((tile, 1), lambda i: (i, 0))
    return pl.pallas_call(
        body,
        grid=(rows // tile,),
        in_specs=[block, column, block, block, block, whole_block((8, width))],
        out_specs=[block] * 2 + [whole_block((8, width))],
        out_shape=[
            jax.ShapeDtypeStruct((rows, width), F32),
            jax.ShapeDtypeStruct((rows, width), BF16),
            jax.ShapeDtypeStruct((8, width), F32),
        ],
        compiler_params=params(8),
        name="first_norm_back",
    )(normed1, inv_std1, d_second, d_mid, d_mid_sib, norms)


def out_grads(attended, d_first_low, norm1, norm2):
    rows, width = attended.shape

    def body(att_ref, dl_ref, n1_ref, n2_ref, out_ref):
        out_ref[:, :width] = dot_tn(att_ref[...], dl_ref[...]).astype(BF16)
        stacked = jnp.concatenate(
            [n1_ref[0:1, :], n2_ref[0:1, :], n1_ref[1:2, :], n2_ref[1:2, :],
             jnp.zeros((PAD - 4, width), F32)], axis=0)
        out_ref[:, width:] = jnp.transpose(stacked).astype(BF16)

    operands = (attended, d_first_low, norm1, norm2)
    return pl.pallas_call(
        body,
        grid=(1,),
        in_specs=[whole_block(o.shape) for o in operands],
        out_specs=whole_block((width, width + PAD)),
        out_shape=jax.ShapeDtypeStruct((width, width + PAD), BF16),
        compiler_params=params(10),
        name="out_grads",
    )(*operands)


def unrotated(g, cos, sin):
    g = g.astype(BF16).astype(F32)
    return (g * cos - half_swap(g) * sin).astype(BF16)


def prepare_heads(d_att, att, dom, delta, at):
    n = d_att.shape[0]
    flipped = jnp.transpose(d_att.astype(F32) * att.astype(F32))
    for j in range(GROUP):
        delta[j : j + 1, at : at + n] = jnp.sum(flipped[j * HD : (j + 1) * HD, :], axis=0, keepdims=True)
        block = d_att[:, j // 2 * LANES : j // 2 * LANES + LANES].astype(F32)
        dom[j, at : at + n, :] = head_lanes(block, j, 0.0).astype(BF16)


def pair_up(even, odd):
    return head_lanes(even, 0, odd)


def attend_back_own(d_first, attended, lse, q, k, v, kt, key_from, key_to, cosine, sine, pieces, offsets, pos,
                    k_tile):
    rows, width = d_first.shape
    seq = q.shape[1]
    n_own = rows // k_tile
    group_cols = GROUP * HD
    held = Pieces([pieces], width, slice(3 * width, 4 * width))
    n_in = len(held.flat)
    n_q = key_from.shape[0] * rows // seq

    def body(pos_ref, offs_ref, from_ref, to_ref, d_ref, att_ref, lse_ref, q_ref, k_ref, v_ref, kt_ref,
             cos_ref, sin_ref, *rest):
        w_refs, rest = rest[:n_in], rest[n_in:]
        dq_ref, dk_ref, dv_ref, dom, delta, dq, w_scr, sems = rest
        g = pl.program_id(0)

        @pl.when(g == 0)
        def _():
            held.start(0, w_refs, offs_ref, w_scr, sems)
            held.wait(0, w_refs, offs_ref, w_scr, sems)

        w_rows = w_scr[0, pl.ds(pl.multiple_of(g * group_cols, group_cols), group_cols), :]
        d_att = dot_nt(d_ref[...], w_rows).astype(BF16)
        prepare_heads(d_att, att_ref[...], dom, delta, 0)
        own_low = pos_ref[0] * n_own

        def weights_of(j, at, n):
            cols = slice(j // 2 * LANES, j // 2 * LANES + LANES)
            s = dot_nt(k_ref[j, pl.ds(at, n), :], q_ref[j])
            p = jnp.exp(s - lse_ref[0, j : j + 1, :])
            dp = dot_nt(v_ref[pl.ds(at, n), cols], dom[j])
            return p, (p * (dp - delta[j : j + 1, :])).astype(BF16)

        base = pl.multiple_of(pos_ref[0] * rows, rows)
        for b in range(GROUP // 2):
            dks, dvs = [], []
            for j in (2 * b, 2 * b + 1):
                p, ds = weights_of(j, base, rows)
                dvs.append(dot_nn(p.astype(BF16), dom[j]))
                dks.append(dot_nn(ds, q_ref[j]))
                heads = slice(j * HD, (j + 1) * HD)
                total = None
                for t in range(n_own):
                    part = dot_nn(kt_ref[own_low + t, heads, :], ds[t * k_tile : (t + 1) * k_tile, :])
                    total = part if total is None else total + part
                dq[heads, :] = total
            cols = slice(b * LANES, (b + 1) * LANES)
            dk_ref[:, cols] = pair_up(*dks)
            dv_ref[:, cols] = dvs[0] + dvs[1]

        first_tile = pos_ref[0] * n_q
        low = from_ref[first_tile]
        high = to_ref[first_tile + n_q - 1]
        n_left = jnp.maximum(own_low - low, 0)
        n_right = jnp.maximum(high - own_low - n_own, 0)

        def outside(i, carry):
            tile = jnp.where(i < n_left, low + i, own_low + n_own + i - n_left)
            at = pl.multiple_of(tile * k_tile, k_tile)
            for j in range(GROUP):
                heads = slice(j * HD, (j + 1) * HD)
                _, ds = weights_of(j, at, k_tile)
                dq[heads, :] += dot_nn(kt_ref[tile, heads, :], ds)
            return carry

        lax.fori_loop(0, n_left + n_right, outside, 0)
        turned = jnp.transpose(dq[...]) * (HD**-0.5)
        for b in range(GROUP // 2):
            cols = slice(b * LANES, (b + 1) * LANES)
            dq_ref[:, cols] = unrotated(turned[:, cols], cos_ref[...], sin_ref[...])

    def col_block(n):
        return pl.BlockSpec((n, group_cols), lambda g, *_: (0, g))

    table = pl.BlockSpec((rows, LANES), lambda g, p, *_: (p[0], 0))
    sum_shape = jax.ShapeDtypeStruct((rows, width), F32)
    return pl.pallas_call(
        body,
        grid_spec=pltpu.PrefetchScalarGridSpec(
            num_scalar_prefetch=4,
            grid=(H // GROUP,),
            in_specs=[
                whole_block((rows, width)),
                col_block(rows),
                pl.BlockSpec((1, 8, rows), lambda g, *_: (g, 0, 0)),
                pl.BlockSpec((GROUP, rows, LANES), lambda g, p, *_: (g, p[0], 0)),
                pl.BlockSpec((GROUP, seq, LANES), lambda g, *_: (g, 0, 0)),
                col_block(seq),
                pl.BlockSpec((seq // k_tile, group_cols, k_tile), lambda g, *_: (0, g, 0)),
                table,
                table,
            ]
            + held.in_specs,
            out_specs=[col_block(rows)] * 3,
            scratch_shapes=[
                pltpu.VMEM((GROUP, rows, LANES), BF16),
                pltpu.VMEM((8, rows), F32),
                pltpu.VMEM((group_cols, rows), F32),
            ]
            + held.scratch,
        ),
        out_shape=[jax.ShapeDtypeStruct((rows, width), BF16), sum_shape, sum_shape],
        compiler_params=params(20),
        name="attend_back_own",
    )(pos, offsets, key_from, key_to, d_first, attended, lse, q, k, in_hbm(v), in_hbm(kt), cosine, sine, *held.flat)


def attend_back_others(d_others, att_others, lse_others, sums, q, k, v, key_from, key_to, cosine, sine, pieces,
                       offsets, pos, q_tile, k_tile):
    rows, width = sums[0].shape
    seq = q.shape[1]
    n_q = rows // q_tile
    n_own = rows // k_tile
    n_tiles = d_others.shape[0] // q_tile
    group_cols = GROUP * HD
    held = Pieces([pieces], width, slice(3 * width, 4 * width))
    n_in = len(held.flat)

    def body(pos_ref, offs_ref, from_ref, to_ref, d_ref, att_ref, lse_ref, q_ref, k_ref, v_ref, dk_in, dv_in,
             cos_ref, sin_ref, *rest):
        w_refs, rest = rest[:n_in], rest[n_in:]
        dk_ref, dv_ref, dom, delta, dk, dv, w_scr, sems = rest
        g = pl.program_id(0)

        @pl.when(g == 0)
        def _():
            held.start(0, w_refs, offs_ref, w_scr, sems)
            held.wait(0, w_refs, offs_ref, w_scr, sems)

        dk[...] = dk_in[...]
        dv[...] = dv_in[...]
        own_low = pos_ref[0] * n_own

        for i in range(n_tiles):
            true_tile = (pos_ref[0] ^ (1 + i // n_q)) * n_q + i % n_q
            low = jnp.maximum(from_ref[true_tile], own_low)
            high = jnp.minimum(to_ref[true_tile], own_low + n_own)
            here = slice(i * q_tile, (i + 1) * q_tile)

            @pl.when(high > low)
            def _(i=i, true_tile=true_tile, low=low, high=high, here=here):
                w_rows = w_scr[0, pl.ds(pl.multiple_of(g * group_cols, group_cols), group_cols), :]
                d_att = dot_nt(d_ref[here, :], w_rows).astype(BF16)
                prepare_heads(d_att, att_ref[here, :], dom, delta, 0)
                q_at = pl.multiple_of(true_tile * q_tile, q_tile)

                def one(tile, carry):
                    at = pl.ds(pl.multiple_of((tile - own_low) * k_tile, k_tile), k_tile)
                    for b in range(GROUP // 2):
                        cols = slice(b * LANES, (b + 1) * LANES)
                        dks, dvs = [], []
                        for j in (2 * b, 2 * b + 1):
                            q_head = q_ref[j, pl.ds(q_at, q_tile), :]
                            s = dot_nt(k_ref[j, at, :], q_head)
                            p = jnp.exp(s - lse_ref[0, j : j + 1, here])
                            dp = dot_nt(v_ref[at, cols], dom[j])
                            ds = (p * (dp - delta[j : j + 1, :])).astype(BF16)
                            dvs.append(dot_nn(p.astype(BF16), dom[j]))
                            dks.append(dot_nn(ds, q_head))
                        dk[at, cols] += pair_up(*dks)
                        dv[at, cols] += dvs[0] + dvs[1]
                    return carry

                lax.fori_loop(low, high, one, 0)

        for b in range(GROUP // 2):
            cols = slice(b * LANES, (b + 1) * LANES)
            dk_ref[:, cols] = unrotated(dk[:, cols], cos_ref[...], sin_ref[...])
        dv_ref[...] = dv[...].astype(BF16)

    def col_block(n):
        return pl.BlockSpec((n, group_cols), lambda g, *_: (0, g))

    table = pl.BlockSpec((rows, LANES), lambda g, p, *_: (p[0], 0))
    return pl.pallas_call(
        body,
        grid_spec=pltpu.PrefetchScalarGridSpec(
            num_scalar_prefetch=4,
            grid=(H // GROUP,),
            in_specs=[
                whole_block(d_others.shape),
                col_block(d_others.shape[0]),
                pl.BlockSpec((1, 8, d_others.shape[0]), lambda g, *_: (g, 0, 0)),
                pl.BlockSpec((GROUP, seq, LANES), lambda g, *_: (g, 0, 0)),
                pl.BlockSpec((GROUP, rows, LANES), lambda g, p, *_: (g, p[0], 0)),
                pl.BlockSpec((rows, group_cols), lambda g, p, *_: (p[0], g)),
                col_block(rows),
                col_block(rows),
                table,
                table,
            ]
            + held.in_specs,
            out_specs=[col_block(rows)] * 2,
            scratch_shapes=[
                pltpu.VMEM((GROUP, q_tile, LANES), BF16),
                pltpu.VMEM((8, q_tile), F32),
                pltpu.VMEM((rows, group_cols), F32),
                pltpu.VMEM((rows, group_cols), F32),
            ]
            + held.scratch,
        ),
        out_shape=[jax.ShapeDtypeStruct((rows, width), BF16)] * 2,
        compiler_params=params(18),
        name="attend_back_others",
    )(pos, offsets, key_from, key_to, d_others, att_others, lse_others, q, k, in_hbm(v), *sums, cosine, sine,
      *held.flat)


def qkv_grads(x_own, merged, out_part, offsets, groups, n_blocks, block_rows):
    rows, width = x_own.shape
    wide = 3 * width + out_part.shape[1]

    def body(offs_ref, x_ref, dq_ref, dk_ref, dv_ref, out_ref, *rest):
        group_refs, g_scr = rest[:-1], rest[-1]
        x_t = jnp.transpose(x_ref[...])
        for j, ref in enumerate((dq_ref, dk_ref, dv_ref)):
            g_scr[:, j * width : (j + 1) * width] = dot_nn(x_t, ref[...])
        g_scr[:, 3 * width :] = out_ref[...].astype(F32)
        store_groups(groups, group_refs, offs_ref, n_blocks, block_rows, g_scr)

    group_shapes = [(len(picks), n_blocks, block_rows, wide) for picks, _ in groups]
    return pl.pallas_call(
        body,
        grid_spec=pltpu.PrefetchScalarGridSpec(
            num_scalar_prefetch=1,
            grid=(1,),
            in_specs=[whole_block((rows, width))] * 4 + [whole_block(out_part.shape)],
            out_specs=[whole_block(s) for s in group_shapes],
            scratch_shapes=[pltpu.VMEM((width, wide), F32)],
        ),
        out_shape=[jax.ShapeDtypeStruct(s, dtype) for s, (_, dtype) in zip(group_shapes, groups)],
        compiler_params=params(26),
        name="qkv_grads",
    )(offsets, x_own, *merged, out_part)


def input_grads(merged, d_first, pieces, offsets):
    rows, width = d_first.shape
    tile = min(256, rows)
    held = Pieces([pieces], width, slice(0, 3 * width))
    n_in = len(held.flat)

    def body(offs_ref, dq_ref, dk_ref, dv_ref, df_ref, *rest):
        w_refs, (out_ref, w_scr, sems) = rest[:n_in], rest[n_in:]

        @pl.when(pl.program_id(0) == 0)
        def _():
            held.start(0, w_refs, offs_ref, w_scr, sems)
            held.wait(0, w_refs, offs_ref, w_scr, sems)

        total = df_ref[...]
        for j, ref in enumerate((dq_ref, dk_ref, dv_ref)):
            total = total + dot_nt(ref[...], w_scr[0, :, j * width : (j + 1) * width])
        out_ref[...] = total

    block = pl.BlockSpec((tile, width), lambda i, o: (i, 0))
    return pl.pallas_call(
        body,
        grid_spec=pltpu.PrefetchScalarGridSpec(
            num_scalar_prefetch=1,
            grid=(rows // tile,),
            in_specs=[block] * 4 + held.in_specs,
            out_specs=block,
            scratch_shapes=held.scratch,
        ),
        out_shape=jax.ShapeDtypeStruct((rows, width), F32),
        compiler_params=params(12),
        name="input_grads",
    )(offsets, *merged, d_first, *held.flat)


def combine(kept, got):
    _, n_blocks, block_rows, wide = kept.shape

    def body(kept_ref, got_ref, own_ref, on_ref):
        own_ref[...] = kept_ref[0].astype(F32) + got_ref[0].astype(F32)
        on_ref[...] = (kept_ref[1].astype(F32) + got_ref[1].astype(F32)).astype(BF16)

    two = pl.BlockSpec((2, 1, block_rows, wide), lambda i: (0, i, 0, 0))
    one = pl.BlockSpec((1, block_rows, wide), lambda i: (i, 0, 0))
    shape = (n_blocks, block_rows, wide)
    return pl.pallas_call(
        body,
        grid=(n_blocks,),
        in_specs=[two, two],
        out_specs=[one, one],
        out_shape=[jax.ShapeDtypeStruct(shape, F32), jax.ShapeDtypeStruct(shape, BF16)],
        compiler_params=params(6),
        name="combine",
    )(kept, got)


def make_per_device(ndp, nt):
    plane = ndp // 2

    def move(value, chip=0, core=0, flip=0):
        pairs = []
        for d in range(ndp):
            for t in range(nt):
                to_d = ((d // 2) ^ chip) * 2 + ((d % 2) ^ core)
                pairs.append((d * nt + t, to_d * nt + (t ^ flip)))
        return lax.ppermute(value, AXES, pairs)

    def after(value, *others):
        return lax.optimization_barrier((value, *others))[0]

    def per_device(inputs, segment_ids, qkv_weight, out_weight, norm_gains, norm_biases,
                   gate_weight, up_weight, down_weight, out_grad):
        rows, width = inputs.shape
        seq = segment_ids.shape[1]
        n_row = seq // rows
        q_tile = min(256, rows)
        k_tile = min(256, rows)
        shard = qkv_weight.shape[0]
        ffn_rows, ffn_cols = gate_weight.shape
        half = ffn_cols // 2
        fast = plane == 4 and nt == 4 and n_row == 2

        d_index = lax.axis_index("dp")
        core = d_index % 2
        chip = d_index // 2
        t_index = lax.axis_index("tensor")
        pos = (t_index % n_row).astype(jnp.int32)
        block_at = [((chip ^ dxy) * 2 + (core ^ other)) for dxy in range(4) for other in range(2)]

        packed = jnp.concatenate(
            [qkv_weight, out_weight, norm_gains.T, norm_biases.T,
             jnp.zeros((shard, PAD - 4), BF16)], axis=1)
        seg = lax.dynamic_index_in_dim(segment_ids, t_index // n_row, 0, keepdims=False)
        doc_from = jnp.sum((seg[None, :] < seg[:, None]).astype(jnp.int32), axis=1)
        doc_to = jnp.sum((seg[None, :] <= seg[:, None]).astype(jnp.int32), axis=1)
        place = (jnp.arange(seq, dtype=jnp.int32) - doc_from).astype(F32)
        lane = np.arange(LANES)
        frequency = rope_base ** (-jnp.asarray(lane % (HD // 2), F32) * 2.0 / HD)
        angles = place[:, None] * frequency[None, :]
        cosine = jnp.cos(angles)
        sine = jnp.sin(angles) * jnp.asarray(np.where(lane % HD < HD // 2, -1.0, 1.0), F32)[None, :]
        key_from = doc_from[::q_tile] // k_tile
        key_to = (doc_to[q_tile - 1 :: q_tile] + k_tile - 1) // k_tile
        seg_col = seg[:, None]
        seg_row = seg.reshape(seq // q_tile, 1, q_tile)
        pos_arr = pos[None]

        ffn = (gate_weight, up_weight, down_weight.T)
        mine, given = [
            jnp.concatenate([lax.dynamic_slice_in_dim(w, c * half, half, 1) for w in ffn], axis=1)
            for c in (core, 1 - core)
        ]
        if fast:
            pair = jnp.stack([mine, move(given, core=1)])
            slots = [[pair, move(pair, chip=1), move(pair, chip=2)]]
            x_others = [move(inputs, flip=1)]
            slots += [[move(pair, flip=s)] for s in (1, 2, 3)]

            def spread(s, *others):
                one = after(slots[s][0], *others)
                slots[s] += [move(one, chip=1), move(one, chip=2)]

            def spread_on(s, *others):
                side, chip_step = (1, 2) if s % 2 == 0 else (2, 1)
                slots[s].append(move(after(slots[s][side], *others), chip=chip_step))

            by_flip = [packed] + [move(packed, flip=e) for e in range(1, nt)]
            near = jnp.concatenate(
                [lax.select_n(t_index, *[by_flip[j ^ t] for t in range(nt)]) for j in range(nt)], axis=0)[None]
            far = [move(near, chip=dxy) for dxy in range(1, 4)]
            near_sib = move(near, core=1)
            far_sib = move(
                after(jnp.concatenate(far, axis=0), slots[1][0], *x_others, cosine, sine, key_from, key_to,
                      seg_col),
                core=1)
            spread_on(0, *far)
            spread(1, *far)
            x_rel = after(jnp.concatenate([inputs] + x_others, axis=0), *slots[1][1:])
            w_pieces = [near, *far, near_sib, far_sib]
            w_offsets = jnp.stack(
                [((chip ^ dxy) * 2 + (core ^ other)) * (nt * shard) for other in range(2) for dxy in range(4)]
            ).astype(jnp.int32)
            f_offsets = jnp.stack([b * ffn_rows for b in block_at]).astype(jnp.int32)
            n_blocks, block_rows = 2, ffn_rows
        else:
            x_others = [move(inputs, flip=e) for e in range(1, n_row)]
            x_rel = jnp.concatenate([inputs] + x_others, axis=0)
            w_pieces = [lax.all_gather(packed, AXES, axis=0, tiled=True)[None]]
            w_offsets = jnp.zeros((1,), jnp.int32)
            full = lax.all_gather(mine, "dp", axis=0, tiled=True).reshape(width, 3, half)
            full = lax.all_gather(full, "tensor", axis=2, tiled=True)
            slots = [[full.reshape(1, width, 3 * half * nt)]]
            f_offsets = jnp.zeros((1,), jnp.int32)
            n_blocks, block_rows = 1, width

        q, k, v, kt, vt, norms = project(
            x_rel, w_pieces, w_offsets, cosine, sine, seg_col, pos_arr, n_row, k_tile)
        if fast:
            spread_on(1, q)
        attended, lse, normed1, inv_std1, mid = attend(
            inputs, q, k, vt, w_pieces, w_offsets, norms, pos_arr)
        if fast:
            spread(2, mid)
            spread(3, mid)
            spread_on(2, mid)
            spread_on(3, mid)
        mid_sib = move(mid, core=1)

        calls = [slots[:2], slots[2:]] if fast else [slots]
        acts, partial = [], None
        for j, some in enumerate(calls):
            hid, fac_a, fac_b, *partial = feed_forward(
                mid, mid_sib, some, f_offsets, partial[0] if j else None, j == len(calls) - 1)
            acts.append((hid, fac_a, fac_b))
        part_own, part_sib = partial
        att_others = [move(attended, flip=e) for e in range(1, n_row)]
        lse_others = [move(lse, flip=e) for e in range(1, n_row)]
        part_sib = move(after(part_sib, *att_others, *lse_others), core=1)
        outputs, d_second, d_ffn, norm2 = second_norm(normed1, part_own, part_sib, out_grad, norms)
        d_ffn_sib = move(d_ffn, core=1)
        d_both, d_mid, d_mid_give = hidden_back(
            (d_ffn, d_ffn_sib), [a[1:] for a in acts], slots, f_offsets)
        d_mid_sib = move(d_mid_give, core=1)

        def groups_of(s):
            if not fast:
                return [((0,), BF16)]
            if s % 2 == 0:
                return [((2, 3), BF16), ((0, 1), BF16)]
            return [((1, 3), BF16), ((0, 2), BF16)]

        def weight_grads(j, d_both):
            first = sum(len(c) for c in calls[:j])
            return ffn_grads(
                first, (mid, mid_sib), (d_ffn, d_ffn_sib), acts[j][0], d_both, f_offsets,
                [groups_of(first + i) for i in range(len(calls[j]))], n_blocks, block_rows)

        d_first, d_first_low, norm1 = first_norm_back(
            normed1, inv_std1, d_second, d_mid, d_mid_sib, norms)
        d_others = [move(d_first_low, flip=e) for e in range(1, n_row)]
        d_both = after(d_both, d_first_low)
        reduced = [r for j in range(len(calls)) for r in weight_grads(j, d_both)]

        def turn(s):
            return (2, 1) if s % 2 == 0 else (1, 2)

        arrived, owned = {}, {}
        if fast:
            arrived = {s: move(reduced[s][0], chip=turn(s)[0]) for s in range(nt)}

        def combine_on(s):
            own, on = combine(reduced[s][1], arrived[s])
            owned[s] = (own, move(on, chip=turn(s)[1]))

        def owned_sum(s, *others):
            own, on = owned[s]
            mine = own + after(on, *others).astype(F32)
            return mine.astype(BF16) if s else mine

        dq, *sums = attend_back_own(
            after(d_first_low, *[r[-1] for r in reduced]), attended, lse, q, k, v, kt, key_from, key_to,
            cosine, sine, w_pieces, w_offsets, pos_arr, k_tile)
        if fast:
            arrived[0], arrived[1] = after(arrived[0], dq), after(arrived[1], dq)
            combine_on(0)
            combine_on(1)
            sums[0] = after(sums[0], owned[0][0], owned[1][0])
        dk, dv = attend_back_others(
            jnp.concatenate(d_others, axis=0), jnp.concatenate(att_others, axis=0),
            jnp.concatenate(lse_others, axis=2), sums, q, k, v, key_from, key_to, cosine, sine,
            w_pieces, w_offsets, pos_arr, q_tile, k_tile)
        out_part = out_grads(attended, d_first_low, norm1, norm2)
        if fast:
            sent = {s: owned_sum(s, dk) for s in (0, 1)}
            arrived[2], arrived[3] = after(arrived[2], dk), after(arrived[3], dk)
            combine_on(2)
            combine_on(3)
            back = [move(sent[1], flip=1)]
            dv = after(dv, owned[2][0], owned[3][0], sent[0], sent[1])
        merged = (dq, dk, dv)

        if fast:
            q_groups = [((1, 3, 5, 7), BF16), ((0, 2, 4, 6), BF16)]
            q_offsets = jnp.stack([b * (nt * shard) for b in block_at]).astype(jnp.int32)
            q_rows = nt * shard
        else:
            q_groups = [((0,), F32)]
            q_offsets = jnp.zeros((1,), jnp.int32)
            q_rows = width
        q_parts = qkv_grads(inputs, merged, out_part, q_offsets, q_groups, 1, q_rows)
        if fast:
            sent.update({s: owned_sum(s, q_parts[0]) for s in (2, 3)})
            back += [move(sent[s], flip=s) for s in (2, 3)]
            d_first = after(d_first, sent[2], sent[3])
        inputs_grad = input_grads(merged, d_first, w_pieces, w_offsets)

        if fast:
            q_other = after(move(q_parts[0], core=1), inputs_grad)
            q_sum = q_parts[1][:, 0].astype(F32) + q_other[:, 0].astype(F32)
            q_own = q_sum[0]
            for dxy in range(1, 4):
                q_own = q_own + move(q_sum[dxy].astype(BF16), chip=dxy).astype(F32)
            back = lax.optimization_barrier((*back, q_own))[:-1]
            total = sent[0] + sum(b.astype(F32) for b in back)
            packed_grad = None
            for e in range(nt):
                piece = lax.dynamic_slice_in_dim(q_own, (t_index ^ e) * shard, shard, 0)
                if e:
                    piece = move(piece.astype(BF16), flip=e).astype(F32)
                packed_grad = piece if packed_grad is None else packed_grad + piece
            other = move(total[1], core=1)
            mine = total[0]
            grads = []
            for m in range(3):
                part = slice(m * half, (m + 1) * half)
                grads.append(jnp.where(
                    core == 0,
                    jnp.concatenate([mine[:, part], other[:, part]], axis=1),
                    jnp.concatenate([other[:, part], mine[:, part]], axis=1)))
        else:
            summed = lax.psum_scatter(
                reduced[0][0][0, 0].reshape(width, 3, half * nt), "tensor", scatter_dimension=2, tiled=True)
            spread = jnp.zeros((width, 3, 2 * half), BF16)
            spread = lax.dynamic_update_slice_in_dim(spread, summed.astype(BF16), core * half, 2)
            spread = lax.psum_scatter(spread, "dp", scatter_dimension=0, tiled=True).astype(F32)
            grads = [spread[:, m] for m in range(3)]
            packed_grad = lax.psum_scatter(q_parts[0][0, 0], AXES, scatter_dimension=0, tiled=True)

        return (
            outputs,
            inputs_grad,
            packed_grad[:, : 3 * width],
            packed_grad[:, 3 * width : 4 * width],
            packed_grad[:, 4 * width : 4 * width + 2].T,
            packed_grad[:, 4 * width + 2 : 4 * width + 4].T,
            grads[0],
            grads[1],
            grads[2].T,
        )

    return per_device


def solution(mesh):
    tokens = P(AXES, None)
    both = P("dp", "tensor")
    return jax.shard_map(
        make_per_device(mesh.shape["dp"], mesh.shape["tensor"]),
        mesh=mesh,
        in_specs=(tokens, P("dp", None), tokens, tokens, P(None, AXES), P(None, AXES),
                  both, both, P("tensor", "dp"), tokens),
        out_specs=(tokens, tokens, tokens, tokens, P(None, AXES), P(None, AXES),
                   both, both, P("tensor", "dp")),
        check_vma=False,
    )
```

```python
import jax
import jax.numpy as jnp
import numpy as np
from jax import lax
from jax.experimental import pallas as pl
from jax.experimental.pallas import tpu as pltpu
from jax.sharding import PartitionSpec as P

H = 12
HD = 64
LANES = 128
PAD = 128
NEG = -1e30

rope_base = 1000.0
layer_eps = 1e-12

AXES = ("dp", "tensor")
F32 = jnp.float32
BF16 = jnp.bfloat16


def params(mebibytes):
    return pltpu.CompilerParams(
        dimension_semantics=("arbitrary",), vmem_limit_bytes=mebibytes * 2**20
    )


def whole_block(shape):
    zeros = (0,) * len(shape)
    return pl.BlockSpec(shape, lambda *_: zeros, pipeline_mode=pl.Buffered(1))


def dot_nn(a, b):
    return lax.dot_general(a, b, (((1,), (0,)), ((), ())), preferred_element_type=F32)


def dot_nt(a, b):
    return lax.dot_general(a, b, (((1,), (1,)), ((), ())), preferred_element_type=F32)


def dot_tn(a, b):
    return lax.dot_general(a, b, (((0,), (0,)), ((), ())), preferred_element_type=F32)


def half_swap(block):
    lane = lax.broadcasted_iota(jnp.int32, block.shape, 1)
    return jnp.where(
        lane % HD < HD // 2, pltpu.roll(block, LANES - HD // 2, 1), pltpu.roll(block, HD // 2, 1)
    )


def normalise(summed):
    mean = jnp.mean(summed, axis=-1, keepdims=True)
    centred = summed - mean
    inv_std = lax.rsqrt(jnp.mean(centred * centred, axis=-1, keepdims=True) + layer_eps)
    return centred * inv_std, inv_std


def norm_back(normed, inv_std, gain, grad):
    scaled = grad * gain
    return inv_std * (
        scaled
        - jnp.mean(scaled, axis=-1, keepdims=True)
        - normed * jnp.mean(scaled * normed, axis=-1, keepdims=True)
    )


def in_hbm(x):
    return pltpu.with_memory_space_constraint(x, pltpu.HBM)


class Pieces:
    def __init__(self, slots, width, cols=None):
        arrays = []
        self.where = []
        for slot in slots:
            for array, index in slot:
                known = [i for i, other in enumerate(arrays) if other is array]
                if not known:
                    arrays.append(array)
                self.where.append((known[0] if known else len(arrays) - 1, index))
        self.flat = [in_hbm(x) for x in arrays]
        self.n_slots = len(slots)
        self.n_pieces = len(slots[0])
        self.blocks = [(p, b) for p, (x, _) in enumerate(slots[0]) for b in range(x.shape[1])]
        _, _, self.block_rows, wide = slots[0][0][0].shape
        self.cols = cols or slice(0, wide)
        self.in_specs = [pl.BlockSpec(memory_space=pl.ANY)] * len(self.flat)
        self.scratch = [
            pltpu.VMEM((self.n_slots, width, self.cols.stop - self.cols.start), BF16),
            pltpu.SemaphoreType.DMA((self.n_slots, len(self.blocks))),
        ]

    def copies(self, slot, refs, offs_ref, scr, sems):
        for j, (p, b) in enumerate(self.blocks):
            start = pl.multiple_of(offs_ref[j], 16)
            array, index = self.where[slot * self.n_pieces + p]
            yield pltpu.make_async_copy(
                refs[array].at[index, b, :, self.cols],
                scr.at[slot, pl.ds(start, self.block_rows), :],
                sems.at[slot, j],
            )

    def start(self, slot, *args):
        for copy in self.copies(slot, *args):
            copy.start()

    def wait(self, slot, *args):
        for copy in self.copies(slot, *args):
            copy.wait()

    def start_all(self, *args):
        for s in range(self.n_slots):
            self.start(s, *args)

    def wait_for_step(self, step, *args):
        for s in range(self.n_slots):

            @pl.when(step == s)
            def _(s=s):
                self.wait(s, *args)


def head_lanes(block, h, extra):
    lane = lax.broadcasted_iota(jnp.int32, block.shape, 1)
    mine = lane < HD if h % 2 == 0 else lane >= HD
    return jnp.where(mine, block, extra)


def project(x_rel, pieces, offsets, cosine, sine, seg_col, pos, n_row, k_tile):
    seq, width = x_rel.shape
    rows = seq // n_row
    tile = min(256, rows)
    per_piece = rows // tile
    held = Pieces([pieces], width)
    n_in = len(held.flat)

    def true_tile(i, pos_ref):
        return (pos_ref[0] ^ (i // per_piece)) * per_piece + i % per_piece

    def body(pos_ref, offs_ref, x_ref, cos_ref, sin_ref, seg_ref, *rest):
        w_refs, rest = rest[:n_in], rest[n_in:]
        q_ref, k_ref, v_ref, kt_ref, vt_ref, norm_ref, w_scr, sems = rest

        @pl.when(pl.program_id(0) == 0)
        def _():
            held.start(0, w_refs, offs_ref, w_scr, sems)
            held.wait(0, w_refs, offs_ref, w_scr, sems)
            norm_ref[...] = jnp.transpose(w_scr[0, :, 4 * width :].astype(F32))[:8, :]

        x = x_ref[...]
        cos = cos_ref[...]
        sin = sin_ref[...]
        lane = lax.broadcasted_iota(jnp.int32, (tile, LANES), 1)
        same = lane % HD == seg_ref[...]
        key_extra = jnp.where(same, 1.0, 0.0)
        query_extra = jnp.where(same, 0.0, NEG)
        merged = dot_nn(x, w_scr[0, :, : 3 * width])
        for b in range(width // LANES):
            cols = slice(b * LANES, (b + 1) * LANES)
            q = merged[:, b * LANES : (b + 1) * LANES]
            k = merged[:, width + b * LANES : width + (b + 1) * LANES]
            v = merged[:, 2 * width + b * LANES : 2 * width + (b + 1) * LANES]
            q = (q * cos + half_swap(q) * sin) * (HD**-0.5)
            k = k * cos + half_swap(k) * sin
            for h in (2 * b, 2 * b + 1):
                q_ref[h] = head_lanes(q, h, query_extra).astype(BF16)
                k_ref[h] = head_lanes(k, h, key_extra).astype(BF16)
            v_ref[:, cols] = v.astype(BF16)
            vt_ref[cols, :] = jnp.transpose(v).astype(BF16)
            for j in range(tile // k_tile):
                kt_ref[j, cols, :] = jnp.transpose(k[j * k_tile : (j + 1) * k_tile, :]).astype(BF16)

    row_block = pl.BlockSpec((tile, width), lambda i, p, o: (true_tile(i, p), 0))
    head_block = pl.BlockSpec((H, tile, LANES), lambda i, p, o: (0, true_tile(i, p), 0))
    table_block = pl.BlockSpec((tile, LANES), lambda i, p, o: (true_tile(i, p), 0))
    return pl.pallas_call(
        body,
        grid_spec=pltpu.PrefetchScalarGridSpec(
            num_scalar_prefetch=2,
            grid=(seq // tile,),
            in_specs=[
                pl.BlockSpec((tile, width), lambda i, p, o: (i, 0)),
                table_block,
                table_block,
                pl.BlockSpec((tile, 1), lambda i, p, o: (true_tile(i, p), 0)),
            ]
            + held.in_specs,
            out_specs=[
                head_block,
                head_block,
                row_block,
                pl.BlockSpec((tile // k_tile, width, k_tile), lambda i, p, o: (true_tile(i, p), 0, 0)),
                pl.BlockSpec((width, tile), lambda i, p, o: (0, true_tile(i, p))),
                whole_block((8, width)),
            ],
            scratch_shapes=held.scratch,
        ),
        out_shape=[jax.ShapeDtypeStruct((H, seq, LANES), BF16)] * 2
        + [
            jax.ShapeDtypeStruct((seq, width), BF16),
            jax.ShapeDtypeStruct((seq // k_tile, width, k_tile), BF16),
            jax.ShapeDtypeStruct((width, seq), BF16),
            jax.ShapeDtypeStruct((8, width), F32),
        ],
        compiler_params=params(20),
        name="project",
    )(pos, offsets, x_rel, cosine, sine, seg_col, *held.flat)


GROUP = 4


def attend(x_own, q, k, vt, pieces, offsets, norms, pos):
    rows, width = x_own.shape
    seq = q.shape[1]
    group_cols = GROUP * HD
    n_steps = H // GROUP
    held = Pieces([pieces], width, slice(3 * width, 4 * width))
    n_in = len(held.flat)

    def body(pos_ref, offs_ref, x_ref, q_ref, k_ref, vt_ref, norm_ref, *rest):
        w_refs, rest = rest[:n_in], rest[n_in:]
        att_ref, lse_ref, n_ref, istd_ref, mid_ref, acc, lse, w_scr, sems = rest
        g = pl.program_id(0)

        @pl.when(g == 0)
        def _():
            held.start(0, w_refs, offs_ref, w_scr, sems)

        for j in range(GROUP):
            s = dot_nt(k_ref[j], q_ref[j])
            peak = jnp.max(s, axis=0, keepdims=True)
            e = jnp.exp(s - peak)
            total = jnp.sum(e, axis=0, keepdims=True)
            out = dot_nn(vt_ref[j * HD : (j + 1) * HD, :], e.astype(BF16))
            acc[g, j * HD : (j + 1) * HD, :] = out / total
            lse[g, j : j + 1, :] = peak + jnp.log(total)

        @pl.when(g == n_steps - 1)
        def _():
            held.wait(0, w_refs, offs_ref, w_scr, sems)
            for i in range(n_steps):
                lse_ref[i] = lse[i]
                att_ref[:, i * group_cols : (i + 1) * group_cols] = jnp.transpose(acc[i]).astype(BF16)
            first_sum = x_ref[...].astype(F32) + dot_nn(att_ref[...], w_scr[0])
            normed, inv_std = normalise(first_sum)
            n_ref[...] = normed
            istd_ref[...] = inv_std
            mid_ref[...] = (normed * norm_ref[0:1, :] + norm_ref[2:3, :]).astype(BF16)

    own = whole_block((rows, width))
    return pl.pallas_call(
        body,
        grid_spec=pltpu.PrefetchScalarGridSpec(
            num_scalar_prefetch=2,
            grid=(n_steps,),
            in_specs=[
                own,
                pl.BlockSpec((GROUP, rows, LANES), lambda g, p, o: (g, p[0], 0)),
                pl.BlockSpec((GROUP, seq, LANES), lambda g, p, o: (g, 0, 0)),
                pl.BlockSpec((group_cols, seq), lambda g, p, o: (g, 0)),
                whole_block((8, width)),
            ]
            + held.in_specs,
            out_specs=[own, whole_block((n_steps, 8, rows)), own, whole_block((rows, 1)), own],
            scratch_shapes=[
                pltpu.VMEM((n_steps, group_cols, rows), F32),
                pltpu.VMEM((n_steps, 8, rows), F32),
            ]
            + held.scratch,
        ),
        out_shape=[
            jax.ShapeDtypeStruct((rows, width), BF16),
            jax.ShapeDtypeStruct((n_steps, 8, rows), F32),
            jax.ShapeDtypeStruct((rows, width), F32),
            jax.ShapeDtypeStruct((rows, 1), F32),
            jax.ShapeDtypeStruct((rows, width), BF16),
        ],
        compiler_params=params(18),
        name="attend",
    )(pos, offsets, x_own, q, k, vt, norms, *held.flat)


def feed_forward(mid_own, mid_sib, slots, offsets, before, last):
    rows, width = mid_own.shape
    held = Pieces(slots, width)
    n_slots, cols = held.n_slots, held.cols.stop // 3
    n_in = len(held.flat)

    def body(offs_ref, own_ref, sib_ref, *rest):
        w_refs, rest = rest[:n_in], rest[n_in:]
        if before is not None:
            before_ref, rest = rest[0], rest[1:]
        if last:
            hid_ref, a_ref, b_ref, out_own, out_sib, acc, w_scr, sems = rest
        else:
            hid_ref, a_ref, b_ref, acc, w_scr, sems = rest
        s = pl.program_id(0)

        @pl.when(s == 0)
        def _():
            held.start_all(w_refs, offs_ref, w_scr, sems)
            acc[...] = jnp.zeros(acc.shape, F32) if before is None else before_ref[...]

        held.wait_for_step(s, w_refs, offs_ref, w_scr, sems)
        for i, x_ref in enumerate((own_ref, sib_ref)):
            part = slice(i * rows, (i + 1) * rows)
            both = dot_nn(x_ref[...], w_scr[s, :, : 2 * cols])
            gate, up = both[:, :cols], both[:, cols:]
            sig = 0.5 * jnp.tanh(0.5 * gate) + 0.5
            silu = gate * sig
            hidden = (silu * up).astype(BF16)
            hid_ref[0, part, :] = hidden
            a_ref[0, part, :] = (up * (sig + silu * (1.0 - sig))).astype(BF16)
            b_ref[0, part, :] = silu.astype(BF16)
            acc[part, :] += dot_nt(hidden, w_scr[s, :, 2 * cols :])

        if last:

            @pl.when(s == n_slots - 1)
            def _():
                out_own[...] = acc[:rows, :]
                out_sib[...] = acc[rows:, :].astype(BF16)

    full = whole_block((rows, width))
    both_block = whole_block((2 * rows, width))
    act = pl.BlockSpec((1, 2 * rows, cols), lambda i, *_: (i, 0, 0))
    act_shape = jax.ShapeDtypeStruct((n_slots, 2 * rows, cols), BF16)
    extra = [] if before is None else [before]
    if last:
        acc_specs = [full, full]
        acc_shapes = [jax.ShapeDtypeStruct((rows, width), F32), jax.ShapeDtypeStruct((rows, width), BF16)]
        acc_scratch = [pltpu.VMEM((2 * rows, width), F32)]
    else:
        acc_specs = [both_block]
        acc_shapes = [jax.ShapeDtypeStruct((2 * rows, width), F32)]
        acc_scratch = []
    return pl.pallas_call(
        body,
        grid_spec=pltpu.PrefetchScalarGridSpec(
            num_scalar_prefetch=1,
            grid=(n_slots,),
            in_specs=[full, full] + held.in_specs + [both_block] * len(extra),
            out_specs=[act] * 3 + acc_specs,
            scratch_shapes=acc_scratch + held.scratch,
        ),
        out_shape=[act_shape] * 3 + acc_shapes,
        compiler_params=params(18),
        name="feed_forward",
    )(offsets, mid_own, mid_sib, *held.flat, *extra)


def second_norm(normed1, part_own, part_sib, out_grad, norms):
    rows, width = normed1.shape
    tile = min(256, rows)

    def body(n_ref, own_ref, sib_ref, g_ref, norm_ref, out_ref, d_ref, dl_ref, ng_ref):
        middle = n_ref[...] * norm_ref[0:1, :] + norm_ref[2:3, :]
        second_sum = middle + (own_ref[...] + sib_ref[...].astype(F32))
        normed, inv_std = normalise(second_sum)
        out_ref[...] = (normed * norm_ref[1:2, :] + norm_ref[3:4, :]).astype(BF16)
        grad = g_ref[...].astype(F32)
        d = norm_back(normed, inv_std, norm_ref[1:2, :], grad)
        d_ref[...] = d
        dl_ref[...] = d.astype(BF16)

        @pl.when(pl.program_id(0) == 0)
        def _():
            ng_ref[...] = jnp.zeros(ng_ref.shape, F32)

        ng_ref[0:1, :] += jnp.sum(grad * normed, axis=0, keepdims=True)
        ng_ref[1:2, :] += jnp.sum(grad, axis=0, keepdims=True)

    block = pl.BlockSpec((tile, width), lambda i: (i, 0))
    return pl.pallas_call(
        body,
        grid=(rows // tile,),
        in_specs=[block] * 4 + [whole_block((8, width))],
        out_specs=[block] * 3 + [whole_block((8, width))],
        out_shape=[
            jax.ShapeDtypeStruct((rows, width), BF16),
            jax.ShapeDtypeStruct((rows, width), F32),
            jax.ShapeDtypeStruct((rows, width), BF16),
            jax.ShapeDtypeStruct((8, width), F32),
        ],
        compiler_params=params(10),
        name="second_norm",
    )(normed1, part_own, part_sib, out_grad, norms)


def hidden_back(dffs, factors, slots, offsets):
    rows, width = dffs[0].shape
    held = Pieces(slots, width)
    n_slots, cols = held.n_slots, held.cols.stop // 3
    n_in = len(held.flat)
    per_call = factors[0][0].shape[0]
    n_fac = len(factors)

    def body(offs_ref, do_ref, ds_ref, *rest):
        fac_refs, rest = rest[: 2 * n_fac], rest[2 * n_fac :]
        w_refs, rest = rest[:n_in], rest[n_in:]
        d_ref, out_own, out_sib, acc, w_scr, sems = rest
        s = pl.program_id(0)

        @pl.when(s == 0)
        def _():
            held.start_all(w_refs, offs_ref, w_scr, sems)
            acc[...] = jnp.zeros(acc.shape, F32)

        held.wait_for_step(s, w_refs, offs_ref, w_scr, sems)

        def work(a_ref, b_ref):
            for i, x_ref in enumerate((do_ref, ds_ref)):
                part = slice(i * rows, (i + 1) * rows)
                dh = dot_nn(x_ref[...], w_scr[s, :, 2 * cols :])
                d_ref[0, part, :cols] = (dh * a_ref[0, part, :].astype(F32)).astype(BF16)
                d_ref[0, part, cols:] = (dh * b_ref[0, part, :].astype(F32)).astype(BF16)
                acc[part, :] += dot_nt(d_ref[0, part, :], w_scr[s, :, : 2 * cols])

        for f in range(n_fac):

            @pl.when(s // per_call == f)
            def _(f=f):
                work(fac_refs[2 * f], fac_refs[2 * f + 1])

        @pl.when(s == n_slots - 1)
        def _():
            out_own[...] = acc[:rows, :]
            out_sib[...] = acc[rows:, :].astype(BF16)

    full = whole_block((rows, width))

    def fac_spec(f):
        return pl.BlockSpec(
            (1, 2 * rows, cols), lambda i, *_: (jnp.clip(i - f * per_call, 0, per_call - 1), 0, 0)
        )

    return pl.pallas_call(
        body,
        grid_spec=pltpu.PrefetchScalarGridSpec(
            num_scalar_prefetch=1,
            grid=(n_slots,),
            in_specs=[full, full]
            + [fac_spec(f) for f in range(n_fac) for _ in range(2)]
            + held.in_specs,
            out_specs=[pl.BlockSpec((1, 2 * rows, 2 * cols), lambda i, *_: (i, 0, 0)), full, full],
            scratch_shapes=[pltpu.VMEM((2 * rows, width), F32)] + held.scratch,
        ),
        out_shape=[
            jax.ShapeDtypeStruct((n_slots, 2 * rows, 2 * cols), BF16),
            jax.ShapeDtypeStruct((rows, width), F32),
            jax.ShapeDtypeStruct((rows, width), BF16),
        ],
        compiler_params=params(22),
        name="hidden_back",
    )(offsets, *dffs, *[x for pair in factors for x in pair], *held.flat)


def store_groups(groups, group_refs, offs_ref, n_blocks, block_rows, source):
    for (picks, dtype), ref in zip(groups, group_refs):
        for j, p in enumerate(picks):
            for b in range(n_blocks):
                start = pl.multiple_of(offs_ref[p * n_blocks + b], 8)
                ref[j, b] = source[pl.ds(start, block_rows), :].astype(dtype)


def ffn_grads(first, mids, dffs, hidden, d_both, offsets, groups, n_blocks, block_rows):
    rows, width = mids[0].shape
    n_slots, _, cols = hidden.shape
    shapes = [[(len(picks), n_blocks, block_rows, 3 * cols) for picks, _ in gs] for gs in groups]
    n_out = [len(gs) for gs in groups]

    def body(offs_ref, mo, ms, do, ds, hid_ref, d_ref, *rest):
        outs, rest = rest[: sum(n_out)], rest[sum(n_out) :]
        stages, (mid_t, dff_t, g_scr, sems) = rest[: sum(n_out)], rest[sum(n_out) :]
        s = pl.program_id(0)

        @pl.when(s == 0)
        def _():
            for i, (m_ref, x_ref) in enumerate(((mo, do), (ms, ds))):
                part = slice(i * rows, (i + 1) * rows)
                mid_t[:, part] = jnp.transpose(m_ref[...])
                dff_t[:, part] = jnp.transpose(x_ref[...])

        g_scr[:, : 2 * cols] = dot_nn(mid_t[...], d_ref[0])
        g_scr[:, 2 * cols :] = dot_nn(dff_t[...], hid_ref[0])
        for j in range(n_slots):
            at = sum(n_out[:j])

            @pl.when(s == j)
            def _(j=j, at=at):
                store_groups(groups[j], stages[at : at + n_out[j]], offs_ref, n_blocks, block_rows, g_scr)
                for o in range(at, at + n_out[j]):
                    pltpu.make_async_copy(stages[o], outs[o], sems.at[o]).start()

        @pl.when(s == n_slots - 1)
        def _():
            for o in range(sum(n_out)):
                pltpu.make_async_copy(stages[o], outs[o], sems.at[o]).wait()

    flat = [(shape, dtype) for ss, gs in zip(shapes, groups) for shape, (_, dtype) in zip(ss, gs)]
    full = whole_block((rows, width))
    results = pl.pallas_call(
        body,
        grid_spec=pltpu.PrefetchScalarGridSpec(
            num_scalar_prefetch=1,
            grid=(n_slots,),
            in_specs=[full] * 4
            + [
                pl.BlockSpec((1, 2 * rows, cols), lambda i, *_: (i, 0, 0)),
                pl.BlockSpec((1, 2 * rows, 2 * cols), lambda i, *_: (first + i, 0, 0)),
            ],
            out_specs=[pl.BlockSpec(memory_space=pl.ANY)] * len(flat),
            scratch_shapes=[pltpu.VMEM(shape, dtype) for shape, dtype in flat]
            + [
                pltpu.VMEM((width, 2 * rows), BF16),
                pltpu.VMEM((width, 2 * rows), BF16),
                pltpu.VMEM((width, 3 * cols), F32),
                pltpu.SemaphoreType.DMA((len(flat),)),
            ],
        ),
        out_shape=[jax.ShapeDtypeStruct(shape, dtype) for shape, dtype in flat],
        compiler_params=params(22),
        name="ffn_grads",
    )(offsets, *mids, *dffs, hidden, d_both)
    return [results[sum(n_out[:j]) : sum(n_out[: j + 1])] for j in range(n_slots)]


def first_norm_back(normed1, inv_std1, d_second, d_mid, d_mid_sib, norms):
    rows, width = normed1.shape
    tile = min(256, rows)

    def body(n_ref, istd_ref, d2_ref, dm_ref, ds_ref, norm_ref, d_ref, dl_ref, ng_ref):
        grad = d2_ref[...] + dm_ref[...] + ds_ref[...].astype(F32)
        normed = n_ref[...]
        d = norm_back(normed, istd_ref[...], norm_ref[0:1, :], grad)
        d_ref[...] = d
        dl_ref[...] = d.astype(BF16)

        @pl.when(pl.program_id(0) == 0)
        def _():
            ng_ref[...] = jnp.zeros(ng_ref.shape, F32)

        ng_ref[0:1, :] += jnp.sum(grad * normed, axis=0, keepdims=True)
        ng_ref[1:2, :] += jnp.sum(grad, axis=0, keepdims=True)

    block = pl.BlockSpec((tile, width), lambda i: (i, 0))
    column = pl.BlockSpec((tile, 1), lambda i: (i, 0))
    return pl.pallas_call(
        body,
        grid=(rows // tile,),
        in_specs=[block, column, block, block, block, whole_block((8, width))],
        out_specs=[block] * 2 + [whole_block((8, width))],
        out_shape=[
            jax.ShapeDtypeStruct((rows, width), F32),
            jax.ShapeDtypeStruct((rows, width), BF16),
            jax.ShapeDtypeStruct((8, width), F32),
        ],
        compiler_params=params(8),
        name="first_norm_back",
    )(normed1, inv_std1, d_second, d_mid, d_mid_sib, norms)


def out_grads(attended, d_first_low, norm1, norm2):
    rows, width = attended.shape

    def body(att_ref, dl_ref, n1_ref, n2_ref, out_ref):
        out_ref[:, :width] = dot_tn(att_ref[...], dl_ref[...]).astype(BF16)
        stacked = jnp.concatenate(
            [n1_ref[0:1, :], n2_ref[0:1, :], n1_ref[1:2, :], n2_ref[1:2, :],
             jnp.zeros((PAD - 4, width), F32)], axis=0)
        out_ref[:, width:] = jnp.transpose(stacked).astype(BF16)

    operands = (attended, d_first_low, norm1, norm2)
    return pl.pallas_call(
        body,
        grid=(1,),
        in_specs=[whole_block(o.shape) for o in operands],
        out_specs=whole_block((width, width + PAD)),
        out_shape=jax.ShapeDtypeStruct((width, width + PAD), BF16),
        compiler_params=params(10),
        name="out_grads",
    )(*operands)


def unrotated(g, cos, sin):
    g = g.astype(BF16).astype(F32)
    return (g * cos - half_swap(g) * sin).astype(BF16)


def prepare_heads(d_att, att, dom, delta, at):
    n = d_att.shape[0]
    flipped = jnp.transpose(d_att.astype(F32) * att.astype(F32))
    for j in range(GROUP):
        delta[j : j + 1, at : at + n] = jnp.sum(flipped[j * HD : (j + 1) * HD, :], axis=0, keepdims=True)
        block = d_att[:, j // 2 * LANES : j // 2 * LANES + LANES].astype(F32)
        dom[j, at : at + n, :] = head_lanes(block, j, 0.0).astype(BF16)


def pair_up(even, odd):
    return head_lanes(even, 0, odd)


def attend_back_own(d_first, attended, lse, q, k, v, kt, key_from, key_to, cosine, sine, pieces, offsets, pos,
                    k_tile):
    rows, width = d_first.shape
    seq = q.shape[1]
    n_own = rows // k_tile
    group_cols = GROUP * HD
    held = Pieces([pieces], width, slice(3 * width, 4 * width))
    n_in = len(held.flat)
    n_q = key_from.shape[0] * rows // seq

    def body(pos_ref, offs_ref, from_ref, to_ref, d_ref, att_ref, lse_ref, q_ref, k_ref, v_ref, kt_ref,
             cos_ref, sin_ref, *rest):
        w_refs, rest = rest[:n_in], rest[n_in:]
        dq_ref, dk_ref, dv_ref, dom, delta, dq, w_scr, sems = rest
        g = pl.program_id(0)

        @pl.when(g == 0)
        def _():
            held.start(0, w_refs, offs_ref, w_scr, sems)
            held.wait(0, w_refs, offs_ref, w_scr, sems)

        w_rows = w_scr[0, pl.ds(pl.multiple_of(g * group_cols, group_cols), group_cols), :]
        d_att = dot_nt(d_ref[...], w_rows).astype(BF16)
        prepare_heads(d_att, att_ref[...], dom, delta, 0)
        own_low = pos_ref[0] * n_own

        def weights_of(j, at, n):
            cols = slice(j // 2 * LANES, j // 2 * LANES + LANES)
            s = dot_nt(k_ref[j, pl.ds(at, n), :], q_ref[j])
            p = jnp.exp(s - lse_ref[0, j : j + 1, :])
            dp = dot_nt(v_ref[pl.ds(at, n), cols], dom[j])
            return p, (p * (dp - delta[j : j + 1, :])).astype(BF16)

        base = pl.multiple_of(pos_ref[0] * rows, rows)
        for b in range(GROUP // 2):
            dks, dvs = [], []
            for j in (2 * b, 2 * b + 1):
                p, ds = weights_of(j, base, rows)
                dvs.append(dot_nn(p.astype(BF16), dom[j]))
                dks.append(dot_nn(ds, q_ref[j]))
                heads = slice(j * HD, (j + 1) * HD)
                total = None
                for t in range(n_own):
                    part = dot_nn(kt_ref[own_low + t, heads, :], ds[t * k_tile : (t + 1) * k_tile, :])
                    total = part if total is None else total + part
                dq[heads, :] = total
            cols = slice(b * LANES, (b + 1) * LANES)
            dk_ref[:, cols] = pair_up(*dks)
            dv_ref[:, cols] = dvs[0] + dvs[1]

        first_tile = pos_ref[0] * n_q
        low = from_ref[first_tile]
        high = to_ref[first_tile + n_q - 1]
        n_left = jnp.maximum(own_low - low, 0)
        n_right = jnp.maximum(high - own_low - n_own, 0)

        def outside(i, carry):
            tile = jnp.where(i < n_left, low + i, own_low + n_own + i - n_left)
            at = pl.multiple_of(tile * k_tile, k_tile)
            for j in range(GROUP):
                heads = slice(j * HD, (j + 1) * HD)
                _, ds = weights_of(j, at, k_tile)
                dq[heads, :] += dot_nn(kt_ref[tile, heads, :], ds)
            return carry

        lax.fori_loop(0, n_left + n_right, outside, 0)
        turned = jnp.transpose(dq[...]) * (HD**-0.5)
        for b in range(GROUP // 2):
            cols = slice(b * LANES, (b + 1) * LANES)
            dq_ref[:, cols] = unrotated(turned[:, cols], cos_ref[...], sin_ref[...])

    def col_block(n):
        return pl.BlockSpec((n, group_cols), lambda g, *_: (0, g))

    table = pl.BlockSpec((rows, LANES), lambda g, p, *_: (p[0], 0))
    sum_shape = jax.ShapeDtypeStruct((rows, width), F32)
    return pl.pallas_call(
        body,
        grid_spec=pltpu.PrefetchScalarGridSpec(
            num_scalar_prefetch=4,
            grid=(H // GROUP,),
            in_specs=[
                whole_block((rows, width)),
                col_block(rows),
                pl.BlockSpec((1, 8, rows), lambda g, *_: (g, 0, 0)),
                pl.BlockSpec((GROUP, rows, LANES), lambda g, p, *_: (g, p[0], 0)),
                pl.BlockSpec((GROUP, seq, LANES), lambda g, *_: (g, 0, 0)),
                col_block(seq),
                pl.BlockSpec((seq // k_tile, group_cols, k_tile), lambda g, *_: (0, g, 0)),
                table,
                table,
            ]
            + held.in_specs,
            out_specs=[col_block(rows)] * 3,
            scratch_shapes=[
                pltpu.VMEM((GROUP, rows, LANES), BF16),
                pltpu.VMEM((8, rows), F32),
                pltpu.VMEM((group_cols, rows), F32),
            ]
            + held.scratch,
        ),
        out_shape=[jax.ShapeDtypeStruct((rows, width), BF16), sum_shape, sum_shape],
        compiler_params=params(20),
        name="attend_back_own",
    )(pos, offsets, key_from, key_to, d_first, attended, lse, q, k, in_hbm(v), in_hbm(kt), cosine, sine, *held.flat)


def attend_back_others(d_others, att_others, lse_others, sums, q, k, v, key_from, key_to, cosine, sine, pieces,
                       offsets, pos, q_tile, k_tile):
    rows, width = sums[0].shape
    seq = q.shape[1]
    n_q = rows // q_tile
    n_own = rows // k_tile
    n_tiles = d_others.shape[0] // q_tile
    group_cols = GROUP * HD
    held = Pieces([pieces], width, slice(3 * width, 4 * width))
    n_in = len(held.flat)

    def body(pos_ref, offs_ref, from_ref, to_ref, d_ref, att_ref, lse_ref, q_ref, k_ref, v_ref, dk_in, dv_in,
             cos_ref, sin_ref, *rest):
        w_refs, rest = rest[:n_in], rest[n_in:]
        dk_ref, dv_ref, dom, delta, dk, dv, w_scr, sems = rest
        g = pl.program_id(0)

        @pl.when(g == 0)
        def _():
            held.start(0, w_refs, offs_ref, w_scr, sems)
            held.wait(0, w_refs, offs_ref, w_scr, sems)

        dk[...] = dk_in[...]
        dv[...] = dv_in[...]
        own_low = pos_ref[0] * n_own

        for i in range(n_tiles):
            true_tile = (pos_ref[0] ^ (1 + i // n_q)) * n_q + i % n_q
            low = jnp.maximum(from_ref[true_tile], own_low)
            high = jnp.minimum(to_ref[true_tile], own_low + n_own)
            here = slice(i * q_tile, (i + 1) * q_tile)

            @pl.when(high > low)
            def _(i=i, true_tile=true_tile, low=low, high=high, here=here):
                w_rows = w_scr[0, pl.ds(pl.multiple_of(g * group_cols, group_cols), group_cols), :]
                d_att = dot_nt(d_ref[here, :], w_rows).astype(BF16)
                prepare_heads(d_att, att_ref[here, :], dom, delta, 0)
                q_at = pl.multiple_of(true_tile * q_tile, q_tile)

                def one(tile, carry):
                    at = pl.ds(pl.multiple_of((tile - own_low) * k_tile, k_tile), k_tile)
                    for b in range(GROUP // 2):
                        cols = slice(b * LANES, (b + 1) * LANES)
                        dks, dvs = [], []
                        for j in (2 * b, 2 * b + 1):
                            q_head = q_ref[j, pl.ds(q_at, q_tile), :]
                            s = dot_nt(k_ref[j, at, :], q_head)
                            p = jnp.exp(s - lse_ref[0, j : j + 1, here])
                            dp = dot_nt(v_ref[at, cols], dom[j])
                            ds = (p * (dp - delta[j : j + 1, :])).astype(BF16)
                            dvs.append(dot_nn(p.astype(BF16), dom[j]))
                            dks.append(dot_nn(ds, q_head))
                        dk[at, cols] += pair_up(*dks)
                        dv[at, cols] += dvs[0] + dvs[1]
                    return carry

                lax.fori_loop(low, high, one, 0)

        for b in range(GROUP // 2):
            cols = slice(b * LANES, (b + 1) * LANES)
            dk_ref[:, cols] = unrotated(dk[:, cols], cos_ref[...], sin_ref[...])
        dv_ref[...] = dv[...].astype(BF16)

    def col_block(n):
        return pl.BlockSpec((n, group_cols), lambda g, *_: (0, g))

    table = pl.BlockSpec((rows, LANES), lambda g, p, *_: (p[0], 0))
    return pl.pallas_call(
        body,
        grid_spec=pltpu.PrefetchScalarGridSpec(
            num_scalar_prefetch=4,
            grid=(H // GROUP,),
            in_specs=[
                whole_block(d_others.shape),
                col_block(d_others.shape[0]),
                pl.BlockSpec((1, 8, d_others.shape[0]), lambda g, *_: (g, 0, 0)),
                pl.BlockSpec((GROUP, seq, LANES), lambda g, *_: (g, 0, 0)),
                pl.BlockSpec((GROUP, rows, LANES), lambda g, p, *_: (g, p[0], 0)),
                pl.BlockSpec((rows, group_cols), lambda g, p, *_: (p[0], g)),
                col_block(rows),
                col_block(rows),
                table,
                table,
            ]
            + held.in_specs,
            out_specs=[col_block(rows)] * 2,
            scratch_shapes=[
                pltpu.VMEM((GROUP, q_tile, LANES), BF16),
                pltpu.VMEM((8, q_tile), F32),
                pltpu.VMEM((rows, group_cols), F32),
                pltpu.VMEM((rows, group_cols), F32),
            ]
            + held.scratch,
        ),
        out_shape=[jax.ShapeDtypeStruct((rows, width), BF16)] * 2,
        compiler_params=params(18),
        name="attend_back_others",
    )(pos, offsets, key_from, key_to, d_others, att_others, lse_others, q, k, in_hbm(v), *sums, cosine, sine,
      *held.flat)


def qkv_grads(x_own, merged, out_part, offsets, groups, n_blocks, block_rows):
    rows, width = x_own.shape
    wide = 3 * width + out_part.shape[1]

    def body(offs_ref, x_ref, dq_ref, dk_ref, dv_ref, out_ref, *rest):
        group_refs, g_scr = rest[:-1], rest[-1]
        x_t = jnp.transpose(x_ref[...])
        for j, ref in enumerate((dq_ref, dk_ref, dv_ref)):
            g_scr[:, j * width : (j + 1) * width] = dot_nn(x_t, ref[...])
        g_scr[:, 3 * width :] = out_ref[...].astype(F32)
        store_groups(groups, group_refs, offs_ref, n_blocks, block_rows, g_scr)

    group_shapes = [(len(picks), n_blocks, block_rows, wide) for picks, _ in groups]
    return pl.pallas_call(
        body,
        grid_spec=pltpu.PrefetchScalarGridSpec(
            num_scalar_prefetch=1,
            grid=(1,),
            in_specs=[whole_block((rows, width))] * 4 + [whole_block(out_part.shape)],
            out_specs=[whole_block(s) for s in group_shapes],
            scratch_shapes=[pltpu.VMEM((width, wide), F32)],
        ),
        out_shape=[jax.ShapeDtypeStruct(s, dtype) for s, (_, dtype) in zip(group_shapes, groups)],
        compiler_params=params(26),
        name="qkv_grads",
    )(offsets, x_own, *merged, out_part)


def input_grads(merged, d_first, pieces, offsets):
    rows, width = d_first.shape
    tile = min(256, rows)
    held = Pieces([pieces], width, slice(0, 3 * width))
    n_in = len(held.flat)

    def body(offs_ref, dq_ref, dk_ref, dv_ref, df_ref, *rest):
        w_refs, (out_ref, w_scr, sems) = rest[:n_in], rest[n_in:]

        @pl.when(pl.program_id(0) == 0)
        def _():
            held.start(0, w_refs, offs_ref, w_scr, sems)
            held.wait(0, w_refs, offs_ref, w_scr, sems)

        total = df_ref[...]
        for j, ref in enumerate((dq_ref, dk_ref, dv_ref)):
            total = total + dot_nt(ref[...], w_scr[0, :, j * width : (j + 1) * width])
        out_ref[...] = total

    block = pl.BlockSpec((tile, width), lambda i, o: (i, 0))
    return pl.pallas_call(
        body,
        grid_spec=pltpu.PrefetchScalarGridSpec(
            num_scalar_prefetch=1,
            grid=(rows // tile,),
            in_specs=[block] * 4 + held.in_specs,
            out_specs=block,
            scratch_shapes=held.scratch,
        ),
        out_shape=jax.ShapeDtypeStruct((rows, width), F32),
        compiler_params=params(12),
        name="input_grads",
    )(offsets, *merged, d_first, *held.flat)


def combine(kept, got):
    _, n_blocks, block_rows, wide = kept.shape

    def body(kept_ref, got_ref, own_ref, on_ref):
        own_ref[...] = kept_ref[0].astype(F32) + got_ref[0].astype(F32)
        on_ref[...] = (kept_ref[1].astype(F32) + got_ref[1].astype(F32)).astype(BF16)

    two = pl.BlockSpec((2, 1, block_rows, wide), lambda i: (0, i, 0, 0))
    one = pl.BlockSpec((1, block_rows, wide), lambda i: (i, 0, 0))
    shape = (n_blocks, block_rows, wide)
    return pl.pallas_call(
        body,
        grid=(n_blocks,),
        in_specs=[two, two],
        out_specs=[one, one],
        out_shape=[jax.ShapeDtypeStruct(shape, F32), jax.ShapeDtypeStruct(shape, BF16)],
        compiler_params=params(6),
        name="combine",
    )(kept, got)


def make_per_device(ndp, nt):
    plane = ndp // 2

    def move(value, chip=0, core=0, flip=0):
        pairs = []
        for d in range(ndp):
            for t in range(nt):
                to_d = ((d // 2) ^ chip) * 2 + ((d % 2) ^ core)
                pairs.append((d * nt + t, to_d * nt + (t ^ flip)))
        return lax.ppermute(value, AXES, pairs)

    def after(value, *others):
        return lax.optimization_barrier((value, *others))[0]

    def per_device(inputs, segment_ids, qkv_weight, out_weight, norm_gains, norm_biases,
                   gate_weight, up_weight, down_weight, out_grad):
        rows, width = inputs.shape
        seq = segment_ids.shape[1]
        n_row = seq // rows
        q_tile = min(256, rows)
        k_tile = min(256, rows)
        shard = qkv_weight.shape[0]
        ffn_rows, ffn_cols = gate_weight.shape
        half = ffn_cols // 2
        fast = plane == 4 and nt == 4 and n_row == 2

        d_index = lax.axis_index("dp")
        core = d_index % 2
        chip = d_index // 2
        t_index = lax.axis_index("tensor")
        pos = (t_index % n_row).astype(jnp.int32)
        block_at = [((chip ^ dxy) * 2 + (core ^ other)) for dxy in range(4) for other in range(2)]

        packed = jnp.concatenate(
            [qkv_weight, out_weight, norm_gains.T, norm_biases.T,
             jnp.zeros((shard, PAD - 4), BF16)], axis=1)
        seg = lax.dynamic_index_in_dim(segment_ids, t_index // n_row, 0, keepdims=False)
        doc_from = jnp.sum((seg[None, :] < seg[:, None]).astype(jnp.int32), axis=1)
        doc_to = jnp.sum((seg[None, :] <= seg[:, None]).astype(jnp.int32), axis=1)
        place = (jnp.arange(seq, dtype=jnp.int32) - doc_from).astype(F32)
        lane = np.arange(LANES)
        frequency = rope_base ** (-jnp.asarray(lane % (HD // 2), F32) * 2.0 / HD)
        angles = place[:, None] * frequency[None, :]
        cosine = jnp.cos(angles)
        sine = jnp.sin(angles) * jnp.asarray(np.where(lane % HD < HD // 2, -1.0, 1.0), F32)[None, :]
        key_from = doc_from[::q_tile] // k_tile
        key_to = (doc_to[q_tile - 1 :: q_tile] + k_tile - 1) // k_tile
        seg_col = seg[:, None]
        seg_row = seg.reshape(seq // q_tile, 1, q_tile)
        pos_arr = pos[None]

        ffn = (gate_weight, up_weight, down_weight.T)
        mine, given = [
            jnp.concatenate([lax.dynamic_slice_in_dim(w, c * half, half, 1) for w in ffn], axis=1)
            for c in (core, 1 - core)
        ]
        if fast:
            pair = jnp.stack([mine, move(given, core=1)])
            x_others = [move(inputs, flip=1)]
            second = move(pair, flip=2)
            by_flip = [packed] + [move(packed, flip=e) for e in range(1, nt)]
            near = jnp.concatenate(
                [lax.select_n(t_index, *[by_flip[j ^ t] for t in range(nt)]) for j in range(nt)], axis=0)[None]
            far = [move(near, chip=dxy) for dxy in range(1, 4)]
            last_two = move(jnp.stack([pair, second]), flip=1)
            plane_rows = after(jnp.concatenate([near] + far, axis=0), second, *x_others,
                               cosine, sine, key_from, key_to, seg_col)
            plane_sib = move(plane_rows, core=1)

            def spread(one):
                return one, move(one, chip=1), move(one, chip=2)

            def spread_on(sides, index, along_x, *others):
                passed = after(sides[1 if along_x else 2][index], *others)
                across = move(passed, chip=2 if along_x else 1)
                return [(side, index) for side in sides] + [(across[None], 0)]

            side_0 = spread(pair[None])
            side_1 = spread(after(second, *far)[None])
            x_rel = after(jnp.concatenate([inputs] + x_others, axis=0), *side_1[1:])
            w_pieces = [(plane_rows[None], 0), (plane_sib[None], 0)]
            w_offsets = jnp.stack(
                [((chip ^ dxy) * 2 + (core ^ other)) * (nt * shard) for other in range(2) for dxy in range(4)]
            ).astype(jnp.int32)
            f_offsets = jnp.stack([b * ffn_rows for b in block_at]).astype(jnp.int32)
            n_blocks, block_rows = 2, ffn_rows
        else:
            x_others = [move(inputs, flip=e) for e in range(1, n_row)]
            x_rel = jnp.concatenate([inputs] + x_others, axis=0)
            w_pieces = [(lax.all_gather(packed, AXES, axis=0, tiled=True)[None, None], 0)]
            w_offsets = jnp.zeros((1,), jnp.int32)
            full = lax.all_gather(mine, "dp", axis=0, tiled=True).reshape(width, 3, half)
            full = lax.all_gather(full, "tensor", axis=2, tiled=True)
            slots = [[(full.reshape(1, 1, width, 3 * half * nt), 0)]]
            f_offsets = jnp.zeros((1,), jnp.int32)
            n_blocks, block_rows = 1, width

        q, k, v, kt, vt, norms = project(
            x_rel, w_pieces, w_offsets, cosine, sine, seg_col, pos_arr, n_row, k_tile)
        if fast:
            q = after(q, *side_0[1:])
            slots = [spread_on(side_0, 0, True, q), spread_on(side_1, 0, False, q)]
            side_2 = spread(after(last_two, q))
        attended, lse, normed1, inv_std1, mid = attend(
            inputs, q, k, vt, w_pieces, w_offsets, norms, pos_arr)
        if fast:
            slots += [spread_on(side_2, 0, True, mid), spread_on(side_2, 1, False, mid)]
        mid_sib = move(mid, core=1)

        calls = [slots[:2], slots[2:]] if fast else [slots]
        acts, partial = [], None
        for j, some in enumerate(calls):
            hid, fac_a, fac_b, *partial = feed_forward(
                mid, mid_sib, some, f_offsets, partial[0] if j else None, j == len(calls) - 1)
            acts.append((hid, fac_a, fac_b))
        part_own, part_sib = partial
        att_others = [move(attended, flip=e) for e in range(1, n_row)]
        lse_others = [move(lse, flip=e) for e in range(1, n_row)]
        part_sib = move(after(part_sib, *att_others, *lse_others), core=1)
        outputs, d_second, d_ffn, norm2 = second_norm(normed1, part_own, part_sib, out_grad, norms)
        d_ffn_sib = move(d_ffn, core=1)
        d_both, d_mid, d_mid_give = hidden_back(
            (d_ffn, d_ffn_sib), [a[1:] for a in acts], slots, f_offsets)
        d_mid_sib = move(d_mid_give, core=1)

        def groups_of(s):
            if not fast:
                return [((0,), BF16)]
            if s % 2 == 0:
                return [((2, 3), BF16), ((0, 1), BF16)]
            return [((1, 3), BF16), ((0, 2), BF16)]

        def weight_grads(j, d_both):
            first = sum(len(c) for c in calls[:j])
            return ffn_grads(
                first, (mid, mid_sib), (d_ffn, d_ffn_sib), acts[j][0], d_both, f_offsets,
                [groups_of(first + i) for i in range(len(calls[j]))], n_blocks, block_rows)

        d_first, d_first_low, norm1 = first_norm_back(
            normed1, inv_std1, d_second, d_mid, d_mid_sib, norms)
        d_others = [move(d_first_low, flip=e) for e in range(1, n_row)]
        d_both = after(d_both, d_first_low)
        if fast:
            reduced = {2 + i: r for i, r in enumerate(weight_grads(1, d_both))}
            reduced.update(enumerate(weight_grads(0, d_both)))
        else:
            reduced = dict(enumerate(weight_grads(0, d_both)))

        def turn(s):
            return (2, 1) if s % 2 == 0 else (1, 2)

        arrived, owned = {}, {}
        if fast:
            arrived = {s: move(reduced[s][0], chip=turn(s)[0]) for s in range(nt)}

        def combine_on(s):
            own, on = combine(reduced[s][1], arrived[s])
            owned[s] = (own, move(on, chip=turn(s)[1]))

        def owned_sum(s, *others):
            own, on = owned[s]
            return own + after(on, *others).astype(F32)

        dq, *sums = attend_back_own(
            after(d_first_low, *[r[-1] for r in reduced.values()]), attended, lse, q, k, v, kt, key_from, key_to,
            cosine, sine, w_pieces, w_offsets, pos_arr, k_tile)
        if fast:
            arrived[2], arrived[3] = after(arrived[2], dq), after(arrived[3], dq)
            combine_on(2)
            combine_on(3)
            sums[0] = after(sums[0], owned[2][0], owned[3][0])
        dk, dv = attend_back_others(
            jnp.concatenate(d_others, axis=0), jnp.concatenate(att_others, axis=0),
            jnp.concatenate(lse_others, axis=2), sums, q, k, v, key_from, key_to, cosine, sine,
            w_pieces, w_offsets, pos_arr, q_tile, k_tile)
        out_part = out_grads(attended, d_first_low, norm1, norm2)
        if fast:
            arrived[0], arrived[1] = after(arrived[0], dk), after(arrived[1], dk)
            combine_on(0)
            combine_on(1)
            dv = after(dv, owned[0][0], owned[1][0])
        merged = (dq, dk, dv)

        if fast:
            q_groups = [((1, 3, 5, 7), BF16), ((0, 2, 4, 6), BF16)]
            q_offsets = jnp.stack([b * (nt * shard) for b in block_at]).astype(jnp.int32)
            q_rows = nt * shard
        else:
            q_groups = [((0,), F32)]
            q_offsets = jnp.zeros((1,), jnp.int32)
            q_rows = width
        q_parts = qkv_grads(inputs, merged, out_part, q_offsets, q_groups, 1, q_rows)
        inputs_grad = input_grads(merged, d_first, w_pieces, w_offsets)

        if fast:
            leaving = jnp.stack([owned_sum(2, q_parts[0]), owned_sum(3, q_parts[0])]).astype(BF16)
            back = move(leaving, flip=1)
            q_other = after(move(q_parts[0], core=1), inputs_grad, leaving, owned[0][1], owned[1][1])
            q_sum = q_parts[1][:, 0].astype(F32) + q_other[:, 0].astype(F32)
            leaving = owned_sum(1, q_sum) + back[1].astype(F32)
            last_back = move(leaving.astype(BF16), flip=2)
            q_own = q_sum[0]
            for dxy in range(1, 4):
                q_own = q_own + move(q_sum[dxy].astype(BF16), chip=dxy).astype(F32)
            total = owned_sum(0, q_sum) + back[0].astype(F32) + after(last_back, q_own).astype(F32)
            packed_grad = None
            for e in range(nt):
                piece = lax.dynamic_slice_in_dim(q_own, (t_index ^ e) * shard, shard, 0)
                if e:
                    piece = move(piece.astype(BF16), flip=e).astype(F32)
                packed_grad = piece if packed_grad is None else packed_grad + piece
            other = move(total[1], core=1)
            mine = total[0]
            grads = []
            for m in range(3):
                part = slice(m * half, (m + 1) * half)
                grads.append(jnp.where(
                    core == 0,
                    jnp.concatenate([mine[:, part], other[:, part]], axis=1),
                    jnp.concatenate([other[:, part], mine[:, part]], axis=1)))
        else:
            summed = lax.psum_scatter(
                reduced[0][0][0, 0].reshape(width, 3, half * nt), "tensor", scatter_dimension=2, tiled=True)
            spread = jnp.zeros((width, 3, 2 * half), BF16)
            spread = lax.dynamic_update_slice_in_dim(spread, summed.astype(BF16), core * half, 2)
            spread = lax.psum_scatter(spread, "dp", scatter_dimension=0, tiled=True).astype(F32)
            grads = [spread[:, m] for m in range(3)]
            packed_grad = lax.psum_scatter(q_parts[0][0, 0], AXES, scatter_dimension=0, tiled=True)

        return (
            outputs,
            inputs_grad,
            packed_grad[:, : 3 * width],
            packed_grad[:, 3 * width : 4 * width],
            packed_grad[:, 4 * width : 4 * width + 2].T,
            packed_grad[:, 4 * width + 2 : 4 * width + 4].T,
            grads[0],
            grads[1],
            grads[2].T,
        )

    return per_device


def solution(mesh):
    tokens = P(AXES, None)
    both = P("dp", "tensor")
    return jax.shard_map(
        make_per_device(mesh.shape["dp"], mesh.shape["tensor"]),
        mesh=mesh,
        in_specs=(tokens, P("dp", None), tokens, tokens, P(None, AXES), P(None, AXES),
                  both, both, P("tensor", "dp"), tokens),
        out_specs=(tokens, tokens, tokens, tokens, P(None, AXES), P(None, AXES),
                   both, both, P("tensor", "dp")),
        check_vma=False,
    )
```

```python
import jax
import jax.numpy as jnp
import numpy as np
from jax import lax
from jax.experimental import pallas as pl
from jax.experimental.pallas import tpu as pltpu
from jax.sharding import PartitionSpec as P

H = 12
HD = 64
LANES = 128
PAD = 128
NEG = -1e30

rope_base = 1000.0
layer_eps = 1e-12

AXES = ("dp", "tensor")
F32 = jnp.float32
BF16 = jnp.bfloat16


def params(mebibytes):
    return pltpu.CompilerParams(
        dimension_semantics=("arbitrary",), vmem_limit_bytes=mebibytes * 2**20
    )


def whole_block(shape):
    zeros = (0,) * len(shape)
    return pl.BlockSpec(shape, lambda *_: zeros, pipeline_mode=pl.Buffered(1))


def dot_nn(a, b):
    return lax.dot_general(a, b, (((1,), (0,)), ((), ())), preferred_element_type=F32)


def dot_nt(a, b):
    return lax.dot_general(a, b, (((1,), (1,)), ((), ())), preferred_element_type=F32)


def dot_tn(a, b):
    return lax.dot_general(a, b, (((0,), (0,)), ((), ())), preferred_element_type=F32)


def half_swap(block):
    lane = lax.broadcasted_iota(jnp.int32, block.shape, 1)
    return jnp.where(
        lane % HD < HD // 2, pltpu.roll(block, LANES - HD // 2, 1), pltpu.roll(block, HD // 2, 1)
    )


def normalise(summed):
    mean = jnp.mean(summed, axis=-1, keepdims=True)
    centred = summed - mean
    inv_std = lax.rsqrt(jnp.mean(centred * centred, axis=-1, keepdims=True) + layer_eps)
    return centred * inv_std, inv_std


def norm_back(normed, inv_std, gain, grad):
    scaled = grad * gain
    return inv_std * (
        scaled
        - jnp.mean(scaled, axis=-1, keepdims=True)
        - normed * jnp.mean(scaled * normed, axis=-1, keepdims=True)
    )


def in_hbm(x):
    return pltpu.with_memory_space_constraint(x, pltpu.HBM)


class Pieces:
    def __init__(self, slots, width, cols=None):
        arrays = []
        self.where = []
        for slot in slots:
            for array, index in slot:
                known = [i for i, other in enumerate(arrays) if other is array]
                if not known:
                    arrays.append(array)
                self.where.append((known[0] if known else len(arrays) - 1, index))
        self.flat = [in_hbm(x) for x in arrays]
        self.n_slots = len(slots)
        self.n_pieces = len(slots[0])
        self.blocks = [(p, b) for p, (x, _) in enumerate(slots[0]) for b in range(x.shape[1])]
        _, _, self.block_rows, wide = slots[0][0][0].shape
        self.cols = cols or slice(0, wide)
        self.in_specs = [pl.BlockSpec(memory_space=pl.ANY)] * len(self.flat)
        self.scratch = [
            pltpu.VMEM((self.n_slots, width, self.cols.stop - self.cols.start), BF16),
            pltpu.SemaphoreType.DMA((self.n_slots, len(self.blocks))),
        ]

    def copies(self, slot, refs, offs_ref, scr, sems):
        for j, (p, b) in enumerate(self.blocks):
            start = pl.multiple_of(offs_ref[j], 16)
            array, index = self.where[slot * self.n_pieces + p]
            yield pltpu.make_async_copy(
                refs[array].at[index, b, :, self.cols],
                scr.at[slot, pl.ds(start, self.block_rows), :],
                sems.at[slot, j],
            )

    def start(self, slot, *args):
        for copy in self.copies(slot, *args):
            copy.start()

    def wait(self, slot, *args):
        for copy in self.copies(slot, *args):
            copy.wait()

    def start_all(self, *args):
        for s in range(self.n_slots):
            self.start(s, *args)

    def wait_for_step(self, step, *args):
        for s in range(self.n_slots):

            @pl.when(step == s)
            def _(s=s):
                self.wait(s, *args)


def head_lanes(block, h, extra):
    lane = lax.broadcasted_iota(jnp.int32, block.shape, 1)
    mine = lane < HD if h % 2 == 0 else lane >= HD
    return jnp.where(mine, block, extra)


def project(x_rel, pieces, offsets, cosine, sine, seg_col, pos, n_row, k_tile):
    seq, width = x_rel.shape
    rows = seq // n_row
    tile = min(256, rows)
    per_piece = rows // tile
    held = Pieces([pieces], width)
    n_in = len(held.flat)

    def true_tile(i, pos_ref):
        return (pos_ref[0] ^ (i // per_piece)) * per_piece + i % per_piece

    def body(pos_ref, offs_ref, x_ref, cos_ref, sin_ref, seg_ref, *rest):
        w_refs, rest = rest[:n_in], rest[n_in:]
        q_ref, k_ref, v_ref, kt_ref, vt_ref, norm_ref, w_scr, sems = rest

        @pl.when(pl.program_id(0) == 0)
        def _():
            held.start(0, w_refs, offs_ref, w_scr, sems)
            held.wait(0, w_refs, offs_ref, w_scr, sems)
            norm_ref[...] = jnp.transpose(w_scr[0, :, 4 * width :].astype(F32))[:8, :]

        x = x_ref[...]
        cos = cos_ref[...]
        sin = sin_ref[...]
        lane = lax.broadcasted_iota(jnp.int32, (tile, LANES), 1)
        same = lane % HD == seg_ref[...]
        key_extra = jnp.where(same, 1.0, 0.0)
        query_extra = jnp.where(same, 0.0, NEG)
        merged = dot_nn(x, w_scr[0, :, : 3 * width])
        for b in range(width // LANES):
            cols = slice(b * LANES, (b + 1) * LANES)
            q = merged[:, b * LANES : (b + 1) * LANES]
            k = merged[:, width + b * LANES : width + (b + 1) * LANES]
            v = merged[:, 2 * width + b * LANES : 2 * width + (b + 1) * LANES]
            q = (q * cos + half_swap(q) * sin) * (HD**-0.5)
            k = k * cos + half_swap(k) * sin
            for h in (2 * b, 2 * b + 1):
                q_ref[h] = head_lanes(q, h, query_extra).astype(BF16)
                k_ref[h] = head_lanes(k, h, key_extra).astype(BF16)
            v_ref[:, cols] = v.astype(BF16)
            vt_ref[cols, :] = jnp.transpose(v).astype(BF16)
            for j in range(tile // k_tile):
                kt_ref[j, cols, :] = jnp.transpose(k[j * k_tile : (j + 1) * k_tile, :]).astype(BF16)

    row_block = pl.BlockSpec((tile, width), lambda i, p, o: (true_tile(i, p), 0))
    head_block = pl.BlockSpec((H, tile, LANES), lambda i, p, o: (0, true_tile(i, p), 0))
    table_block = pl.BlockSpec((tile, LANES), lambda i, p, o: (true_tile(i, p), 0))
    return pl.pallas_call(
        body,
        grid_spec=pltpu.PrefetchScalarGridSpec(
            num_scalar_prefetch=2,
            grid=(seq // tile,),
            in_specs=[
                pl.BlockSpec((tile, width), lambda i, p, o: (i, 0)),
                table_block,
                table_block,
                pl.BlockSpec((tile, 1), lambda i, p, o: (true_tile(i, p), 0)),
            ]
            + held.in_specs,
            out_specs=[
                head_block,
                head_block,
                row_block,
                pl.BlockSpec((tile // k_tile, width, k_tile), lambda i, p, o: (true_tile(i, p), 0, 0)),
                pl.BlockSpec((width, tile), lambda i, p, o: (0, true_tile(i, p))),
                whole_block((8, width)),
            ],
            scratch_shapes=held.scratch,
        ),
        out_shape=[jax.ShapeDtypeStruct((H, seq, LANES), BF16)] * 2
        + [
            jax.ShapeDtypeStruct((seq, width), BF16),
            jax.ShapeDtypeStruct((seq // k_tile, width, k_tile), BF16),
            jax.ShapeDtypeStruct((width, seq), BF16),
            jax.ShapeDtypeStruct((8, width), F32),
        ],
        compiler_params=params(20),
        name="project",
    )(pos, offsets, x_rel, cosine, sine, seg_col, *held.flat)


GROUP = 4


def attend(x_own, q, k, vt, pieces, offsets, norms, pos):
    rows, width = x_own.shape
    seq = q.shape[1]
    group_cols = GROUP * HD
    n_steps = H // GROUP
    held = Pieces([pieces], width, slice(3 * width, 4 * width))
    n_in = len(held.flat)

    def body(pos_ref, offs_ref, x_ref, q_ref, k_ref, vt_ref, norm_ref, *rest):
        w_refs, rest = rest[:n_in], rest[n_in:]
        att_ref, lse_ref, n_ref, istd_ref, mid_ref, acc, lse, w_scr, sems = rest
        g = pl.program_id(0)

        @pl.when(g == 0)
        def _():
            held.start(0, w_refs, offs_ref, w_scr, sems)

        for j in range(GROUP):
            s = dot_nt(k_ref[j], q_ref[j])
            peak = jnp.max(s, axis=0, keepdims=True)
            e = jnp.exp(s - peak)
            total = jnp.sum(e, axis=0, keepdims=True)
            out = dot_nn(vt_ref[j * HD : (j + 1) * HD, :], e.astype(BF16))
            acc[g, j * HD : (j + 1) * HD, :] = out / total
            lse[g, j : j + 1, :] = peak + jnp.log(total)

        @pl.when(g == n_steps - 1)
        def _():
            held.wait(0, w_refs, offs_ref, w_scr, sems)
            for i in range(n_steps):
                lse_ref[i] = lse[i]
                att_ref[:, i * group_cols : (i + 1) * group_cols] = jnp.transpose(acc[i]).astype(BF16)
            first_sum = x_ref[...].astype(F32) + dot_nn(att_ref[...], w_scr[0])
            normed, inv_std = normalise(first_sum)
            n_ref[...] = normed
            istd_ref[...] = inv_std
            mid_ref[...] = (normed * norm_ref[0:1, :] + norm_ref[2:3, :]).astype(BF16)

    own = whole_block((rows, width))
    return pl.pallas_call(
        body,
        grid_spec=pltpu.PrefetchScalarGridSpec(
            num_scalar_prefetch=2,
            grid=(n_steps,),
            in_specs=[
                own,
                pl.BlockSpec((GROUP, rows, LANES), lambda g, p, o: (g, p[0], 0)),
                pl.BlockSpec((GROUP, seq, LANES), lambda g, p, o: (g, 0, 0)),
                pl.BlockSpec((group_cols, seq), lambda g, p, o: (g, 0)),
                whole_block((8, width)),
            ]
            + held.in_specs,
            out_specs=[own, whole_block((n_steps, 8, rows)), own, whole_block((rows, 1)), own],
            scratch_shapes=[
                pltpu.VMEM((n_steps, group_cols, rows), F32),
                pltpu.VMEM((n_steps, 8, rows), F32),
            ]
            + held.scratch,
        ),
        out_shape=[
            jax.ShapeDtypeStruct((rows, width), BF16),
            jax.ShapeDtypeStruct((n_steps, 8, rows), F32),
            jax.ShapeDtypeStruct((rows, width), F32),
            jax.ShapeDtypeStruct((rows, 1), F32),
            jax.ShapeDtypeStruct((rows, width), BF16),
        ],
        compiler_params=params(18),
        name="attend",
    )(pos, offsets, x_own, q, k, vt, norms, *held.flat)


def feed_forward(mid_own, mid_sib, slots, offsets, before, last):
    rows, width = mid_own.shape
    held = Pieces(slots, width)
    n_slots, cols = held.n_slots, held.cols.stop // 3
    n_in = len(held.flat)

    def body(offs_ref, own_ref, sib_ref, *rest):
        w_refs, rest = rest[:n_in], rest[n_in:]
        if before is not None:
            before_ref, rest = rest[0], rest[1:]
        if last:
            hid_ref, a_ref, b_ref, out_own, out_sib, acc, w_scr, sems = rest
        else:
            hid_ref, a_ref, b_ref, acc, w_scr, sems = rest
        s = pl.program_id(0)

        @pl.when(s == 0)
        def _():
            held.start_all(w_refs, offs_ref, w_scr, sems)
            acc[...] = jnp.zeros(acc.shape, F32) if before is None else before_ref[...]

        held.wait_for_step(s, w_refs, offs_ref, w_scr, sems)
        for i, x_ref in enumerate((own_ref, sib_ref)):
            part = slice(i * rows, (i + 1) * rows)
            both = dot_nn(x_ref[...], w_scr[s, :, : 2 * cols])
            gate, up = both[:, :cols], both[:, cols:]
            sig = 0.5 * jnp.tanh(0.5 * gate) + 0.5
            silu = gate * sig
            hidden = (silu * up).astype(BF16)
            hid_ref[0, part, :] = hidden
            a_ref[0, part, :] = (up * (sig + silu * (1.0 - sig))).astype(BF16)
            b_ref[0, part, :] = silu.astype(BF16)
            acc[part, :] += dot_nt(hidden, w_scr[s, :, 2 * cols :])

        if last:

            @pl.when(s == n_slots - 1)
            def _():
                out_own[...] = acc[:rows, :]
                out_sib[...] = acc[rows:, :].astype(BF16)

    full = whole_block((rows, width))
    both_block = whole_block((2 * rows, width))
    act = pl.BlockSpec((1, 2 * rows, cols), lambda i, *_: (i, 0, 0))
    act_shape = jax.ShapeDtypeStruct((n_slots, 2 * rows, cols), BF16)
    extra = [] if before is None else [before]
    if last:
        acc_specs = [full, full]
        acc_shapes = [jax.ShapeDtypeStruct((rows, width), F32), jax.ShapeDtypeStruct((rows, width), BF16)]
        acc_scratch = [pltpu.VMEM((2 * rows, width), F32)]
    else:
        acc_specs = [both_block]
        acc_shapes = [jax.ShapeDtypeStruct((2 * rows, width), F32)]
        acc_scratch = []
    return pl.pallas_call(
        body,
        grid_spec=pltpu.PrefetchScalarGridSpec(
            num_scalar_prefetch=1,
            grid=(n_slots,),
            in_specs=[full, full] + held.in_specs + [both_block] * len(extra),
            out_specs=[act] * 3 + acc_specs,
            scratch_shapes=acc_scratch + held.scratch,
        ),
        out_shape=[act_shape] * 3 + acc_shapes,
        compiler_params=params(18),
        name="feed_forward",
    )(offsets, mid_own, mid_sib, *held.flat, *extra)


def second_norm(normed1, part_own, part_sib, out_grad, norms):
    rows, width = normed1.shape
    tile = min(256, rows)

    def body(n_ref, own_ref, sib_ref, g_ref, norm_ref, out_ref, d_ref, dl_ref, ng_ref):
        middle = n_ref[...] * norm_ref[0:1, :] + norm_ref[2:3, :]
        second_sum = middle + (own_ref[...] + sib_ref[...].astype(F32))
        normed, inv_std = normalise(second_sum)
        out_ref[...] = (normed * norm_ref[1:2, :] + norm_ref[3:4, :]).astype(BF16)
        grad = g_ref[...].astype(F32)
        d = norm_back(normed, inv_std, norm_ref[1:2, :], grad)
        d_ref[...] = d
        dl_ref[...] = d.astype(BF16)

        @pl.when(pl.program_id(0) == 0)
        def _():
            ng_ref[...] = jnp.zeros(ng_ref.shape, F32)

        ng_ref[0:1, :] += jnp.sum(grad * normed, axis=0, keepdims=True)
        ng_ref[1:2, :] += jnp.sum(grad, axis=0, keepdims=True)

    block = pl.BlockSpec((tile, width), lambda i: (i, 0))
    return pl.pallas_call(
        body,
        grid=(rows // tile,),
        in_specs=[block] * 4 + [whole_block((8, width))],
        out_specs=[block] * 3 + [whole_block((8, width))],
        out_shape=[
            jax.ShapeDtypeStruct((rows, width), BF16),
            jax.ShapeDtypeStruct((rows, width), F32),
            jax.ShapeDtypeStruct((rows, width), BF16),
            jax.ShapeDtypeStruct((8, width), F32),
        ],
        compiler_params=params(10),
        name="second_norm",
    )(normed1, part_own, part_sib, out_grad, norms)


def hidden_back(dffs, factors, slots, offsets):
    rows, width = dffs[0].shape
    held = Pieces(slots, width)
    n_slots, cols = held.n_slots, held.cols.stop // 3
    n_in = len(held.flat)
    per_call = factors[0][0].shape[0]
    n_fac = len(factors)

    def body(offs_ref, do_ref, ds_ref, *rest):
        fac_refs, rest = rest[: 2 * n_fac], rest[2 * n_fac :]
        w_refs, rest = rest[:n_in], rest[n_in:]
        d_ref, out_own, out_sib, acc, w_scr, sems = rest
        s = pl.program_id(0)

        @pl.when(s == 0)
        def _():
            held.start_all(w_refs, offs_ref, w_scr, sems)
            acc[...] = jnp.zeros(acc.shape, F32)

        held.wait_for_step(s, w_refs, offs_ref, w_scr, sems)

        def work(a_ref, b_ref):
            for i, x_ref in enumerate((do_ref, ds_ref)):
                part = slice(i * rows, (i + 1) * rows)
                dh = dot_nn(x_ref[...], w_scr[s, :, 2 * cols :])
                d_ref[0, part, :cols] = (dh * a_ref[0, part, :].astype(F32)).astype(BF16)
                d_ref[0, part, cols:] = (dh * b_ref[0, part, :].astype(F32)).astype(BF16)
                acc[part, :] += dot_nt(d_ref[0, part, :], w_scr[s, :, : 2 * cols])

        for f in range(n_fac):

            @pl.when(s // per_call == f)
            def _(f=f):
                work(fac_refs[2 * f], fac_refs[2 * f + 1])

        @pl.when(s == n_slots - 1)
        def _():
            out_own[...] = acc[:rows, :]
            out_sib[...] = acc[rows:, :].astype(BF16)

    full = whole_block((rows, width))

    def fac_spec(f):
        return pl.BlockSpec(
            (1, 2 * rows, cols), lambda i, *_: (jnp.clip(i - f * per_call, 0, per_call - 1), 0, 0)
        )

    return pl.pallas_call(
        body,
        grid_spec=pltpu.PrefetchScalarGridSpec(
            num_scalar_prefetch=1,
            grid=(n_slots,),
            in_specs=[full, full]
            + [fac_spec(f) for f in range(n_fac) for _ in range(2)]
            + held.in_specs,
            out_specs=[pl.BlockSpec((1, 2 * rows, 2 * cols), lambda i, *_: (i, 0, 0)), full, full],
            scratch_shapes=[pltpu.VMEM((2 * rows, width), F32)] + held.scratch,
        ),
        out_shape=[
            jax.ShapeDtypeStruct((n_slots, 2 * rows, 2 * cols), BF16),
            jax.ShapeDtypeStruct((rows, width), F32),
            jax.ShapeDtypeStruct((rows, width), BF16),
        ],
        compiler_params=params(22),
        name="hidden_back",
    )(offsets, *dffs, *[x for pair in factors for x in pair], *held.flat)


def store_groups(groups, group_refs, offs_ref, n_blocks, block_rows, source):
    for (picks, dtype), ref in zip(groups, group_refs):
        for j, p in enumerate(picks):
            for b in range(n_blocks):
                start = pl.multiple_of(offs_ref[p * n_blocks + b], 8)
                ref[j, b] = source[pl.ds(start, block_rows), :].astype(dtype)


def ffn_grads(first, mids, dffs, hidden, d_both, offsets, groups, n_blocks, block_rows):
    rows, width = mids[0].shape
    n_slots, _, cols = hidden.shape
    shapes = [[(len(picks), n_blocks, block_rows, 3 * cols) for picks, _ in gs] for gs in groups]
    n_out = [len(gs) for gs in groups]

    def body(offs_ref, mo, ms, do, ds, hid_ref, d_ref, *rest):
        outs, rest = rest[: sum(n_out)], rest[sum(n_out) :]
        stages, (mid_t, dff_t, g_scr, sems) = rest[: sum(n_out)], rest[sum(n_out) :]
        s = pl.program_id(0)

        @pl.when(s == 0)
        def _():
            for i, (m_ref, x_ref) in enumerate(((mo, do), (ms, ds))):
                part = slice(i * rows, (i + 1) * rows)
                mid_t[:, part] = jnp.transpose(m_ref[...])
                dff_t[:, part] = jnp.transpose(x_ref[...])

        g_scr[:, : 2 * cols] = dot_nn(mid_t[...], d_ref[0])
        g_scr[:, 2 * cols :] = dot_nn(dff_t[...], hid_ref[0])
        for j in range(n_slots):
            at = sum(n_out[:j])

            @pl.when(s == j)
            def _(j=j, at=at):
                store_groups(groups[j], stages[at : at + n_out[j]], offs_ref, n_blocks, block_rows, g_scr)
                for o in range(at, at + n_out[j]):
                    pltpu.make_async_copy(stages[o], outs[o], sems.at[o]).start()

        @pl.when(s == n_slots - 1)
        def _():
            for o in range(sum(n_out)):
                pltpu.make_async_copy(stages[o], outs[o], sems.at[o]).wait()

    flat = [(shape, dtype) for ss, gs in zip(shapes, groups) for shape, (_, dtype) in zip(ss, gs)]
    full = whole_block((rows, width))
    results = pl.pallas_call(
        body,
        grid_spec=pltpu.PrefetchScalarGridSpec(
            num_scalar_prefetch=1,
            grid=(n_slots,),
            in_specs=[full] * 4
            + [
                pl.BlockSpec((1, 2 * rows, cols), lambda i, *_: (i, 0, 0)),
                pl.BlockSpec((1, 2 * rows, 2 * cols), lambda i, *_: (first + i, 0, 0)),
            ],
            out_specs=[pl.BlockSpec(memory_space=pl.ANY)] * len(flat),
            scratch_shapes=[pltpu.VMEM(shape, dtype) for shape, dtype in flat]
            + [
                pltpu.VMEM((width, 2 * rows), BF16),
                pltpu.VMEM((width, 2 * rows), BF16),
                pltpu.VMEM((width, 3 * cols), F32),
                pltpu.SemaphoreType.DMA((len(flat),)),
            ],
        ),
        out_shape=[jax.ShapeDtypeStruct(shape, dtype) for shape, dtype in flat],
        compiler_params=params(22),
        name="ffn_grads",
    )(offsets, *mids, *dffs, hidden, d_both)
    return [results[sum(n_out[:j]) : sum(n_out[: j + 1])] for j in range(n_slots)]


def first_norm_back(normed1, inv_std1, d_second, d_mid, d_mid_sib, norms):
    rows, width = normed1.shape
    tile = min(256, rows)

    def body(n_ref, istd_ref, d2_ref, dm_ref, ds_ref, norm_ref, d_ref, dl_ref, ng_ref):
        grad = d2_ref[...] + dm_ref[...] + ds_ref[...].astype(F32)
        normed = n_ref[...]
        d = norm_back(normed, istd_ref[...], norm_ref[0:1, :], grad)
        d_ref[...] = d
        dl_ref[...] = d.astype(BF16)

        @pl.when(pl.program_id(0) == 0)
        def _():
            ng_ref[...] = jnp.zeros(ng_ref.shape, F32)

        ng_ref[0:1, :] += jnp.sum(grad * normed, axis=0, keepdims=True)
        ng_ref[1:2, :] += jnp.sum(grad, axis=0, keepdims=True)

    block = pl.BlockSpec((tile, width), lambda i: (i, 0))
    column = pl.BlockSpec((tile, 1), lambda i: (i, 0))
    return pl.pallas_call(
        body,
        grid=(rows // tile,),
        in_specs=[block, column, block, block, block, whole_block((8, width))],
        out_specs=[block] * 2 + [whole_block((8, width))],
        out_shape=[
            jax.ShapeDtypeStruct((rows, width), F32),
            jax.ShapeDtypeStruct((rows, width), BF16),
            jax.ShapeDtypeStruct((8, width), F32),
        ],
        compiler_params=params(8),
        name="first_norm_back",
    )(normed1, inv_std1, d_second, d_mid, d_mid_sib, norms)


def out_grads(attended, d_first_low, norm1, norm2):
    rows, width = attended.shape

    def body(att_ref, dl_ref, n1_ref, n2_ref, out_ref):
        out_ref[:, :width] = dot_tn(att_ref[...], dl_ref[...]).astype(BF16)
        stacked = jnp.concatenate(
            [n1_ref[0:1, :], n2_ref[0:1, :], n1_ref[1:2, :], n2_ref[1:2, :],
             jnp.zeros((PAD - 4, width), F32)], axis=0)
        out_ref[:, width:] = jnp.transpose(stacked).astype(BF16)

    operands = (attended, d_first_low, norm1, norm2)
    return pl.pallas_call(
        body,
        grid=(1,),
        in_specs=[whole_block(o.shape) for o in operands],
        out_specs=whole_block((width, width + PAD)),
        out_shape=jax.ShapeDtypeStruct((width, width + PAD), BF16),
        compiler_params=params(10),
        name="out_grads",
    )(*operands)


def unrotated(g, cos, sin):
    g = g.astype(BF16).astype(F32)
    return (g * cos - half_swap(g) * sin).astype(BF16)


def prepare_heads(d_att, att, dom, delta, at):
    n = d_att.shape[0]
    flipped = jnp.transpose(d_att.astype(F32) * att.astype(F32))
    for j in range(GROUP):
        delta[j : j + 1, at : at + n] = jnp.sum(flipped[j * HD : (j + 1) * HD, :], axis=0, keepdims=True)
        block = d_att[:, j // 2 * LANES : j // 2 * LANES + LANES].astype(F32)
        dom[j, at : at + n, :] = head_lanes(block, j, 0.0).astype(BF16)


def pair_up(even, odd):
    return head_lanes(even, 0, odd)


def attend_back_own(d_first, attended, lse, q, k, v, kt, key_from, key_to, cosine, sine, pieces, offsets, pos,
                    k_tile):
    rows, width = d_first.shape
    seq = q.shape[1]
    n_own = rows // k_tile
    group_cols = GROUP * HD
    held = Pieces([pieces], width, slice(3 * width, 4 * width))
    n_in = len(held.flat)
    n_q = key_from.shape[0] * rows // seq

    def body(pos_ref, offs_ref, from_ref, to_ref, d_ref, att_ref, lse_ref, q_ref, k_ref, v_ref, kt_ref,
             cos_ref, sin_ref, *rest):
        w_refs, rest = rest[:n_in], rest[n_in:]
        dq_ref, dk_ref, dv_ref, dom, delta, dq, w_scr, sems = rest
        g = pl.program_id(0)

        @pl.when(g == 0)
        def _():
            held.start(0, w_refs, offs_ref, w_scr, sems)
            held.wait(0, w_refs, offs_ref, w_scr, sems)

        w_rows = w_scr[0, pl.ds(pl.multiple_of(g * group_cols, group_cols), group_cols), :]
        d_att = dot_nt(d_ref[...], w_rows).astype(BF16)
        prepare_heads(d_att, att_ref[...], dom, delta, 0)
        own_low = pos_ref[0] * n_own

        def weights_of(j, at, n, some):
            cols = slice(j // 2 * LANES, j // 2 * LANES + LANES)
            s = dot_nt(k_ref[j, pl.ds(at, n), :], q_ref[j, some, :])
            p = jnp.exp(s - lse_ref[0, j : j + 1, some])
            dp = dot_nt(v_ref[pl.ds(at, n), cols], dom[j, some, :])
            return p, (p * (dp - delta[j : j + 1, some])).astype(BF16)

        base = pl.multiple_of(pos_ref[0] * rows, rows)
        for b in range(GROUP // 2):
            dks, dvs = [], []
            for j in (2 * b, 2 * b + 1):
                p, ds = weights_of(j, base, rows, slice(0, rows))
                dvs.append(dot_nn(p.astype(BF16), dom[j]))
                dks.append(dot_nn(ds, q_ref[j]))
                heads = slice(j * HD, (j + 1) * HD)
                total = None
                for t in range(n_own):
                    part = dot_nn(kt_ref[own_low + t, heads, :], ds[t * k_tile : (t + 1) * k_tile, :])
                    total = part if total is None else total + part
                dq[heads, :] = total
            cols = slice(b * LANES, (b + 1) * LANES)
            dk_ref[:, cols] = pair_up(*dks)
            dv_ref[:, cols] = dvs[0] + dvs[1]

        first_tile = pos_ref[0] * n_q
        for i in range(n_q):
            some = slice(i * rows // n_q, (i + 1) * rows // n_q)
            low = from_ref[first_tile + i]
            n_left = jnp.maximum(own_low - low, 0)
            n_right = jnp.maximum(to_ref[first_tile + i] - own_low - n_own, 0)

            def outside(t, carry, some=some, low=low, n_left=n_left):
                tile = jnp.where(t < n_left, low + t, own_low + n_own + t - n_left)
                at = pl.multiple_of(tile * k_tile, k_tile)
                for j in range(GROUP):
                    heads = slice(j * HD, (j + 1) * HD)
                    _, ds = weights_of(j, at, k_tile, some)
                    dq[heads, some] += dot_nn(kt_ref[tile, heads, :], ds)
                return carry

            lax.fori_loop(0, n_left + n_right, outside, 0)

        turned = jnp.transpose(dq[...]) * (HD**-0.5)
        for b in range(GROUP // 2):
            cols = slice(b * LANES, (b + 1) * LANES)
            dq_ref[:, cols] = unrotated(turned[:, cols], cos_ref[...], sin_ref[...])

    def col_block(n):
        return pl.BlockSpec((n, group_cols), lambda g, *_: (0, g))

    table = pl.BlockSpec((rows, LANES), lambda g, p, *_: (p[0], 0))
    sum_shape = jax.ShapeDtypeStruct((rows, width), F32)
    return pl.pallas_call(
        body,
        grid_spec=pltpu.PrefetchScalarGridSpec(
            num_scalar_prefetch=4,
            grid=(H // GROUP,),
            in_specs=[
                whole_block((rows, width)),
                col_block(rows),
                pl.BlockSpec((1, 8, rows), lambda g, *_: (g, 0, 0)),
                pl.BlockSpec((GROUP, rows, LANES), lambda g, p, *_: (g, p[0], 0)),
                pl.BlockSpec((GROUP, seq, LANES), lambda g, *_: (g, 0, 0)),
                col_block(seq),
                pl.BlockSpec((seq // k_tile, group_cols, k_tile), lambda g, *_: (0, g, 0)),
                table,
                table,
            ]
            + held.in_specs,
            out_specs=[col_block(rows)] * 3,
            scratch_shapes=[
                pltpu.VMEM((GROUP, rows, LANES), BF16),
                pltpu.VMEM((8, rows), F32),
                pltpu.VMEM((group_cols, rows), F32),
            ]
            + held.scratch,
        ),
        out_shape=[jax.ShapeDtypeStruct((rows, width), BF16), sum_shape, sum_shape],
        compiler_params=params(20),
        name="attend_back_own",
    )(pos, offsets, key_from, key_to, d_first, attended, lse, q, k, in_hbm(v), in_hbm(kt), cosine, sine, *held.flat)


def attend_back_others(d_others, att_others, lse_others, sums, q, k, v, key_from, key_to, cosine, sine, pieces,
                       offsets, pos, q_tile, k_tile):
    rows, width = sums[0].shape
    seq = q.shape[1]
    n_q = rows // q_tile
    n_own = rows // k_tile
    n_tiles = d_others.shape[0] // q_tile
    group_cols = GROUP * HD
    held = Pieces([pieces], width, slice(3 * width, 4 * width))
    n_in = len(held.flat)

    def body(pos_ref, offs_ref, from_ref, to_ref, d_ref, att_ref, lse_ref, q_ref, k_ref, v_ref, dk_in, dv_in,
             cos_ref, sin_ref, *rest):
        w_refs, rest = rest[:n_in], rest[n_in:]
        dk_ref, dv_ref, dom, delta, dk, dv, w_scr, sems = rest
        g = pl.program_id(0)

        @pl.when(g == 0)
        def _():
            held.start(0, w_refs, offs_ref, w_scr, sems)
            held.wait(0, w_refs, offs_ref, w_scr, sems)

        dk[...] = dk_in[...]
        dv[...] = dv_in[...]
        own_low = pos_ref[0] * n_own

        for i in range(n_tiles):
            true_tile = (pos_ref[0] ^ (1 + i // n_q)) * n_q + i % n_q
            low = jnp.maximum(from_ref[true_tile], own_low)
            high = jnp.minimum(to_ref[true_tile], own_low + n_own)
            here = slice(i * q_tile, (i + 1) * q_tile)

            @pl.when(high > low)
            def _(i=i, true_tile=true_tile, low=low, high=high, here=here):
                w_rows = w_scr[0, pl.ds(pl.multiple_of(g * group_cols, group_cols), group_cols), :]
                d_att = dot_nt(d_ref[here, :], w_rows).astype(BF16)
                prepare_heads(d_att, att_ref[here, :], dom, delta, 0)
                q_at = pl.multiple_of(true_tile * q_tile, q_tile)

                def one(tile, carry):
                    at = pl.ds(pl.multiple_of((tile - own_low) * k_tile, k_tile), k_tile)
                    for b in range(GROUP // 2):
                        cols = slice(b * LANES, (b + 1) * LANES)
                        dks, dvs = [], []
                        for j in (2 * b, 2 * b + 1):
                            q_head = q_ref[j, pl.ds(q_at, q_tile), :]
                            s = dot_nt(k_ref[j, at, :], q_head)
                            p = jnp.exp(s - lse_ref[0, j : j + 1, here])
                            dp = dot_nt(v_ref[at, cols], dom[j])
                            ds = (p * (dp - delta[j : j + 1, :])).astype(BF16)
                            dvs.append(dot_nn(p.astype(BF16), dom[j]))
                            dks.append(dot_nn(ds, q_head))
                        dk[at, cols] += pair_up(*dks)
                        dv[at, cols] += dvs[0] + dvs[1]
                    return carry

                lax.fori_loop(low, high, one, 0)

        for b in range(GROUP // 2):
            cols = slice(b * LANES, (b + 1) * LANES)
            dk_ref[:, cols] = unrotated(dk[:, cols], cos_ref[...], sin_ref[...])
        dv_ref[...] = dv[...].astype(BF16)

    def col_block(n):
        return pl.BlockSpec((n, group_cols), lambda g, *_: (0, g))

    table = pl.BlockSpec((rows, LANES), lambda g, p, *_: (p[0], 0))
    return pl.pallas_call(
        body,
        grid_spec=pltpu.PrefetchScalarGridSpec(
            num_scalar_prefetch=4,
            grid=(H // GROUP,),
            in_specs=[
                whole_block(d_others.shape),
                col_block(d_others.shape[0]),
                pl.BlockSpec((1, 8, d_others.shape[0]), lambda g, *_: (g, 0, 0)),
                pl.BlockSpec((GROUP, seq, LANES), lambda g, *_: (g, 0, 0)),
                pl.BlockSpec((GROUP, rows, LANES), lambda g, p, *_: (g, p[0], 0)),
                pl.BlockSpec((rows, group_cols), lambda g, p, *_: (p[0], g)),
                col_block(rows),
                col_block(rows),
                table,
                table,
            ]
            + held.in_specs,
            out_specs=[col_block(rows)] * 2,
            scratch_shapes=[
                pltpu.VMEM((GROUP, q_tile, LANES), BF16),
                pltpu.VMEM((8, q_tile), F32),
                pltpu.VMEM((rows, group_cols), F32),
                pltpu.VMEM((rows, group_cols), F32),
            ]
            + held.scratch,
        ),
        out_shape=[jax.ShapeDtypeStruct((rows, width), BF16)] * 2,
        compiler_params=params(18),
        name="attend_back_others",
    )(pos, offsets, key_from, key_to, d_others, att_others, lse_others, q, k, in_hbm(v), *sums, cosine, sine,
      *held.flat)


def qkv_grads(x_own, merged, out_part, offsets, groups, n_blocks, block_rows):
    rows, width = x_own.shape
    wide = 3 * width + out_part.shape[1]

    def body(offs_ref, x_ref, dq_ref, dk_ref, dv_ref, out_ref, *rest):
        group_refs, g_scr = rest[:-1], rest[-1]
        x_t = jnp.transpose(x_ref[...])
        for j, ref in enumerate((dq_ref, dk_ref, dv_ref)):
            g_scr[:, j * width : (j + 1) * width] = dot_nn(x_t, ref[...])
        g_scr[:, 3 * width :] = out_ref[...].astype(F32)
        store_groups(groups, group_refs, offs_ref, n_blocks, block_rows, g_scr)

    group_shapes = [(len(picks), n_blocks, block_rows, wide) for picks, _ in groups]
    return pl.pallas_call(
        body,
        grid_spec=pltpu.PrefetchScalarGridSpec(
            num_scalar_prefetch=1,
            grid=(1,),
            in_specs=[whole_block((rows, width))] * 4 + [whole_block(out_part.shape)],
            out_specs=[whole_block(s) for s in group_shapes],
            scratch_shapes=[pltpu.VMEM((width, wide), F32)],
        ),
        out_shape=[jax.ShapeDtypeStruct(s, dtype) for s, (_, dtype) in zip(group_shapes, groups)],
        compiler_params=params(20),
        name="qkv_grads",
    )(offsets, x_own, *merged, out_part)


def input_grads(merged, d_first, pieces, offsets):
    rows, width = d_first.shape
    tile = min(256, rows)
    held = Pieces([pieces], width, slice(0, 3 * width))
    n_in = len(held.flat)

    def body(offs_ref, dq_ref, dk_ref, dv_ref, df_ref, *rest):
        w_refs, (out_ref, w_scr, sems) = rest[:n_in], rest[n_in:]

        @pl.when(pl.program_id(0) == 0)
        def _():
            held.start(0, w_refs, offs_ref, w_scr, sems)
            held.wait(0, w_refs, offs_ref, w_scr, sems)

        total = df_ref[...]
        for j, ref in enumerate((dq_ref, dk_ref, dv_ref)):
            total = total + dot_nt(ref[...], w_scr[0, :, j * width : (j + 1) * width])
        out_ref[...] = total

    block = pl.BlockSpec((tile, width), lambda i, o: (i, 0))
    return pl.pallas_call(
        body,
        grid_spec=pltpu.PrefetchScalarGridSpec(
            num_scalar_prefetch=1,
            grid=(rows // tile,),
            in_specs=[block] * 4 + held.in_specs,
            out_specs=block,
            scratch_shapes=held.scratch,
        ),
        out_shape=jax.ShapeDtypeStruct((rows, width), F32),
        compiler_params=params(12),
        name="input_grads",
    )(offsets, *map(in_hbm, merged), in_hbm(d_first), *held.flat)


def combine(kept, got):
    _, n_blocks, block_rows, wide = kept.shape

    def body(kept_ref, got_ref, own_ref, on_ref):
        own_ref[...] = kept_ref[0].astype(F32) + got_ref[0].astype(F32)
        on_ref[...] = (kept_ref[1].astype(F32) + got_ref[1].astype(F32)).astype(BF16)

    two = pl.BlockSpec((2, 1, block_rows, wide), lambda i: (0, i, 0, 0))
    one = pl.BlockSpec((1, block_rows, wide), lambda i: (i, 0, 0))
    shape = (n_blocks, block_rows, wide)
    return pl.pallas_call(
        body,
        grid=(n_blocks,),
        in_specs=[two, two],
        out_specs=[one, one],
        out_shape=[jax.ShapeDtypeStruct(shape, F32), jax.ShapeDtypeStruct(shape, BF16)],
        compiler_params=params(6),
        name="combine",
    )(kept, got)


def make_per_device(ndp, nt):
    plane = ndp // 2

    def move(value, chip=0, core=0, flip=0):
        pairs = []
        for d in range(ndp):
            for t in range(nt):
                to_d = ((d // 2) ^ chip) * 2 + ((d % 2) ^ core)
                pairs.append((d * nt + t, to_d * nt + (t ^ flip)))
        return lax.ppermute(value, AXES, pairs)

    def after(value, *others):
        return lax.optimization_barrier((value, *others))[0]

    def per_device(inputs, segment_ids, qkv_weight, out_weight, norm_gains, norm_biases,
                   gate_weight, up_weight, down_weight, out_grad):
        rows, width = inputs.shape
        seq = segment_ids.shape[1]
        n_row = seq // rows
        q_tile = min(256, rows)
        k_tile = min(256, rows)
        shard = qkv_weight.shape[0]
        ffn_rows, ffn_cols = gate_weight.shape
        half = ffn_cols // 2
        fast = plane == 4 and nt == 4 and n_row == 2

        d_index = lax.axis_index("dp")
        core = d_index % 2
        chip = d_index // 2
        t_index = lax.axis_index("tensor")
        pos = (t_index % n_row).astype(jnp.int32)
        block_at = [((chip ^ dxy) * 2 + (core ^ other)) for dxy in range(4) for other in range(2)]

        packed = jnp.concatenate(
            [qkv_weight, out_weight, norm_gains.T, norm_biases.T,
             jnp.zeros((shard, PAD - 4), BF16)], axis=1)
        seg = lax.dynamic_index_in_dim(segment_ids, t_index // n_row, 0, keepdims=False)
        doc_from = jnp.sum((seg[None, :] < seg[:, None]).astype(jnp.int32), axis=1)
        doc_to = jnp.sum((seg[None, :] <= seg[:, None]).astype(jnp.int32), axis=1)
        place = (jnp.arange(seq, dtype=jnp.int32) - doc_from).astype(F32)
        lane = np.arange(LANES)
        frequency = rope_base ** (-jnp.asarray(lane % (HD // 2), F32) * 2.0 / HD)
        angles = place[:, None] * frequency[None, :]
        cosine = jnp.cos(angles)
        sine = jnp.sin(angles) * jnp.asarray(np.where(lane % HD < HD // 2, -1.0, 1.0), F32)[None, :]
        key_from = doc_from[::q_tile] // k_tile
        key_to = (doc_to[q_tile - 1 :: q_tile] + k_tile - 1) // k_tile
        seg_col = seg[:, None]
        seg_row = seg.reshape(seq // q_tile, 1, q_tile)
        pos_arr = pos[None]

        ffn = (gate_weight, up_weight, down_weight.T)
        mine, given = [
            jnp.concatenate([lax.dynamic_slice_in_dim(w, c * half, half, 1) for w in ffn], axis=1)
            for c in (core, 1 - core)
        ]
        if fast:
            pair = jnp.stack([mine, move(given, core=1)])
            x_others = [move(inputs, flip=1)]
            second = move(pair, flip=2)
            by_flip = [packed] + [move(packed, flip=e) for e in range(1, nt)]
            near = jnp.concatenate(
                [lax.select_n(t_index, *[by_flip[j ^ t] for t in range(nt)]) for j in range(nt)], axis=0)[None]
            far = [move(near, chip=dxy) for dxy in range(1, 4)]
            last_two = move(jnp.stack([pair, second]), flip=1)
            plane_rows = after(jnp.concatenate([near] + far, axis=0), second, *x_others,
                               cosine, sine, key_from, key_to, seg_col)
            plane_sib = move(plane_rows, core=1)

            def spread(one):
                return one, move(one, chip=1), move(one, chip=2)

            def spread_on(sides, index, along_x, *others):
                passed = after(sides[1 if along_x else 2][index], *others)
                across = move(passed, chip=2 if along_x else 1)
                return [(side, index) for side in sides] + [(across[None], 0)]

            side_0 = spread(pair[None])
            side_1 = spread(after(second, *far)[None])
            x_rel = jnp.concatenate([inputs] + x_others, axis=0)
            w_pieces = [(plane_rows[None], 0), (plane_sib[None], 0)]
            w_offsets = jnp.stack(
                [((chip ^ dxy) * 2 + (core ^ other)) * (nt * shard) for other in range(2) for dxy in range(4)]
            ).astype(jnp.int32)
            f_offsets = jnp.stack([b * ffn_rows for b in block_at]).astype(jnp.int32)
            n_blocks, block_rows = 2, ffn_rows
        else:
            x_others = [move(inputs, flip=e) for e in range(1, n_row)]
            x_rel = jnp.concatenate([inputs] + x_others, axis=0)
            w_pieces = [(lax.all_gather(packed, AXES, axis=0, tiled=True)[None, None], 0)]
            w_offsets = jnp.zeros((1,), jnp.int32)
            full = lax.all_gather(mine, "dp", axis=0, tiled=True).reshape(width, 3, half)
            full = lax.all_gather(full, "tensor", axis=2, tiled=True)
            slots = [[(full.reshape(1, 1, width, 3 * half * nt), 0)]]
            f_offsets = jnp.zeros((1,), jnp.int32)
            n_blocks, block_rows = 1, width

        q, k, v, kt, vt, norms = project(
            x_rel, w_pieces, w_offsets, cosine, sine, seg_col, pos_arr, n_row, k_tile)
        if fast:
            q = after(q, *side_0[1:], *side_1[1:])
            slots = [spread_on(side_0, 0, True, q), spread_on(side_1, 0, False, q)]
            side_2 = spread(after(last_two, q))
        attended, lse, normed1, inv_std1, mid = attend(
            inputs, q, k, vt, w_pieces, w_offsets, norms, pos_arr)
        if fast:
            slots += [spread_on(side_2, 0, True, mid), spread_on(side_2, 1, False, mid)]
        mid_sib = move(mid, core=1)

        calls = [slots[:2], slots[2:]] if fast else [slots]
        acts, partial = [], None
        for j, some in enumerate(calls):
            hid, fac_a, fac_b, *partial = feed_forward(
                mid, mid_sib, some, f_offsets, partial[0] if j else None, j == len(calls) - 1)
            acts.append((hid, fac_a, fac_b))
        part_own, part_sib = partial
        att_others = [move(attended, flip=e) for e in range(1, n_row)]
        lse_others = [move(lse, flip=e) for e in range(1, n_row)]
        part_sib = move(after(part_sib, *att_others, *lse_others), core=1)
        outputs, d_second, d_ffn, norm2 = second_norm(normed1, part_own, part_sib, out_grad, norms)
        d_ffn_sib = move(d_ffn, core=1)
        d_both, d_mid, d_mid_give = hidden_back(
            (d_ffn, d_ffn_sib), [a[1:] for a in acts], slots, f_offsets)
        d_mid_sib = move(d_mid_give, core=1)

        def groups_of(s):
            if not fast:
                return [((0,), BF16)]
            if s % 2 == 0:
                return [((2, 3), BF16), ((0, 1), BF16)]
            return [((1, 3), BF16), ((0, 2), BF16)]

        def weight_grads(j, d_both):
            first = sum(len(c) for c in calls[:j])
            return ffn_grads(
                first, (mid, mid_sib), (d_ffn, d_ffn_sib), acts[j][0], d_both, f_offsets,
                [groups_of(first + i) for i in range(len(calls[j]))], n_blocks, block_rows)

        d_first, d_first_low, norm1 = first_norm_back(
            normed1, inv_std1, d_second, d_mid, d_mid_sib, norms)
        d_others = [move(d_first_low, flip=e) for e in range(1, n_row)]
        d_both = after(d_both, d_first_low)
        if fast:
            reduced = {2 + i: r for i, r in enumerate(weight_grads(1, d_both))}
            reduced.update(enumerate(weight_grads(0, d_both)))
        else:
            reduced = dict(enumerate(weight_grads(0, d_both)))

        def turn(s):
            return (2, 1) if s % 2 == 0 else (1, 2)

        arrived, owned = {}, {}
        if fast:
            arrived = {s: move(reduced[s][0], chip=turn(s)[0]) for s in range(nt)}

        def combine_on(s):
            own, on = combine(reduced[s][1], arrived[s])
            owned[s] = (own, move(on, chip=turn(s)[1]))

        def owned_sum(s, *others):
            own, on = owned[s]
            return own + after(on, *others).astype(F32)

        dq, *sums = attend_back_own(
            after(d_first_low, *[r[-1] for r in reduced.values()]), attended, lse, q, k, v, kt, key_from, key_to,
            cosine, sine, w_pieces, w_offsets, pos_arr, k_tile)
        if fast:
            arrived[2], arrived[3] = after(arrived[2], dq), after(arrived[3], dq)
            combine_on(2)
            combine_on(3)
            sums[0] = after(sums[0], owned[2][0], owned[3][0])
        dk, dv = attend_back_others(
            jnp.concatenate(d_others, axis=0), jnp.concatenate(att_others, axis=0),
            jnp.concatenate(lse_others, axis=2), sums, q, k, v, key_from, key_to, cosine, sine,
            w_pieces, w_offsets, pos_arr, q_tile, k_tile)
        out_part = out_grads(attended, d_first_low, norm1, norm2)
        if fast:
            arrived[0], arrived[1] = after(arrived[0], dk), after(arrived[1], dk)
            combine_on(0)
            combine_on(1)
            dv = after(dv, owned[0][0], owned[1][0])
        merged = (dq, dk, dv)

        if fast:
            q_groups = [((1, 3, 5, 7), BF16), ((0, 2, 4, 6), BF16)]
            q_offsets = jnp.stack([b * (nt * shard) for b in block_at]).astype(jnp.int32)
            q_rows = nt * shard
        else:
            q_groups = [((0,), F32)]
            q_offsets = jnp.zeros((1,), jnp.int32)
            q_rows = width
        q_parts = qkv_grads(inputs, merged, out_part, q_offsets, q_groups, 1, q_rows)
        inputs_grad = input_grads(merged, d_first, w_pieces, w_offsets)

        if fast:
            leaving = jnp.stack([owned_sum(2, q_parts[0]), owned_sum(3, q_parts[0])]).astype(BF16)
            back = move(leaving, flip=1)
            q_other = after(move(q_parts[0], core=1), inputs_grad, leaving, owned[0][1], owned[1][1])
            q_sum = q_parts[1][:, 0].astype(F32) + q_other[:, 0].astype(F32)
            leaving = owned_sum(1, q_sum) + back[1].astype(F32)
            last_back = move(leaving.astype(BF16), flip=2)
            q_own = q_sum[0]
            for dxy in range(1, 4):
                q_own = q_own + move(q_sum[dxy].astype(BF16), chip=dxy).astype(F32)
            total = owned_sum(0, q_sum) + back[0].astype(F32) + after(last_back, q_own).astype(F32)
            packed_grad = None
            for e in range(nt):
                piece = lax.dynamic_slice_in_dim(q_own, (t_index ^ e) * shard, shard, 0)
                if e:
                    piece = move(piece.astype(BF16), flip=e).astype(F32)
                packed_grad = piece if packed_grad is None else packed_grad + piece
            other = move(total[1], core=1)
            mine = total[0]
            grads = []
            for m in range(3):
                part = slice(m * half, (m + 1) * half)
                grads.append(jnp.where(
                    core == 0,
                    jnp.concatenate([mine[:, part], other[:, part]], axis=1),
                    jnp.concatenate([other[:, part], mine[:, part]], axis=1)))
        else:
            summed = lax.psum_scatter(
                reduced[0][0][0, 0].reshape(width, 3, half * nt), "tensor", scatter_dimension=2, tiled=True)
            spread = jnp.zeros((width, 3, 2 * half), BF16)
            spread = lax.dynamic_update_slice_in_dim(spread, summed.astype(BF16), core * half, 2)
            spread = lax.psum_scatter(spread, "dp", scatter_dimension=0, tiled=True).astype(F32)
            grads = [spread[:, m] for m in range(3)]
            packed_grad = lax.psum_scatter(q_parts[0][0, 0], AXES, scatter_dimension=0, tiled=True)

        return (
            outputs,
            inputs_grad,
            packed_grad[:, : 3 * width],
            packed_grad[:, 3 * width : 4 * width],
            packed_grad[:, 4 * width : 4 * width + 2].T,
            packed_grad[:, 4 * width + 2 : 4 * width + 4].T,
            grads[0],
            grads[1],
            grads[2].T,
        )

    return per_device


def solution(mesh):
    tokens = P(AXES, None)
    both = P("dp", "tensor")
    return jax.shard_map(
        make_per_device(mesh.shape["dp"], mesh.shape["tensor"]),
        mesh=mesh,
        in_specs=(tokens, P("dp", None), tokens, tokens, P(None, AXES), P(None, AXES),
                  both, both, P("tensor", "dp"), tokens),
        out_specs=(tokens, tokens, tokens, tokens, P(None, AXES), P(None, AXES),
                   both, both, P("tensor", "dp")),
        check_vma=False,
    )
```

```python
import jax
import jax.numpy as jnp
import numpy as np
from jax import lax
from jax.experimental import pallas as pl
from jax.experimental.pallas import tpu as pltpu
from jax.sharding import PartitionSpec as P

H = 12
HD = 64
LANES = 128
PAD = 128
NEG = -1e30

rope_base = 1000.0
layer_eps = 1e-12

AXES = ("dp", "tensor")
F32 = jnp.float32
BF16 = jnp.bfloat16


def params(mebibytes):
    return pltpu.CompilerParams(
        dimension_semantics=("arbitrary",), vmem_limit_bytes=mebibytes * 2**20
    )


def whole_block(shape):
    zeros = (0,) * len(shape)
    return pl.BlockSpec(shape, lambda *_: zeros, pipeline_mode=pl.Buffered(1))


def dot_nn(a, b):
    return lax.dot_general(a, b, (((1,), (0,)), ((), ())), preferred_element_type=F32)


def dot_nt(a, b):
    return lax.dot_general(a, b, (((1,), (1,)), ((), ())), preferred_element_type=F32)


def dot_tn(a, b):
    return lax.dot_general(a, b, (((0,), (0,)), ((), ())), preferred_element_type=F32)


def half_swap(block):
    lane = lax.broadcasted_iota(jnp.int32, block.shape, 1)
    return jnp.where(
        lane % HD < HD // 2, pltpu.roll(block, LANES - HD // 2, 1), pltpu.roll(block, HD // 2, 1)
    )


def normalise(summed):
    mean = jnp.mean(summed, axis=-1, keepdims=True)
    centred = summed - mean
    inv_std = lax.rsqrt(jnp.mean(centred * centred, axis=-1, keepdims=True) + layer_eps)
    return centred * inv_std, inv_std


def norm_back(normed, inv_std, gain, grad):
    scaled = grad * gain
    return inv_std * (
        scaled
        - jnp.mean(scaled, axis=-1, keepdims=True)
        - normed * jnp.mean(scaled * normed, axis=-1, keepdims=True)
    )


def in_hbm(x):
    return pltpu.with_memory_space_constraint(x, pltpu.HBM)


class Pieces:
    def __init__(self, slots, width, cols=None):
        arrays = []
        self.where = []
        for slot in slots:
            for array, index in slot:
                known = [i for i, other in enumerate(arrays) if other is array]
                if not known:
                    arrays.append(array)
                self.where.append((known[0] if known else len(arrays) - 1, index))
        self.flat = [in_hbm(x) for x in arrays]
        self.n_slots = len(slots)
        self.n_pieces = len(slots[0])
        self.blocks = [(p, b) for p, (x, _) in enumerate(slots[0]) for b in range(x.shape[1])]
        _, _, self.block_rows, wide = slots[0][0][0].shape
        self.cols = cols or slice(0, wide)
        self.in_specs = [pl.BlockSpec(memory_space=pl.ANY)] * len(self.flat)
        self.scratch = [
            pltpu.VMEM((self.n_slots, width, self.cols.stop - self.cols.start), BF16),
            pltpu.SemaphoreType.DMA((self.n_slots, len(self.blocks))),
        ]

    def copies(self, slot, refs, offs_ref, scr, sems):
        for j, (p, b) in enumerate(self.blocks):
            start = pl.multiple_of(offs_ref[j], 16)
            array, index = self.where[slot * self.n_pieces + p]
            yield pltpu.make_async_copy(
                refs[array].at[index, b, :, self.cols],
                scr.at[slot, pl.ds(start, self.block_rows), :],
                sems.at[slot, j],
            )

    def start(self, slot, *args):
        for copy in self.copies(slot, *args):
            copy.start()

    def wait(self, slot, *args):
        for copy in self.copies(slot, *args):
            copy.wait()

    def start_all(self, *args):
        for s in range(self.n_slots):
            self.start(s, *args)

    def wait_for_step(self, step, *args):
        for s in range(self.n_slots):

            @pl.when(step == s)
            def _(s=s):
                self.wait(s, *args)


def head_lanes(block, h, extra):
    lane = lax.broadcasted_iota(jnp.int32, block.shape, 1)
    mine = lane < HD if h % 2 == 0 else lane >= HD
    return jnp.where(mine, block, extra)


def project(x_rel, pieces, offsets, cosine, sine, seg_col, pos, n_row, k_tile):
    seq, width = x_rel.shape
    rows = seq // n_row
    tile = min(256, rows)
    per_piece = rows // tile
    held = Pieces([pieces], width)
    n_in = len(held.flat)

    def true_tile(i, pos_ref):
        return (pos_ref[0] ^ (i // per_piece)) * per_piece + i % per_piece

    def body(pos_ref, offs_ref, x_ref, cos_ref, sin_ref, seg_ref, *rest):
        w_refs, rest = rest[:n_in], rest[n_in:]
        q_ref, k_ref, v_ref, kt_ref, vt_ref, norm_ref, w_scr, sems = rest

        @pl.when(pl.program_id(0) == 0)
        def _():
            held.start(0, w_refs, offs_ref, w_scr, sems)
            held.wait(0, w_refs, offs_ref, w_scr, sems)
            norm_ref[...] = jnp.transpose(w_scr[0, :, 4 * width :].astype(F32))[:8, :]

        x = x_ref[...]
        cos = cos_ref[...]
        sin = sin_ref[...]
        lane = lax.broadcasted_iota(jnp.int32, (tile, LANES), 1)
        same = lane % HD == seg_ref[...]
        key_extra = jnp.where(same, 1.0, 0.0)
        query_extra = jnp.where(same, 0.0, NEG)
        merged = dot_nn(x, w_scr[0, :, : 3 * width])
        for b in range(width // LANES):
            cols = slice(b * LANES, (b + 1) * LANES)
            q = merged[:, b * LANES : (b + 1) * LANES]
            k = merged[:, width + b * LANES : width + (b + 1) * LANES]
            v = merged[:, 2 * width + b * LANES : 2 * width + (b + 1) * LANES]
            q = (q * cos + half_swap(q) * sin) * (HD**-0.5)
            k = k * cos + half_swap(k) * sin
            for h in (2 * b, 2 * b + 1):
                q_ref[h] = head_lanes(q, h, query_extra).astype(BF16)
                k_ref[h] = head_lanes(k, h, key_extra).astype(BF16)
            v_ref[:, cols] = v.astype(BF16)
            vt_ref[cols, :] = jnp.transpose(v).astype(BF16)
            for j in range(tile // k_tile):
                kt_ref[j, cols, :] = jnp.transpose(k[j * k_tile : (j + 1) * k_tile, :]).astype(BF16)

    row_block = pl.BlockSpec((tile, width), lambda i, p, o: (true_tile(i, p), 0))
    head_block = pl.BlockSpec((H, tile, LANES), lambda i, p, o: (0, true_tile(i, p), 0))
    table_block = pl.BlockSpec((tile, LANES), lambda i, p, o: (true_tile(i, p), 0))
    return pl.pallas_call(
        body,
        grid_spec=pltpu.PrefetchScalarGridSpec(
            num_scalar_prefetch=2,
            grid=(seq // tile,),
            in_specs=[
                pl.BlockSpec((tile, width), lambda i, p, o: (i, 0)),
                table_block,
                table_block,
                pl.BlockSpec((tile, 1), lambda i, p, o: (true_tile(i, p), 0)),
            ]
            + held.in_specs,
            out_specs=[
                head_block,
                head_block,
                row_block,
                pl.BlockSpec((tile // k_tile, width, k_tile), lambda i, p, o: (true_tile(i, p), 0, 0)),
                pl.BlockSpec((width, tile), lambda i, p, o: (0, true_tile(i, p))),
                whole_block((8, width)),
            ],
            scratch_shapes=held.scratch,
        ),
        out_shape=[jax.ShapeDtypeStruct((H, seq, LANES), BF16)] * 2
        + [
            jax.ShapeDtypeStruct((seq, width), BF16),
            jax.ShapeDtypeStruct((seq // k_tile, width, k_tile), BF16),
            jax.ShapeDtypeStruct((width, seq), BF16),
            jax.ShapeDtypeStruct((8, width), F32),
        ],
        compiler_params=params(20),
        name="project",
    )(pos, offsets, x_rel, cosine, sine, seg_col, *held.flat)


GROUP = 4


def attend(x_own, q, k, vt, pieces, offsets, norms, pos):
    rows, width = x_own.shape
    seq = q.shape[1]
    group_cols = GROUP * HD
    n_steps = H // GROUP
    held = Pieces([pieces], width, slice(3 * width, 4 * width))
    n_in = len(held.flat)

    def body(pos_ref, offs_ref, x_ref, q_ref, k_ref, vt_ref, norm_ref, *rest):
        w_refs, rest = rest[:n_in], rest[n_in:]
        att_ref, lse_ref, n_ref, istd_ref, mid_ref, acc, lse, w_scr, sems = rest
        g = pl.program_id(0)

        @pl.when(g == 0)
        def _():
            held.start(0, w_refs, offs_ref, w_scr, sems)

        for j in range(GROUP):
            s = dot_nt(k_ref[j], q_ref[j])
            peak = jnp.max(s, axis=0, keepdims=True)
            e = jnp.exp(s - peak)
            total = jnp.sum(e, axis=0, keepdims=True)
            out = dot_nn(vt_ref[j * HD : (j + 1) * HD, :], e.astype(BF16))
            acc[g, j * HD : (j + 1) * HD, :] = out / total
            lse[g, j : j + 1, :] = peak + jnp.log(total)

        @pl.when(g == n_steps - 1)
        def _():
            held.wait(0, w_refs, offs_ref, w_scr, sems)
            for i in range(n_steps):
                lse_ref[i] = lse[i]
                att_ref[:, i * group_cols : (i + 1) * group_cols] = jnp.transpose(acc[i]).astype(BF16)
            first_sum = x_ref[...].astype(F32) + dot_nn(att_ref[...], w_scr[0])
            normed, inv_std = normalise(first_sum)
            n_ref[...] = normed
            istd_ref[...] = inv_std
            mid_ref[...] = (normed * norm_ref[0:1, :] + norm_ref[2:3, :]).astype(BF16)

    own = whole_block((rows, width))
    return pl.pallas_call(
        body,
        grid_spec=pltpu.PrefetchScalarGridSpec(
            num_scalar_prefetch=2,
            grid=(n_steps,),
            in_specs=[
                own,
                pl.BlockSpec((GROUP, rows, LANES), lambda g, p, o: (g, p[0], 0)),
                pl.BlockSpec((GROUP, seq, LANES), lambda g, p, o: (g, 0, 0)),
                pl.BlockSpec((group_cols, seq), lambda g, p, o: (g, 0)),
                whole_block((8, width)),
            ]
            + held.in_specs,
            out_specs=[own, whole_block((n_steps, 8, rows)), own, whole_block((rows, 1)), own],
            scratch_shapes=[
                pltpu.VMEM((n_steps, group_cols, rows), F32),
                pltpu.VMEM((n_steps, 8, rows), F32),
            ]
            + held.scratch,
        ),
        out_shape=[
            jax.ShapeDtypeStruct((rows, width), BF16),
            jax.ShapeDtypeStruct((n_steps, 8, rows), F32),
            jax.ShapeDtypeStruct((rows, width), F32),
            jax.ShapeDtypeStruct((rows, 1), F32),
            jax.ShapeDtypeStruct((rows, width), BF16),
        ],
        compiler_params=params(18),
        name="attend",
    )(pos, offsets, x_own, q, k, vt, norms, *held.flat)


def feed_forward(mid_own, mid_sib, slots, offsets, before, last):
    rows, width = mid_own.shape
    held = Pieces(slots, width)
    n_slots, cols = held.n_slots, held.cols.stop // 3
    n_in = len(held.flat)

    def body(offs_ref, own_ref, sib_ref, *rest):
        w_refs, rest = rest[:n_in], rest[n_in:]
        if before is not None:
            before_ref, rest = rest[0], rest[1:]
        if last:
            hid_ref, a_ref, b_ref, out_own, out_sib, acc, w_scr, sems = rest
        else:
            hid_ref, a_ref, b_ref, acc, w_scr, sems = rest
        s = pl.program_id(0)

        @pl.when(s == 0)
        def _():
            held.start_all(w_refs, offs_ref, w_scr, sems)
            acc[...] = jnp.zeros(acc.shape, F32) if before is None else before_ref[...]

        held.wait_for_step(s, w_refs, offs_ref, w_scr, sems)
        for i, x_ref in enumerate((own_ref, sib_ref)):
            part = slice(i * rows, (i + 1) * rows)
            both = dot_nn(x_ref[...], w_scr[s, :, : 2 * cols])
            gate, up = both[:, :cols], both[:, cols:]
            sig = 0.5 * jnp.tanh(0.5 * gate) + 0.5
            silu = gate * sig
            hidden = (silu * up).astype(BF16)
            hid_ref[0, part, :] = hidden
            a_ref[0, part, :] = (up * (sig + silu * (1.0 - sig))).astype(BF16)
            b_ref[0, part, :] = silu.astype(BF16)
            acc[part, :] += dot_nt(hidden, w_scr[s, :, 2 * cols :])

        if last:

            @pl.when(s == n_slots - 1)
            def _():
                out_own[...] = acc[:rows, :]
                out_sib[...] = acc[rows:, :].astype(BF16)

    full = whole_block((rows, width))
    both_block = whole_block((2 * rows, width))
    act = pl.BlockSpec((1, 2 * rows, cols), lambda i, *_: (i, 0, 0))
    act_shape = jax.ShapeDtypeStruct((n_slots, 2 * rows, cols), BF16)
    extra = [] if before is None else [before]
    if last:
        acc_specs = [full, full]
        acc_shapes = [jax.ShapeDtypeStruct((rows, width), F32), jax.ShapeDtypeStruct((rows, width), BF16)]
        acc_scratch = [pltpu.VMEM((2 * rows, width), F32)]
    else:
        acc_specs = [both_block]
        acc_shapes = [jax.ShapeDtypeStruct((2 * rows, width), F32)]
        acc_scratch = []
    return pl.pallas_call(
        body,
        grid_spec=pltpu.PrefetchScalarGridSpec(
            num_scalar_prefetch=1,
            grid=(n_slots,),
            in_specs=[full, full] + held.in_specs + [both_block] * len(extra),
            out_specs=[act] * 3 + acc_specs,
            scratch_shapes=acc_scratch + held.scratch,
        ),
        out_shape=[act_shape] * 3 + acc_shapes,
        compiler_params=params(18),
        name="feed_forward",
    )(offsets, mid_own, mid_sib, *held.flat, *extra)


def second_norm(normed1, part_own, part_sib, out_grad, norms):
    rows, width = normed1.shape
    tile = min(256, rows)

    def body(n_ref, own_ref, sib_ref, g_ref, norm_ref, out_ref, d_ref, dl_ref, ng_ref):
        middle = n_ref[...] * norm_ref[0:1, :] + norm_ref[2:3, :]
        second_sum = middle + (own_ref[...] + sib_ref[...].astype(F32))
        normed, inv_std = normalise(second_sum)
        out_ref[...] = (normed * norm_ref[1:2, :] + norm_ref[3:4, :]).astype(BF16)
        grad = g_ref[...].astype(F32)
        d = norm_back(normed, inv_std, norm_ref[1:2, :], grad)
        d_ref[...] = d
        dl_ref[...] = d.astype(BF16)

        @pl.when(pl.program_id(0) == 0)
        def _():
            ng_ref[...] = jnp.zeros(ng_ref.shape, F32)

        ng_ref[0:1, :] += jnp.sum(grad * normed, axis=0, keepdims=True)
        ng_ref[1:2, :] += jnp.sum(grad, axis=0, keepdims=True)

    block = pl.BlockSpec((tile, width), lambda i: (i, 0))
    return pl.pallas_call(
        body,
        grid=(rows // tile,),
        in_specs=[block] * 4 + [whole_block((8, width))],
        out_specs=[block] * 3 + [whole_block((8, width))],
        out_shape=[
            jax.ShapeDtypeStruct((rows, width), BF16),
            jax.ShapeDtypeStruct((rows, width), F32),
            jax.ShapeDtypeStruct((rows, width), BF16),
            jax.ShapeDtypeStruct((8, width), F32),
        ],
        compiler_params=params(10),
        name="second_norm",
    )(normed1, part_own, part_sib, out_grad, norms)


def hidden_back(dffs, factors, slots, offsets):
    rows, width = dffs[0].shape
    held = Pieces(slots, width)
    n_slots, cols = held.n_slots, held.cols.stop // 3
    n_in = len(held.flat)
    per_call = factors[0][0].shape[0]
    n_fac = len(factors)

    def body(offs_ref, do_ref, ds_ref, *rest):
        fac_refs, rest = rest[: 2 * n_fac], rest[2 * n_fac :]
        w_refs, rest = rest[:n_in], rest[n_in:]
        d_ref, out_own, out_sib, acc, w_scr, sems = rest
        s = pl.program_id(0)

        @pl.when(s == 0)
        def _():
            held.start_all(w_refs, offs_ref, w_scr, sems)
            acc[...] = jnp.zeros(acc.shape, F32)

        held.wait_for_step(s, w_refs, offs_ref, w_scr, sems)

        def work(a_ref, b_ref):
            for i, x_ref in enumerate((do_ref, ds_ref)):
                part = slice(i * rows, (i + 1) * rows)
                dh = dot_nn(x_ref[...], w_scr[s, :, 2 * cols :])
                d_ref[0, part, :cols] = (dh * a_ref[0, part, :].astype(F32)).astype(BF16)
                d_ref[0, part, cols:] = (dh * b_ref[0, part, :].astype(F32)).astype(BF16)
                acc[part, :] += dot_nt(d_ref[0, part, :], w_scr[s, :, : 2 * cols])

        for f in range(n_fac):

            @pl.when(s // per_call == f)
            def _(f=f):
                work(fac_refs[2 * f], fac_refs[2 * f + 1])

        @pl.when(s == n_slots - 1)
        def _():
            out_own[...] = acc[:rows, :]
            out_sib[...] = acc[rows:, :].astype(BF16)

    full = whole_block((rows, width))

    def fac_spec(f):
        return pl.BlockSpec(
            (1, 2 * rows, cols), lambda i, *_: (jnp.clip(i - f * per_call, 0, per_call - 1), 0, 0)
        )

    return pl.pallas_call(
        body,
        grid_spec=pltpu.PrefetchScalarGridSpec(
            num_scalar_prefetch=1,
            grid=(n_slots,),
            in_specs=[full, full]
            + [fac_spec(f) for f in range(n_fac) for _ in range(2)]
            + held.in_specs,
            out_specs=[pl.BlockSpec((1, 2 * rows, 2 * cols), lambda i, *_: (i, 0, 0)), full, full],
            scratch_shapes=[pltpu.VMEM((2 * rows, width), F32)] + held.scratch,
        ),
        out_shape=[
            jax.ShapeDtypeStruct((n_slots, 2 * rows, 2 * cols), BF16),
            jax.ShapeDtypeStruct((rows, width), F32),
            jax.ShapeDtypeStruct((rows, width), BF16),
        ],
        compiler_params=params(22),
        name="hidden_back",
    )(offsets, *dffs, *[x for pair in factors for x in pair], *held.flat)


def store_groups(groups, group_refs, offs_ref, n_blocks, block_rows, source):
    for (picks, dtype), ref in zip(groups, group_refs):
        for j, p in enumerate(picks):
            for b in range(n_blocks):
                start = pl.multiple_of(offs_ref[p * n_blocks + b], 8)
                ref[j, b] = source[pl.ds(start, block_rows), :].astype(dtype)


def ffn_grads(first, mids, dffs, hidden, d_both, offsets, groups, n_blocks, block_rows):
    rows, width = mids[0].shape
    n_slots, _, cols = hidden.shape
    shapes = [[(len(picks), n_blocks, block_rows, 3 * cols) for picks, _ in gs] for gs in groups]
    n_out = [len(gs) for gs in groups]

    def body(offs_ref, mo, ms, do, ds, hid_ref, d_ref, *rest):
        outs, rest = rest[: sum(n_out)], rest[sum(n_out) :]
        stages, (mid_t, dff_t, g_scr, sems) = rest[: sum(n_out)], rest[sum(n_out) :]
        s = pl.program_id(0)

        @pl.when(s == 0)
        def _():
            for i, (m_ref, x_ref) in enumerate(((mo, do), (ms, ds))):
                part = slice(i * rows, (i + 1) * rows)
                mid_t[:, part] = jnp.transpose(m_ref[...])
                dff_t[:, part] = jnp.transpose(x_ref[...])

        g_scr[:, : 2 * cols] = dot_nn(mid_t[...], d_ref[0])
        g_scr[:, 2 * cols :] = dot_nn(dff_t[...], hid_ref[0])
        for j in range(n_slots):
            at = sum(n_out[:j])

            @pl.when(s == j)
            def _(j=j, at=at):
                store_groups(groups[j], stages[at : at + n_out[j]], offs_ref, n_blocks, block_rows, g_scr)
                for o in range(at, at + n_out[j]):
                    pltpu.make_async_copy(stages[o], outs[o], sems.at[o]).start()

        @pl.when(s == n_slots - 1)
        def _():
            for o in range(sum(n_out)):
                pltpu.make_async_copy(stages[o], outs[o], sems.at[o]).wait()

    flat = [(shape, dtype) for ss, gs in zip(shapes, groups) for shape, (_, dtype) in zip(ss, gs)]
    full = whole_block((rows, width))
    results = pl.pallas_call(
        body,
        grid_spec=pltpu.PrefetchScalarGridSpec(
            num_scalar_prefetch=1,
            grid=(n_slots,),
            in_specs=[full] * 4
            + [
                pl.BlockSpec((1, 2 * rows, cols), lambda i, *_: (i, 0, 0)),
                pl.BlockSpec((1, 2 * rows, 2 * cols), lambda i, *_: (first + i, 0, 0)),
            ],
            out_specs=[pl.BlockSpec(memory_space=pl.ANY)] * len(flat),
            scratch_shapes=[pltpu.VMEM(shape, dtype) for shape, dtype in flat]
            + [
                pltpu.VMEM((width, 2 * rows), BF16),
                pltpu.VMEM((width, 2 * rows), BF16),
                pltpu.VMEM((width, 3 * cols), F32),
                pltpu.SemaphoreType.DMA((len(flat),)),
            ],
        ),
        out_shape=[jax.ShapeDtypeStruct(shape, dtype) for shape, dtype in flat],
        compiler_params=params(22),
        name="ffn_grads",
    )(offsets, *mids, *dffs, hidden, d_both)
    return [results[sum(n_out[:j]) : sum(n_out[: j + 1])] for j in range(n_slots)]


def first_norm_back(normed1, inv_std1, d_second, d_mid, d_mid_sib, norms):
    rows, width = normed1.shape
    tile = min(256, rows)

    def body(n_ref, istd_ref, d2_ref, dm_ref, ds_ref, norm_ref, d_ref, dl_ref, ng_ref):
        grad = d2_ref[...] + dm_ref[...] + ds_ref[...].astype(F32)
        normed = n_ref[...]
        d = norm_back(normed, istd_ref[...], norm_ref[0:1, :], grad)
        d_ref[...] = d
        dl_ref[...] = d.astype(BF16)

        @pl.when(pl.program_id(0) == 0)
        def _():
            ng_ref[...] = jnp.zeros(ng_ref.shape, F32)

        ng_ref[0:1, :] += jnp.sum(grad * normed, axis=0, keepdims=True)
        ng_ref[1:2, :] += jnp.sum(grad, axis=0, keepdims=True)

    block = pl.BlockSpec((tile, width), lambda i: (i, 0))
    column = pl.BlockSpec((tile, 1), lambda i: (i, 0))
    return pl.pallas_call(
        body,
        grid=(rows // tile,),
        in_specs=[block, column, block, block, block, whole_block((8, width))],
        out_specs=[block] * 2 + [whole_block((8, width))],
        out_shape=[
            jax.ShapeDtypeStruct((rows, width), F32),
            jax.ShapeDtypeStruct((rows, width), BF16),
            jax.ShapeDtypeStruct((8, width), F32),
        ],
        compiler_params=params(8),
        name="first_norm_back",
    )(normed1, inv_std1, d_second, d_mid, d_mid_sib, norms)


def out_grads(attended, d_first_low, norm1, norm2):
    rows, width = attended.shape

    def body(att_ref, dl_ref, n1_ref, n2_ref, out_ref):
        out_ref[:, :width] = dot_tn(att_ref[...], dl_ref[...]).astype(BF16)
        stacked = jnp.concatenate(
            [n1_ref[0:1, :], n2_ref[0:1, :], n1_ref[1:2, :], n2_ref[1:2, :],
             jnp.zeros((PAD - 4, width), F32)], axis=0)
        out_ref[:, width:] = jnp.transpose(stacked).astype(BF16)

    operands = (attended, d_first_low, norm1, norm2)
    return pl.pallas_call(
        body,
        grid=(1,),
        in_specs=[whole_block(o.shape) for o in operands],
        out_specs=whole_block((width, width + PAD)),
        out_shape=jax.ShapeDtypeStruct((width, width + PAD), BF16),
        compiler_params=params(10),
        name="out_grads",
    )(*operands)


def unrotated(g, cos, sin):
    g = g.astype(BF16).astype(F32)
    return (g * cos - half_swap(g) * sin).astype(BF16)


def prepare_heads(d_att, att, dom, delta, at):
    n = d_att.shape[0]
    flipped = jnp.transpose(d_att.astype(F32) * att.astype(F32))
    for j in range(GROUP):
        delta[j : j + 1, at : at + n] = jnp.sum(flipped[j * HD : (j + 1) * HD, :], axis=0, keepdims=True)
        block = d_att[:, j // 2 * LANES : j // 2 * LANES + LANES].astype(F32)
        dom[j, at : at + n, :] = head_lanes(block, j, 0.0).astype(BF16)


def pair_up(even, odd):
    return head_lanes(even, 0, odd)


def attend_back_own(d_first, attended, lse, q, k, v, kt, key_from, key_to, cosine, sine, pieces, offsets, pos,
                    k_tile):
    rows, width = d_first.shape
    seq = q.shape[1]
    n_own = rows // k_tile
    group_cols = GROUP * HD
    held = Pieces([pieces], width, slice(3 * width, 4 * width))
    n_in = len(held.flat)
    n_q = key_from.shape[0] * rows // seq

    def body(pos_ref, offs_ref, from_ref, to_ref, d_ref, att_ref, lse_ref, q_ref, k_ref, v_ref, kt_ref,
             cos_ref, sin_ref, *rest):
        w_refs, rest = rest[:n_in], rest[n_in:]
        dq_ref, dk_ref, dv_ref, dom, delta, dq, w_scr, sems = rest
        g = pl.program_id(0)

        @pl.when(g == 0)
        def _():
            held.start(0, w_refs, offs_ref, w_scr, sems)
            held.wait(0, w_refs, offs_ref, w_scr, sems)

        w_rows = w_scr[0, pl.ds(pl.multiple_of(g * group_cols, group_cols), group_cols), :]
        d_att = dot_nt(d_ref[...], w_rows).astype(BF16)
        prepare_heads(d_att, att_ref[...], dom, delta, 0)
        own_low = pos_ref[0] * n_own

        def weights_of(j, at, n, some):
            cols = slice(j // 2 * LANES, j // 2 * LANES + LANES)
            s = dot_nt(k_ref[j, pl.ds(at, n), :], q_ref[j, some, :])
            p = jnp.exp(s - lse_ref[0, j : j + 1, some])
            dp = dot_nt(v_ref[pl.ds(at, n), cols], dom[j, some, :])
            return p, (p * (dp - delta[j : j + 1, some])).astype(BF16)

        base = pl.multiple_of(pos_ref[0] * rows, rows)
        for b in range(GROUP // 2):
            dks, dvs = [], []
            for j in (2 * b, 2 * b + 1):
                p, ds = weights_of(j, base, rows, slice(0, rows))
                dvs.append(dot_nn(p.astype(BF16), dom[j]))
                dks.append(dot_nn(ds, q_ref[j]))
                heads = slice(j * HD, (j + 1) * HD)
                total = None
                for t in range(n_own):
                    part = dot_nn(kt_ref[own_low + t, heads, :], ds[t * k_tile : (t + 1) * k_tile, :])
                    total = part if total is None else total + part
                dq[heads, :] = total
            cols = slice(b * LANES, (b + 1) * LANES)
            dk_ref[:, cols] = pair_up(*dks)
            dv_ref[:, cols] = dvs[0] + dvs[1]

        first_tile = pos_ref[0] * n_q
        for i in range(n_q):
            some = slice(i * rows // n_q, (i + 1) * rows // n_q)
            low = from_ref[first_tile + i]
            n_left = jnp.maximum(own_low - low, 0)
            n_right = jnp.maximum(to_ref[first_tile + i] - own_low - n_own, 0)

            def outside(t, carry, some=some, low=low, n_left=n_left):
                tile = jnp.where(t < n_left, low + t, own_low + n_own + t - n_left)
                at = pl.multiple_of(tile * k_tile, k_tile)
                for j in range(GROUP):
                    heads = slice(j * HD, (j + 1) * HD)
                    _, ds = weights_of(j, at, k_tile, some)
                    dq[heads, some] += dot_nn(kt_ref[tile, heads, :], ds)
                return carry

            lax.fori_loop(0, n_left + n_right, outside, 0)

        turned = jnp.transpose(dq[...]) * (HD**-0.5)
        for b in range(GROUP // 2):
            cols = slice(b * LANES, (b + 1) * LANES)
            dq_ref[:, cols] = unrotated(turned[:, cols], cos_ref[...], sin_ref[...])

    def col_block(n):
        return pl.BlockSpec((n, group_cols), lambda g, *_: (0, g))

    table = pl.BlockSpec((rows, LANES), lambda g, p, *_: (p[0], 0))
    sum_shape = jax.ShapeDtypeStruct((rows, width), F32)
    return pl.pallas_call(
        body,
        grid_spec=pltpu.PrefetchScalarGridSpec(
            num_scalar_prefetch=4,
            grid=(H // GROUP,),
            in_specs=[
                whole_block((rows, width)),
                col_block(rows),
                pl.BlockSpec((1, 8, rows), lambda g, *_: (g, 0, 0)),
                pl.BlockSpec((GROUP, rows, LANES), lambda g, p, *_: (g, p[0], 0)),
                pl.BlockSpec((GROUP, seq, LANES), lambda g, *_: (g, 0, 0)),
                col_block(seq),
                pl.BlockSpec((seq // k_tile, group_cols, k_tile), lambda g, *_: (0, g, 0)),
                table,
                table,
            ]
            + held.in_specs,
            out_specs=[col_block(rows)] * 3,
            scratch_shapes=[
                pltpu.VMEM((GROUP, rows, LANES), BF16),
                pltpu.VMEM((8, rows), F32),
                pltpu.VMEM((group_cols, rows), F32),
            ]
            + held.scratch,
        ),
        out_shape=[jax.ShapeDtypeStruct((rows, width), BF16), sum_shape, sum_shape],
        compiler_params=params(20),
        name="attend_back_own",
    )(pos, offsets, key_from, key_to, d_first, attended, lse, q, k, v, kt, cosine, sine, *held.flat)


def attend_back_others(d_others, att_others, lse_others, sums, q, k, v, key_from, key_to, cosine, sine, pieces,
                       offsets, pos, q_tile, k_tile):
    rows, width = sums[0].shape
    seq = q.shape[1]
    n_q = rows // q_tile
    n_own = rows // k_tile
    n_tiles = d_others.shape[0] // q_tile
    group_cols = GROUP * HD
    held = Pieces([pieces], width, slice(3 * width, 4 * width))
    n_in = len(held.flat)

    def body(pos_ref, offs_ref, from_ref, to_ref, d_ref, att_ref, lse_ref, q_ref, k_ref, v_ref, dk_in, dv_in,
             cos_ref, sin_ref, *rest):
        w_refs, rest = rest[:n_in], rest[n_in:]
        dk_ref, dv_ref, dom, delta, dk, dv, w_scr, sems = rest
        g = pl.program_id(0)

        @pl.when(g == 0)
        def _():
            held.start(0, w_refs, offs_ref, w_scr, sems)
            held.wait(0, w_refs, offs_ref, w_scr, sems)

        dk[...] = dk_in[...]
        dv[...] = dv_in[...]
        own_low = pos_ref[0] * n_own

        for i in range(n_tiles):
            true_tile = (pos_ref[0] ^ (1 + i // n_q)) * n_q + i % n_q
            low = jnp.maximum(from_ref[true_tile], own_low)
            high = jnp.minimum(to_ref[true_tile], own_low + n_own)
            here = slice(i * q_tile, (i + 1) * q_tile)

            @pl.when(high > low)
            def _(i=i, true_tile=true_tile, low=low, high=high, here=here):
                w_rows = w_scr[0, pl.ds(pl.multiple_of(g * group_cols, group_cols), group_cols), :]
                d_att = dot_nt(d_ref[here, :], w_rows).astype(BF16)
                prepare_heads(d_att, att_ref[here, :], dom, delta, 0)
                q_at = pl.multiple_of(true_tile * q_tile, q_tile)

                def one(tile, carry):
                    at = pl.ds(pl.multiple_of((tile - own_low) * k_tile, k_tile), k_tile)
                    for b in range(GROUP // 2):
                        cols = slice(b * LANES, (b + 1) * LANES)
                        dks, dvs = [], []
                        for j in (2 * b, 2 * b + 1):
                            q_head = q_ref[j, pl.ds(q_at, q_tile), :]
                            s = dot_nt(k_ref[j, at, :], q_head)
                            p = jnp.exp(s - lse_ref[0, j : j + 1, here])
                            dp = dot_nt(v_ref[at, cols], dom[j])
                            ds = (p * (dp - delta[j : j + 1, :])).astype(BF16)
                            dvs.append(dot_nn(p.astype(BF16), dom[j]))
                            dks.append(dot_nn(ds, q_head))
                        dk[at, cols] += pair_up(*dks)
                        dv[at, cols] += dvs[0] + dvs[1]
                    return carry

                lax.fori_loop(low, high, one, 0)

        for b in range(GROUP // 2):
            cols = slice(b * LANES, (b + 1) * LANES)
            dk_ref[:, cols] = unrotated(dk[:, cols], cos_ref[...], sin_ref[...])
        dv_ref[...] = dv[...].astype(BF16)

    def col_block(n):
        return pl.BlockSpec((n, group_cols), lambda g, *_: (0, g))

    table = pl.BlockSpec((rows, LANES), lambda g, p, *_: (p[0], 0))
    return pl.pallas_call(
        body,
        grid_spec=pltpu.PrefetchScalarGridSpec(
            num_scalar_prefetch=4,
            grid=(H // GROUP,),
            in_specs=[
                whole_block(d_others.shape),
                col_block(d_others.shape[0]),
                pl.BlockSpec((1, 8, d_others.shape[0]), lambda g, *_: (g, 0, 0)),
                pl.BlockSpec((GROUP, seq, LANES), lambda g, *_: (g, 0, 0)),
                pl.BlockSpec((GROUP, rows, LANES), lambda g, p, *_: (g, p[0], 0)),
                pl.BlockSpec((rows, group_cols), lambda g, p, *_: (p[0], g)),
                col_block(rows),
                col_block(rows),
                table,
                table,
            ]
            + held.in_specs,
            out_specs=[col_block(rows)] * 2,
            scratch_shapes=[
                pltpu.VMEM((GROUP, q_tile, LANES), BF16),
                pltpu.VMEM((8, q_tile), F32),
                pltpu.VMEM((rows, group_cols), F32),
                pltpu.VMEM((rows, group_cols), F32),
            ]
            + held.scratch,
        ),
        out_shape=[jax.ShapeDtypeStruct((rows, width), BF16)] * 2,
        compiler_params=params(18),
        name="attend_back_others",
    )(pos, offsets, key_from, key_to, d_others, att_others, lse_others, q, k, v, *sums, cosine, sine,
      *held.flat)


def qkv_grads(x_own, merged, out_part, offsets, groups, n_blocks, block_rows):
    rows, width = x_own.shape
    wide = 3 * width + out_part.shape[1]

    def body(offs_ref, x_ref, dq_ref, dk_ref, dv_ref, out_ref, *rest):
        group_refs, g_scr = rest[:-1], rest[-1]
        x_t = jnp.transpose(x_ref[...])
        for j, ref in enumerate((dq_ref, dk_ref, dv_ref)):
            g_scr[:, j * width : (j + 1) * width] = dot_nn(x_t, ref[...])
        g_scr[:, 3 * width :] = out_ref[...].astype(F32)
        store_groups(groups, group_refs, offs_ref, n_blocks, block_rows, g_scr)

    group_shapes = [(len(picks), n_blocks, block_rows, wide) for picks, _ in groups]
    return pl.pallas_call(
        body,
        grid_spec=pltpu.PrefetchScalarGridSpec(
            num_scalar_prefetch=1,
            grid=(1,),
            in_specs=[whole_block((rows, width))] * 4 + [whole_block(out_part.shape)],
            out_specs=[whole_block(s) for s in group_shapes],
            scratch_shapes=[pltpu.VMEM((width, wide), F32)],
        ),
        out_shape=[jax.ShapeDtypeStruct(s, dtype) for s, (_, dtype) in zip(group_shapes, groups)],
        compiler_params=params(20),
        name="qkv_grads",
    )(offsets, x_own, *merged, out_part)


def input_grads(merged, d_first, pieces, offsets):
    rows, width = d_first.shape
    tile = min(256, rows)
    held = Pieces([pieces], width, slice(0, 3 * width))
    n_in = len(held.flat)

    def body(offs_ref, dq_ref, dk_ref, dv_ref, df_ref, *rest):
        w_refs, (out_ref, w_scr, sems) = rest[:n_in], rest[n_in:]

        @pl.when(pl.program_id(0) == 0)
        def _():
            held.start(0, w_refs, offs_ref, w_scr, sems)
            held.wait(0, w_refs, offs_ref, w_scr, sems)

        total = df_ref[...]
        for j, ref in enumerate((dq_ref, dk_ref, dv_ref)):
            total = total + dot_nt(ref[...], w_scr[0, :, j * width : (j + 1) * width])
        out_ref[...] = total

    block = pl.BlockSpec((tile, width), lambda i, o: (i, 0))
    return pl.pallas_call(
        body,
        grid_spec=pltpu.PrefetchScalarGridSpec(
            num_scalar_prefetch=1,
            grid=(rows // tile,),
            in_specs=[block] * 4 + held.in_specs,
            out_specs=block,
            scratch_shapes=held.scratch,
        ),
        out_shape=jax.ShapeDtypeStruct((rows, width), F32),
        compiler_params=params(12),
        name="input_grads",
    )(offsets, *map(in_hbm, merged), in_hbm(d_first), *held.flat)


def combine(kept, got):
    _, n_blocks, block_rows, wide = kept.shape

    def body(kept_ref, got_ref, own_ref, on_ref):
        own_ref[...] = kept_ref[0].astype(F32) + got_ref[0].astype(F32)
        on_ref[...] = (kept_ref[1].astype(F32) + got_ref[1].astype(F32)).astype(BF16)

    two = pl.BlockSpec((2, 1, block_rows, wide), lambda i: (0, i, 0, 0))
    one = pl.BlockSpec((1, block_rows, wide), lambda i: (i, 0, 0))
    shape = (n_blocks, block_rows, wide)
    return pl.pallas_call(
        body,
        grid=(n_blocks,),
        in_specs=[two, two],
        out_specs=[one, one],
        out_shape=[jax.ShapeDtypeStruct(shape, F32), jax.ShapeDtypeStruct(shape, BF16)],
        compiler_params=params(6),
        name="combine",
    )(kept, got)


def make_per_device(ndp, nt):
    plane = ndp // 2

    def move(value, chip=0, core=0, flip=0):
        pairs = []
        for d in range(ndp):
            for t in range(nt):
                to_d = ((d // 2) ^ chip) * 2 + ((d % 2) ^ core)
                pairs.append((d * nt + t, to_d * nt + (t ^ flip)))
        return lax.ppermute(value, AXES, pairs)

    def after(value, *others):
        return lax.optimization_barrier((value, *others))[0]

    def per_device(inputs, segment_ids, qkv_weight, out_weight, norm_gains, norm_biases,
                   gate_weight, up_weight, down_weight, out_grad):
        rows, width = inputs.shape
        seq = segment_ids.shape[1]
        n_row = seq // rows
        q_tile = min(256, rows)
        k_tile = min(256, rows)
        shard = qkv_weight.shape[0]
        ffn_rows, ffn_cols = gate_weight.shape
        half = ffn_cols // 2
        fast = plane == 4 and nt == 4 and n_row == 2

        d_index = lax.axis_index("dp")
        core = d_index % 2
        chip = d_index // 2
        t_index = lax.axis_index("tensor")
        pos = (t_index % n_row).astype(jnp.int32)
        block_at = [((chip ^ dxy) * 2 + (core ^ other)) for dxy in range(4) for other in range(2)]

        packed = jnp.concatenate(
            [qkv_weight, out_weight, norm_gains.T, norm_biases.T,
             jnp.zeros((shard, PAD - 4), BF16)], axis=1)
        seg = lax.dynamic_index_in_dim(segment_ids, t_index // n_row, 0, keepdims=False)
        doc_from = jnp.sum((seg[None, :] < seg[:, None]).astype(jnp.int32), axis=1)
        doc_to = jnp.sum((seg[None, :] <= seg[:, None]).astype(jnp.int32), axis=1)
        place = (jnp.arange(seq, dtype=jnp.int32) - doc_from).astype(F32)
        lane = np.arange(LANES)
        frequency = rope_base ** (-jnp.asarray(lane % (HD // 2), F32) * 2.0 / HD)
        angles = place[:, None] * frequency[None, :]
        cosine = jnp.cos(angles)
        sine = jnp.sin(angles) * jnp.asarray(np.where(lane % HD < HD // 2, -1.0, 1.0), F32)[None, :]
        key_from = doc_from[::q_tile] // k_tile
        key_to = (doc_to[q_tile - 1 :: q_tile] + k_tile - 1) // k_tile
        seg_col = seg[:, None]
        seg_row = seg.reshape(seq // q_tile, 1, q_tile)
        pos_arr = pos[None]

        ffn = (gate_weight, up_weight, down_weight.T)
        mine, given = [
            jnp.concatenate([lax.dynamic_slice_in_dim(w, c * half, half, 1) for w in ffn], axis=1)
            for c in (core, 1 - core)
        ]
        if fast:
            pair = jnp.stack([mine, move(given, core=1)])
            x_others = [move(inputs, flip=1)]
            second = move(pair, flip=2)
            by_flip = [packed] + [move(packed, flip=e) for e in range(1, nt)]
            near = jnp.concatenate(
                [lax.select_n(t_index, *[by_flip[j ^ t] for t in range(nt)]) for j in range(nt)], axis=0)[None]
            far = [move(near, chip=dxy) for dxy in range(1, 4)]
            last_two = move(jnp.stack([pair, second]), flip=1)
            plane_rows = after(jnp.concatenate([near] + far, axis=0), second, *x_others,
                               cosine, sine, key_from, key_to, seg_col)
            plane_sib = move(plane_rows, core=1)

            def spread(one):
                return one, move(one, chip=1), move(one, chip=2)

            def spread_on(sides, index, along_x, *others):
                passed = after(sides[1 if along_x else 2][index], *others)
                across = move(passed, chip=2 if along_x else 1)
                return [(side, index) for side in sides] + [(across[None], 0)]

            side_0 = spread(pair[None])
            side_1 = spread(after(second, *far)[None])
            x_rel = jnp.concatenate([inputs] + x_others, axis=0)
            w_pieces = [(plane_rows[None], 0), (plane_sib[None], 0)]
            w_offsets = jnp.stack(
                [((chip ^ dxy) * 2 + (core ^ other)) * (nt * shard) for other in range(2) for dxy in range(4)]
            ).astype(jnp.int32)
            f_offsets = jnp.stack([b * ffn_rows for b in block_at]).astype(jnp.int32)
            n_blocks, block_rows = 2, ffn_rows
        else:
            x_others = [move(inputs, flip=e) for e in range(1, n_row)]
            x_rel = jnp.concatenate([inputs] + x_others, axis=0)
            w_pieces = [(lax.all_gather(packed, AXES, axis=0, tiled=True)[None, None], 0)]
            w_offsets = jnp.zeros((1,), jnp.int32)
            full = lax.all_gather(mine, "dp", axis=0, tiled=True).reshape(width, 3, half)
            full = lax.all_gather(full, "tensor", axis=2, tiled=True)
            slots = [[(full.reshape(1, 1, width, 3 * half * nt), 0)]]
            f_offsets = jnp.zeros((1,), jnp.int32)
            n_blocks, block_rows = 1, width

        q, k, v, kt, vt, norms = project(
            x_rel, w_pieces, w_offsets, cosine, sine, seg_col, pos_arr, n_row, k_tile)
        if fast:
            q = after(q, *side_0[1:], *side_1[1:])
            slots = [spread_on(side_0, 0, True, q), spread_on(side_1, 0, False, q)]
            side_2 = spread(after(last_two, q))
        attended, lse, normed1, inv_std1, mid = attend(
            inputs, q, k, vt, w_pieces, w_offsets, norms, pos_arr)
        if fast:
            slots += [spread_on(side_2, 0, True, mid), spread_on(side_2, 1, False, mid)]
        mid_sib = move(mid, core=1)

        calls = [slots[:2], slots[2:]] if fast else [slots]
        acts, partial = [], None
        for j, some in enumerate(calls):
            hid, fac_a, fac_b, *partial = feed_forward(
                mid, mid_sib, some, f_offsets, partial[0] if j else None, j == len(calls) - 1)
            acts.append((hid, fac_a, fac_b))
        part_own, part_sib = partial
        att_others = [move(attended, flip=e) for e in range(1, n_row)]
        lse_others = [move(lse, flip=e) for e in range(1, n_row)]
        part_sib = move(after(part_sib, *att_others, *lse_others), core=1)
        outputs, d_second, d_ffn, norm2 = second_norm(normed1, part_own, part_sib, out_grad, norms)
        d_ffn_sib = move(d_ffn, core=1)
        d_both, d_mid, d_mid_give = hidden_back(
            (d_ffn, d_ffn_sib), [a[1:] for a in acts], slots, f_offsets)
        d_mid_sib = move(d_mid_give, core=1)

        def groups_of(s):
            if not fast:
                return [((0,), BF16)]
            if s % 2 == 0:
                return [((2, 3), BF16), ((0, 1), BF16)]
            return [((1, 3), BF16), ((0, 2), BF16)]

        def weight_grads(j, d_both):
            first = sum(len(c) for c in calls[:j])
            return ffn_grads(
                first, (mid, mid_sib), (d_ffn, d_ffn_sib), acts[j][0], d_both, f_offsets,
                [groups_of(first + i) for i in range(len(calls[j]))], n_blocks, block_rows)

        d_first, d_first_low, norm1 = first_norm_back(
            normed1, inv_std1, d_second, d_mid, d_mid_sib, norms)
        d_others = [move(d_first_low, flip=e) for e in range(1, n_row)]
        d_both = after(d_both, d_first_low)
        if fast:
            reduced = {2 + i: r for i, r in enumerate(weight_grads(1, d_both))}
            reduced.update(enumerate(weight_grads(0, d_both)))
        else:
            reduced = dict(enumerate(weight_grads(0, d_both)))

        def turn(s):
            return (2, 1) if s % 2 == 0 else (1, 2)

        arrived, owned = {}, {}
        if fast:
            arrived = {s: move(reduced[s][0], chip=turn(s)[0]) for s in range(nt)}

        def combine_on(s):
            own, on = combine(reduced[s][1], arrived[s])
            owned[s] = (own, move(on, chip=turn(s)[1]))

        def owned_sum(s, *others):
            own, on = owned[s]
            return own + after(on, *others).astype(F32)

        dq, *sums = attend_back_own(
            after(d_first_low, *[r[-1] for r in reduced.values()]), attended, lse, q, k, v, kt, key_from, key_to,
            cosine, sine, w_pieces, w_offsets, pos_arr, k_tile)
        if fast:
            arrived[2], arrived[3] = after(arrived[2], dq), after(arrived[3], dq)
            combine_on(2)
            combine_on(3)
            sums[0] = after(sums[0], owned[2][0], owned[3][0])
        dk, dv = attend_back_others(
            jnp.concatenate(d_others, axis=0), jnp.concatenate(att_others, axis=0),
            jnp.concatenate(lse_others, axis=2), sums, q, k, v, key_from, key_to, cosine, sine,
            w_pieces, w_offsets, pos_arr, q_tile, k_tile)
        out_part = out_grads(attended, d_first_low, norm1, norm2)
        if fast:
            arrived[0], arrived[1] = after(arrived[0], dk), after(arrived[1], dk)
            combine_on(0)
            combine_on(1)
            dv = after(dv, owned[0][0], owned[1][0], owned[2][1], owned[3][1])
        merged = (dq, dk, dv)

        if fast:
            q_groups = [((1, 3, 5, 7), BF16), ((0, 2, 4, 6), BF16)]
            q_offsets = jnp.stack([b * (nt * shard) for b in block_at]).astype(jnp.int32)
            q_rows = nt * shard
        else:
            q_groups = [((0,), F32)]
            q_offsets = jnp.zeros((1,), jnp.int32)
            q_rows = width
        q_parts = qkv_grads(inputs, merged, out_part, q_offsets, q_groups, 1, q_rows)
        if fast:
            leaving = jnp.stack([owned_sum(2, q_parts[0]), owned_sum(3, q_parts[0])]).astype(BF16)
            back = move(leaving, flip=1)
            d_first = after(d_first, leaving)
        inputs_grad = input_grads(merged, d_first, w_pieces, w_offsets)

        if fast:
            q_other = after(move(q_parts[0], core=1), inputs_grad, leaving, owned[0][1], owned[1][1])
            q_sum = q_parts[1][:, 0].astype(F32) + q_other[:, 0].astype(F32)
            leaving = owned_sum(1, q_sum) + back[1].astype(F32)
            last_back = move(leaving.astype(BF16), flip=2)
            q_own = q_sum[0]
            for dxy in range(1, 4):
                q_own = q_own + move(q_sum[dxy].astype(BF16), chip=dxy).astype(F32)
            total = owned_sum(0, q_sum) + back[0].astype(F32) + after(last_back, q_own).astype(F32)
            packed_grad = None
            for e in range(nt):
                piece = lax.dynamic_slice_in_dim(q_own, (t_index ^ e) * shard, shard, 0)
                if e:
                    piece = move(piece.astype(BF16), flip=e).astype(F32)
                packed_grad = piece if packed_grad is None else packed_grad + piece
            other = move(total[1], core=1)
            mine = total[0]
            grads = []
            for m in range(3):
                part = slice(m * half, (m + 1) * half)
                grads.append(jnp.where(
                    core == 0,
                    jnp.concatenate([mine[:, part], other[:, part]], axis=1),
                    jnp.concatenate([other[:, part], mine[:, part]], axis=1)))
        else:
            summed = lax.psum_scatter(
                reduced[0][0][0, 0].reshape(width, 3, half * nt), "tensor", scatter_dimension=2, tiled=True)
            spread = jnp.zeros((width, 3, 2 * half), BF16)
            spread = lax.dynamic_update_slice_in_dim(spread, summed.astype(BF16), core * half, 2)
            spread = lax.psum_scatter(spread, "dp", scatter_dimension=0, tiled=True).astype(F32)
            grads = [spread[:, m] for m in range(3)]
            packed_grad = lax.psum_scatter(q_parts[0][0, 0], AXES, scatter_dimension=0, tiled=True)

        return (
            outputs,
            inputs_grad,
            packed_grad[:, : 3 * width],
            packed_grad[:, 3 * width : 4 * width],
            packed_grad[:, 4 * width : 4 * width + 2].T,
            packed_grad[:, 4 * width + 2 : 4 * width + 4].T,
            grads[0],
            grads[1],
            grads[2].T,
        )

    return per_device


def solution(mesh):
    tokens = P(AXES, None)
    both = P("dp", "tensor")
    return jax.shard_map(
        make_per_device(mesh.shape["dp"], mesh.shape["tensor"]),
        mesh=mesh,
        in_specs=(tokens, P("dp", None), tokens, tokens, P(None, AXES), P(None, AXES),
                  both, both, P("tensor", "dp"), tokens),
        out_specs=(tokens, tokens, tokens, tokens, P(None, AXES), P(None, AXES),
                   both, both, P("tensor", "dp")),
        check_vma=False,
    )
```

```python
import jax
import jax.numpy as jnp
import numpy as np
from jax import lax
from jax.experimental import pallas as pl
from jax.experimental.pallas import tpu as pltpu
from jax.sharding import PartitionSpec as P

H = 12
HD = 64
LANES = 128
PAD = 128
NEG = -1e30

rope_base = 1000.0
layer_eps = 1e-12

AXES = ("dp", "tensor")
F32 = jnp.float32
BF16 = jnp.bfloat16


def params(mebibytes):
    return pltpu.CompilerParams(
        dimension_semantics=("arbitrary",), vmem_limit_bytes=mebibytes * 2**20
    )


def whole_block(shape):
    zeros = (0,) * len(shape)
    return pl.BlockSpec(shape, lambda *_: zeros, pipeline_mode=pl.Buffered(1))


def dot_nn(a, b):
    return lax.dot_general(a, b, (((1,), (0,)), ((), ())), preferred_element_type=F32)


def dot_nt(a, b):
    return lax.dot_general(a, b, (((1,), (1,)), ((), ())), preferred_element_type=F32)


def dot_tn(a, b):
    return lax.dot_general(a, b, (((0,), (0,)), ((), ())), preferred_element_type=F32)


def half_swap(block):
    lane = lax.broadcasted_iota(jnp.int32, block.shape, 1)
    return jnp.where(
        lane % HD < HD // 2, pltpu.roll(block, LANES - HD // 2, 1), pltpu.roll(block, HD // 2, 1)
    )


def normalise(summed):
    mean = jnp.mean(summed, axis=-1, keepdims=True)
    centred = summed - mean
    inv_std = lax.rsqrt(jnp.mean(centred * centred, axis=-1, keepdims=True) + layer_eps)
    return centred * inv_std, inv_std


def norm_back(normed, inv_std, gain, grad):
    scaled = grad * gain
    return inv_std * (
        scaled
        - jnp.mean(scaled, axis=-1, keepdims=True)
        - normed * jnp.mean(scaled * normed, axis=-1, keepdims=True)
    )


def in_hbm(x):
    return pltpu.with_memory_space_constraint(x, pltpu.HBM)


class Pieces:
    def __init__(self, slots, width, cols=None):
        arrays = []
        self.where = []
        for slot in slots:
            for array, index in slot:
                known = [i for i, other in enumerate(arrays) if other is array]
                if not known:
                    arrays.append(array)
                self.where.append((known[0] if known else len(arrays) - 1, index))
        self.flat = [in_hbm(x) for x in arrays]
        self.n_slots = len(slots)
        self.n_pieces = len(slots[0])
        self.blocks = [(p, b) for p, (x, _) in enumerate(slots[0]) for b in range(x.shape[1])]
        _, _, self.block_rows, wide = slots[0][0][0].shape
        self.cols = cols or slice(0, wide)
        self.in_specs = [pl.BlockSpec(memory_space=pl.ANY)] * len(self.flat)
        self.scratch = [
            pltpu.VMEM((self.n_slots, width, self.cols.stop - self.cols.start), BF16),
            pltpu.SemaphoreType.DMA((self.n_slots, len(self.blocks))),
        ]

    def copies(self, slot, refs, offs_ref, scr, sems):
        for j, (p, b) in enumerate(self.blocks):
            start = pl.multiple_of(offs_ref[j], 16)
            array, index = self.where[slot * self.n_pieces + p]
            yield pltpu.make_async_copy(
                refs[array].at[index, b, :, self.cols],
                scr.at[slot, pl.ds(start, self.block_rows), :],
                sems.at[slot, j],
            )

    def start(self, slot, *args):
        for copy in self.copies(slot, *args):
            copy.start()

    def wait(self, slot, *args):
        for copy in self.copies(slot, *args):
            copy.wait()

    def start_all(self, *args):
        for s in range(self.n_slots):
            self.start(s, *args)

    def wait_for_step(self, step, *args):
        for s in range(self.n_slots):

            @pl.when(step == s)
            def _(s=s):
                self.wait(s, *args)


def head_lanes(block, h, extra):
    lane = lax.broadcasted_iota(jnp.int32, block.shape, 1)
    mine = lane < HD if h % 2 == 0 else lane >= HD
    return jnp.where(mine, block, extra)


def project(x_rel, pieces, offsets, cosine, sine, seg_col, pos, n_row, k_tile):
    seq, width = x_rel.shape
    rows = seq // n_row
    tile = min(256, rows)
    per_piece = rows // tile
    held = Pieces([pieces], width)
    n_in = len(held.flat)

    def true_tile(i, pos_ref):
        return (pos_ref[0] ^ (i // per_piece)) * per_piece + i % per_piece

    def body(pos_ref, offs_ref, x_ref, cos_ref, sin_ref, seg_ref, *rest):
        w_refs, rest = rest[:n_in], rest[n_in:]
        q_ref, k_ref, v_ref, kt_ref, vt_ref, norm_ref, w_scr, sems = rest

        @pl.when(pl.program_id(0) == 0)
        def _():
            held.start(0, w_refs, offs_ref, w_scr, sems)
            held.wait(0, w_refs, offs_ref, w_scr, sems)
            norm_ref[...] = jnp.transpose(w_scr[0, :, 4 * width :].astype(F32))[:8, :]

        x = x_ref[...]
        cos = cos_ref[...]
        sin = sin_ref[...]
        lane = lax.broadcasted_iota(jnp.int32, (tile, LANES), 1)
        same = lane % HD == seg_ref[...]
        key_extra = jnp.where(same, 1.0, 0.0)
        query_extra = jnp.where(same, 0.0, NEG)
        merged = dot_nn(x, w_scr[0, :, : 3 * width])
        for b in range(width // LANES):
            cols = slice(b * LANES, (b + 1) * LANES)
            q = merged[:, b * LANES : (b + 1) * LANES]
            k = merged[:, width + b * LANES : width + (b + 1) * LANES]
            v = merged[:, 2 * width + b * LANES : 2 * width + (b + 1) * LANES]
            q = (q * cos + half_swap(q) * sin) * (HD**-0.5)
            k = k * cos + half_swap(k) * sin
            for h in (2 * b, 2 * b + 1):
                q_ref[h] = head_lanes(q, h, query_extra).astype(BF16)
                k_ref[h] = head_lanes(k, h, key_extra).astype(BF16)
            v_ref[:, cols] = v.astype(BF16)
            vt_ref[cols, :] = jnp.transpose(v).astype(BF16)
            for j in range(tile // k_tile):
                kt_ref[j, cols, :] = jnp.transpose(k[j * k_tile : (j + 1) * k_tile, :]).astype(BF16)

    row_block = pl.BlockSpec((tile, width), lambda i, p, o: (true_tile(i, p), 0))
    head_block = pl.BlockSpec((H, tile, LANES), lambda i, p, o: (0, true_tile(i, p), 0))
    table_block = pl.BlockSpec((tile, LANES), lambda i, p, o: (true_tile(i, p), 0))
    return pl.pallas_call(
        body,
        grid_spec=pltpu.PrefetchScalarGridSpec(
            num_scalar_prefetch=2,
            grid=(seq // tile,),
            in_specs=[
                pl.BlockSpec((tile, width), lambda i, p, o: (i, 0)),
                table_block,
                table_block,
                pl.BlockSpec((tile, 1), lambda i, p, o: (true_tile(i, p), 0)),
            ]
            + held.in_specs,
            out_specs=[
                head_block,
                head_block,
                row_block,
                pl.BlockSpec((tile // k_tile, width, k_tile), lambda i, p, o: (true_tile(i, p), 0, 0)),
                pl.BlockSpec((width, tile), lambda i, p, o: (0, true_tile(i, p))),
                whole_block((8, width)),
            ],
            scratch_shapes=held.scratch,
        ),
        out_shape=[jax.ShapeDtypeStruct((H, seq, LANES), BF16)] * 2
        + [
            jax.ShapeDtypeStruct((seq, width), BF16),
            jax.ShapeDtypeStruct((seq // k_tile, width, k_tile), BF16),
            jax.ShapeDtypeStruct((width, seq), BF16),
            jax.ShapeDtypeStruct((8, width), F32),
        ],
        compiler_params=params(20),
        name="project",
    )(pos, offsets, x_rel, cosine, sine, seg_col, *held.flat)


GROUP = 6


def attend(x_own, q, k, vt, pieces, offsets, norms, pos):
    rows, width = x_own.shape
    seq = q.shape[1]
    group_cols = GROUP * HD
    n_steps = H // GROUP
    held = Pieces([pieces], width, slice(3 * width, 4 * width))
    n_in = len(held.flat)

    def body(pos_ref, offs_ref, x_ref, q_ref, k_ref, vt_ref, norm_ref, *rest):
        w_refs, rest = rest[:n_in], rest[n_in:]
        att_ref, lse_ref, n_ref, istd_ref, mid_ref, acc, lse, w_scr, sems = rest
        g = pl.program_id(0)

        @pl.when(g == 0)
        def _():
            held.start(0, w_refs, offs_ref, w_scr, sems)

        for j in range(GROUP):
            s = dot_nt(k_ref[j], q_ref[j])
            peak = jnp.max(s, axis=0, keepdims=True)
            e = jnp.exp(s - peak)
            total = jnp.sum(e, axis=0, keepdims=True)
            out = dot_nn(vt_ref[j * HD : (j + 1) * HD, :], e.astype(BF16))
            acc[g, j * HD : (j + 1) * HD, :] = out / total
            lse[g, j : j + 1, :] = peak + jnp.log(total)

        @pl.when(g == n_steps - 1)
        def _():
            held.wait(0, w_refs, offs_ref, w_scr, sems)
            for i in range(n_steps):
                lse_ref[i] = lse[i]
                att_ref[:, i * group_cols : (i + 1) * group_cols] = jnp.transpose(acc[i]).astype(BF16)
            first_sum = x_ref[...].astype(F32) + dot_nn(att_ref[...], w_scr[0])
            normed, inv_std = normalise(first_sum)
            n_ref[...] = normed
            istd_ref[...] = inv_std
            mid_ref[...] = (normed * norm_ref[0:1, :] + norm_ref[2:3, :]).astype(BF16)

    own = whole_block((rows, width))
    return pl.pallas_call(
        body,
        grid_spec=pltpu.PrefetchScalarGridSpec(
            num_scalar_prefetch=2,
            grid=(n_steps,),
            in_specs=[
                own,
                pl.BlockSpec((GROUP, rows, LANES), lambda g, p, o: (g, p[0], 0)),
                pl.BlockSpec((GROUP, seq, LANES), lambda g, p, o: (g, 0, 0)),
                pl.BlockSpec((group_cols, seq), lambda g, p, o: (g, 0)),
                whole_block((8, width)),
            ]
            + held.in_specs,
            out_specs=[own, whole_block((n_steps, 8, rows)), own, whole_block((rows, 1)), own],
            scratch_shapes=[
                pltpu.VMEM((n_steps, group_cols, rows), F32),
                pltpu.VMEM((n_steps, 8, rows), F32),
            ]
            + held.scratch,
        ),
        out_shape=[
            jax.ShapeDtypeStruct((rows, width), BF16),
            jax.ShapeDtypeStruct((n_steps, 8, rows), F32),
            jax.ShapeDtypeStruct((rows, width), F32),
            jax.ShapeDtypeStruct((rows, 1), F32),
            jax.ShapeDtypeStruct((rows, width), BF16),
        ],
        compiler_params=params(18),
        name="attend",
    )(pos, offsets, x_own, q, k, vt, norms, *held.flat)


def feed_forward(mid_own, mid_sib, slots, offsets, before, last):
    rows, width = mid_own.shape
    held = Pieces(slots, width)
    n_slots, cols = held.n_slots, held.cols.stop // 3
    n_in = len(held.flat)

    def body(offs_ref, own_ref, sib_ref, *rest):
        w_refs, rest = rest[:n_in], rest[n_in:]
        if before is not None:
            before_ref, rest = rest[0], rest[1:]
        if last:
            hid_ref, a_ref, b_ref, out_own, out_sib, acc, w_scr, sems = rest
        else:
            hid_ref, a_ref, b_ref, acc, w_scr, sems = rest
        s = pl.program_id(0)

        @pl.when(s == 0)
        def _():
            held.start_all(w_refs, offs_ref, w_scr, sems)
            acc[...] = jnp.zeros(acc.shape, F32) if before is None else before_ref[...]

        held.wait_for_step(s, w_refs, offs_ref, w_scr, sems)
        for i, x_ref in enumerate((own_ref, sib_ref)):
            part = slice(i * rows, (i + 1) * rows)
            both = dot_nn(x_ref[...], w_scr[s, :, : 2 * cols])
            gate, up = both[:, :cols], both[:, cols:]
            sig = 0.5 * jnp.tanh(0.5 * gate) + 0.5
            silu = gate * sig
            hidden = (silu * up).astype(BF16)
            hid_ref[0, part, :] = hidden
            a_ref[0, part, :] = (up * (sig + silu * (1.0 - sig))).astype(BF16)
            b_ref[0, part, :] = silu.astype(BF16)
            acc[part, :] += dot_nt(hidden, w_scr[s, :, 2 * cols :])

        if last:

            @pl.when(s == n_slots - 1)
            def _():
                out_own[...] = acc[:rows, :]
                out_sib[...] = acc[rows:, :].astype(BF16)

    full = whole_block((rows, width))
    both_block = whole_block((2 * rows, width))
    act = pl.BlockSpec((1, 2 * rows, cols), lambda i, *_: (i, 0, 0))
    act_shape = jax.ShapeDtypeStruct((n_slots, 2 * rows, cols), BF16)
    extra = [] if before is None else [before]
    if last:
        acc_specs = [full, full]
        acc_shapes = [jax.ShapeDtypeStruct((rows, width), F32), jax.ShapeDtypeStruct((rows, width), BF16)]
        acc_scratch = [pltpu.VMEM((2 * rows, width), F32)]
    else:
        acc_specs = [both_block]
        acc_shapes = [jax.ShapeDtypeStruct((2 * rows, width), F32)]
        acc_scratch = []
    return pl.pallas_call(
        body,
        grid_spec=pltpu.PrefetchScalarGridSpec(
            num_scalar_prefetch=1,
            grid=(n_slots,),
            in_specs=[full, full] + held.in_specs + [both_block] * len(extra),
            out_specs=[act] * 3 + acc_specs,
            scratch_shapes=acc_scratch + held.scratch,
        ),
        out_shape=[act_shape] * 3 + acc_shapes,
        compiler_params=params(18),
        name="feed_forward",
    )(offsets, mid_own, mid_sib, *held.flat, *extra)


def second_norm(normed1, part_own, part_sib, out_grad, norms):
    rows, width = normed1.shape
    tile = min(256, rows)

    def body(n_ref, own_ref, sib_ref, g_ref, norm_ref, out_ref, d_ref, dl_ref, ng_ref):
        middle = n_ref[...] * norm_ref[0:1, :] + norm_ref[2:3, :]
        second_sum = middle + (own_ref[...] + sib_ref[...].astype(F32))
        normed, inv_std = normalise(second_sum)
        out_ref[...] = (normed * norm_ref[1:2, :] + norm_ref[3:4, :]).astype(BF16)
        grad = g_ref[...].astype(F32)
        d = norm_back(normed, inv_std, norm_ref[1:2, :], grad)
        d_ref[...] = d
        dl_ref[...] = d.astype(BF16)

        @pl.when(pl.program_id(0) == 0)
        def _():
            ng_ref[...] = jnp.zeros(ng_ref.shape, F32)

        ng_ref[0:1, :] += jnp.sum(grad * normed, axis=0, keepdims=True)
        ng_ref[1:2, :] += jnp.sum(grad, axis=0, keepdims=True)

    block = pl.BlockSpec((tile, width), lambda i: (i, 0))
    return pl.pallas_call(
        body,
        grid=(rows // tile,),
        in_specs=[block] * 4 + [whole_block((8, width))],
        out_specs=[block] * 3 + [whole_block((8, width))],
        out_shape=[
            jax.ShapeDtypeStruct((rows, width), BF16),
            jax.ShapeDtypeStruct((rows, width), F32),
            jax.ShapeDtypeStruct((rows, width), BF16),
            jax.ShapeDtypeStruct((8, width), F32),
        ],
        compiler_params=params(10),
        name="second_norm",
    )(normed1, part_own, part_sib, out_grad, norms)


def hidden_back(dffs, factors, slots, offsets):
    rows, width = dffs[0].shape
    held = Pieces(slots, width)
    n_slots, cols = held.n_slots, held.cols.stop // 3
    n_in = len(held.flat)
    per_call = factors[0][0].shape[0]
    n_fac = len(factors)

    def body(offs_ref, do_ref, ds_ref, *rest):
        fac_refs, rest = rest[: 2 * n_fac], rest[2 * n_fac :]
        w_refs, rest = rest[:n_in], rest[n_in:]
        d_ref, out_own, out_sib, acc, w_scr, sems = rest
        s = pl.program_id(0)

        @pl.when(s == 0)
        def _():
            held.start_all(w_refs, offs_ref, w_scr, sems)
            acc[...] = jnp.zeros(acc.shape, F32)

        held.wait_for_step(s, w_refs, offs_ref, w_scr, sems)

        def work(a_ref, b_ref):
            for i, x_ref in enumerate((do_ref, ds_ref)):
                part = slice(i * rows, (i + 1) * rows)
                dh = dot_nn(x_ref[...], w_scr[s, :, 2 * cols :])
                d_ref[0, part, :cols] = (dh * a_ref[0, part, :].astype(F32)).astype(BF16)
                d_ref[0, part, cols:] = (dh * b_ref[0, part, :].astype(F32)).astype(BF16)
                acc[part, :] += dot_nt(d_ref[0, part, :], w_scr[s, :, : 2 * cols])

        for f in range(n_fac):

            @pl.when(s // per_call == f)
            def _(f=f):
                work(fac_refs[2 * f], fac_refs[2 * f + 1])

        @pl.when(s == n_slots - 1)
        def _():
            out_own[...] = acc[:rows, :]
            out_sib[...] = acc[rows:, :].astype(BF16)

    full = whole_block((rows, width))

    def fac_spec(f):
        return pl.BlockSpec(
            (1, 2 * rows, cols), lambda i, *_: (jnp.clip(i - f * per_call, 0, per_call - 1), 0, 0)
        )

    return pl.pallas_call(
        body,
        grid_spec=pltpu.PrefetchScalarGridSpec(
            num_scalar_prefetch=1,
            grid=(n_slots,),
            in_specs=[full, full]
            + [fac_spec(f) for f in range(n_fac) for _ in range(2)]
            + held.in_specs,
            out_specs=[pl.BlockSpec((1, 2 * rows, 2 * cols), lambda i, *_: (i, 0, 0)), full, full],
            scratch_shapes=[pltpu.VMEM((2 * rows, width), F32)] + held.scratch,
        ),
        out_shape=[
            jax.ShapeDtypeStruct((n_slots, 2 * rows, 2 * cols), BF16),
            jax.ShapeDtypeStruct((rows, width), F32),
            jax.ShapeDtypeStruct((rows, width), BF16),
        ],
        compiler_params=params(22),
        name="hidden_back",
    )(offsets, *dffs, *[x for pair in factors for x in pair], *held.flat)


def store_groups(groups, group_refs, offs_ref, n_blocks, block_rows, source):
    for (picks, dtype), ref in zip(groups, group_refs):
        for j, p in enumerate(picks):
            for b in range(n_blocks):
                start = pl.multiple_of(offs_ref[p * n_blocks + b], 8)
                ref[j, b] = source[pl.ds(start, block_rows), :].astype(dtype)


def ffn_grads(first, mids, dffs, hidden, d_both, offsets, groups, n_blocks, block_rows):
    rows, width = mids[0].shape
    n_slots, _, cols = hidden.shape
    shapes = [[(len(picks), n_blocks, block_rows, 3 * cols) for picks, _ in gs] for gs in groups]
    n_out = [len(gs) for gs in groups]

    def body(offs_ref, mo, ms, do, ds, hid_ref, d_ref, *rest):
        outs, rest = rest[: sum(n_out)], rest[sum(n_out) :]
        stages, (mid_t, dff_t, g_scr, sems) = rest[: sum(n_out)], rest[sum(n_out) :]
        s = pl.program_id(0)

        @pl.when(s == 0)
        def _():
            for i, (m_ref, x_ref) in enumerate(((mo, do), (ms, ds))):
                part = slice(i * rows, (i + 1) * rows)
                mid_t[:, part] = jnp.transpose(m_ref[...])
                dff_t[:, part] = jnp.transpose(x_ref[...])

        g_scr[:, : 2 * cols] = dot_nn(mid_t[...], d_ref[0])
        g_scr[:, 2 * cols :] = dot_nn(dff_t[...], hid_ref[0])
        for j in range(n_slots):
            at = sum(n_out[:j])

            @pl.when(s == j)
            def _(j=j, at=at):
                store_groups(groups[j], stages[at : at + n_out[j]], offs_ref, n_blocks, block_rows, g_scr)
                for o in range(at, at + n_out[j]):
                    pltpu.make_async_copy(stages[o], outs[o], sems.at[o]).start()

        @pl.when(s == n_slots - 1)
        def _():
            for o in range(sum(n_out)):
                pltpu.make_async_copy(stages[o], outs[o], sems.at[o]).wait()

    flat = [(shape, dtype) for ss, gs in zip(shapes, groups) for shape, (_, dtype) in zip(ss, gs)]
    full = whole_block((rows, width))
    results = pl.pallas_call(
        body,
        grid_spec=pltpu.PrefetchScalarGridSpec(
            num_scalar_prefetch=1,
            grid=(n_slots,),
            in_specs=[full] * 4
            + [
                pl.BlockSpec((1, 2 * rows, cols), lambda i, *_: (i, 0, 0)),
                pl.BlockSpec((1, 2 * rows, 2 * cols), lambda i, *_: (first + i, 0, 0)),
            ],
            out_specs=[pl.BlockSpec(memory_space=pl.ANY)] * len(flat),
            scratch_shapes=[pltpu.VMEM(shape, dtype) for shape, dtype in flat]
            + [
                pltpu.VMEM((width, 2 * rows), BF16),
                pltpu.VMEM((width, 2 * rows), BF16),
                pltpu.VMEM((width, 3 * cols), F32),
                pltpu.SemaphoreType.DMA((len(flat),)),
            ],
        ),
        out_shape=[jax.ShapeDtypeStruct(shape, dtype) for shape, dtype in flat],
        compiler_params=params(22),
        name="ffn_grads",
    )(offsets, *mids, *dffs, hidden, d_both)
    return [results[sum(n_out[:j]) : sum(n_out[: j + 1])] for j in range(n_slots)]


def first_norm_back(normed1, inv_std1, d_second, d_mid, d_mid_sib, norms):
    rows, width = normed1.shape
    tile = min(256, rows)

    def body(n_ref, istd_ref, d2_ref, dm_ref, ds_ref, norm_ref, d_ref, dl_ref, ng_ref):
        grad = d2_ref[...] + dm_ref[...] + ds_ref[...].astype(F32)
        normed = n_ref[...]
        d = norm_back(normed, istd_ref[...], norm_ref[0:1, :], grad)
        d_ref[...] = d
        dl_ref[...] = d.astype(BF16)

        @pl.when(pl.program_id(0) == 0)
        def _():
            ng_ref[...] = jnp.zeros(ng_ref.shape, F32)

        ng_ref[0:1, :] += jnp.sum(grad * normed, axis=0, keepdims=True)
        ng_ref[1:2, :] += jnp.sum(grad, axis=0, keepdims=True)

    block = pl.BlockSpec((tile, width), lambda i: (i, 0))
    column = pl.BlockSpec((tile, 1), lambda i: (i, 0))
    return pl.pallas_call(
        body,
        grid=(rows // tile,),
        in_specs=[block, column, block, block, block, whole_block((8, width))],
        out_specs=[block] * 2 + [whole_block((8, width))],
        out_shape=[
            jax.ShapeDtypeStruct((rows, width), F32),
            jax.ShapeDtypeStruct((rows, width), BF16),
            jax.ShapeDtypeStruct((8, width), F32),
        ],
        compiler_params=params(8),
        name="first_norm_back",
    )(normed1, inv_std1, d_second, d_mid, d_mid_sib, norms)


def out_grads(attended, d_first_low, norm1, norm2):
    rows, width = attended.shape

    def body(att_ref, dl_ref, n1_ref, n2_ref, out_ref):
        out_ref[:, :width] = dot_tn(att_ref[...], dl_ref[...]).astype(BF16)
        stacked = jnp.concatenate(
            [n1_ref[0:1, :], n2_ref[0:1, :], n1_ref[1:2, :], n2_ref[1:2, :],
             jnp.zeros((PAD - 4, width), F32)], axis=0)
        out_ref[:, width:] = jnp.transpose(stacked).astype(BF16)

    operands = (attended, d_first_low, norm1, norm2)
    return pl.pallas_call(
        body,
        grid=(1,),
        in_specs=[whole_block(o.shape) for o in operands],
        out_specs=whole_block((width, width + PAD)),
        out_shape=jax.ShapeDtypeStruct((width, width + PAD), BF16),
        compiler_params=params(10),
        name="out_grads",
    )(*operands)


def unrotated(g, cos, sin):
    g = g.astype(BF16).astype(F32)
    return (g * cos - half_swap(g) * sin).astype(BF16)


def prepare_heads(d_att, att, dom, delta, at):
    n = d_att.shape[0]
    flipped = jnp.transpose(d_att.astype(F32) * att.astype(F32))
    for j in range(GROUP):
        delta[j : j + 1, at : at + n] = jnp.sum(flipped[j * HD : (j + 1) * HD, :], axis=0, keepdims=True)
        block = d_att[:, j // 2 * LANES : j // 2 * LANES + LANES].astype(F32)
        dom[j, at : at + n, :] = head_lanes(block, j, 0.0).astype(BF16)


def pair_up(even, odd):
    return head_lanes(even, 0, odd)


def attend_back_own(d_first, attended, lse, q, k, v, kt, key_from, key_to, cosine, sine, pieces, offsets, pos,
                    k_tile):
    rows, width = d_first.shape
    seq = q.shape[1]
    n_own = rows // k_tile
    group_cols = GROUP * HD
    held = Pieces([pieces], width, slice(3 * width, 4 * width))
    n_in = len(held.flat)
    n_q = key_from.shape[0] * rows // seq

    def body(pos_ref, offs_ref, from_ref, to_ref, d_ref, att_ref, lse_ref, q_ref, k_ref, v_ref, kt_ref,
             cos_ref, sin_ref, *rest):
        w_refs, rest = rest[:n_in], rest[n_in:]
        dq_ref, dk_ref, dv_ref, dom, delta, dq, w_scr, sems = rest
        g = pl.program_id(0)

        @pl.when(g == 0)
        def _():
            held.start(0, w_refs, offs_ref, w_scr, sems)
            held.wait(0, w_refs, offs_ref, w_scr, sems)

        w_rows = w_scr[0, pl.ds(pl.multiple_of(g * group_cols, group_cols), group_cols), :]
        d_att = dot_nt(d_ref[...], w_rows).astype(BF16)
        prepare_heads(d_att, att_ref[...], dom, delta, 0)
        own_low = pos_ref[0] * n_own

        def weights_of(j, at, n, some):
            cols = slice(j // 2 * LANES, j // 2 * LANES + LANES)
            s = dot_nt(k_ref[j, pl.ds(at, n), :], q_ref[j, some, :])
            p = jnp.exp(s - lse_ref[0, j : j + 1, some])
            dp = dot_nt(v_ref[pl.ds(at, n), cols], dom[j, some, :])
            return p, (p * (dp - delta[j : j + 1, some])).astype(BF16)

        base = pl.multiple_of(pos_ref[0] * rows, rows)
        for b in range(GROUP // 2):
            dks, dvs = [], []
            for j in (2 * b, 2 * b + 1):
                p, ds = weights_of(j, base, rows, slice(0, rows))
                dvs.append(dot_nn(p.astype(BF16), dom[j]))
                dks.append(dot_nn(ds, q_ref[j]))
                heads = slice(j * HD, (j + 1) * HD)
                total = None
                for t in range(n_own):
                    part = dot_nn(kt_ref[own_low + t, heads, :], ds[t * k_tile : (t + 1) * k_tile, :])
                    total = part if total is None else total + part
                dq[heads, :] = total
            cols = slice(b * LANES, (b + 1) * LANES)
            dk_ref[:, cols] = pair_up(*dks)
            dv_ref[:, cols] = dvs[0] + dvs[1]

        first_tile = pos_ref[0] * n_q
        for i in range(n_q):
            some = slice(i * rows // n_q, (i + 1) * rows // n_q)
            low = from_ref[first_tile + i]
            n_left = jnp.maximum(own_low - low, 0)
            n_right = jnp.maximum(to_ref[first_tile + i] - own_low - n_own, 0)

            def outside(t, carry, some=some, low=low, n_left=n_left):
                tile = jnp.where(t < n_left, low + t, own_low + n_own + t - n_left)
                at = pl.multiple_of(tile * k_tile, k_tile)
                for j in range(GROUP):
                    heads = slice(j * HD, (j + 1) * HD)
                    _, ds = weights_of(j, at, k_tile, some)
                    dq[heads, some] += dot_nn(kt_ref[tile, heads, :], ds)
                return carry

            lax.fori_loop(0, n_left + n_right, outside, 0)

        turned = jnp.transpose(dq[...]) * (HD**-0.5)
        for b in range(GROUP // 2):
            cols = slice(b * LANES, (b + 1) * LANES)
            dq_ref[:, cols] = unrotated(turned[:, cols], cos_ref[...], sin_ref[...])

    def col_block(n):
        return pl.BlockSpec((n, group_cols), lambda g, *_: (0, g))

    table = pl.BlockSpec((rows, LANES), lambda g, p, *_: (p[0], 0))
    sum_shape = jax.ShapeDtypeStruct((rows, width), F32)
    return pl.pallas_call(
        body,
        grid_spec=pltpu.PrefetchScalarGridSpec(
            num_scalar_prefetch=4,
            grid=(H // GROUP,),
            in_specs=[
                whole_block((rows, width)),
                col_block(rows),
                pl.BlockSpec((1, 8, rows), lambda g, *_: (g, 0, 0)),
                pl.BlockSpec((GROUP, rows, LANES), lambda g, p, *_: (g, p[0], 0)),
                pl.BlockSpec((GROUP, seq, LANES), lambda g, *_: (g, 0, 0)),
                col_block(seq),
                pl.BlockSpec((seq // k_tile, group_cols, k_tile), lambda g, *_: (0, g, 0)),
                table,
                table,
            ]
            + held.in_specs,
            out_specs=[col_block(rows)] * 3,
            scratch_shapes=[
                pltpu.VMEM((GROUP, rows, LANES), BF16),
                pltpu.VMEM((8, rows), F32),
                pltpu.VMEM((group_cols, rows), F32),
            ]
            + held.scratch,
        ),
        out_shape=[jax.ShapeDtypeStruct((rows, width), BF16), sum_shape, sum_shape],
        compiler_params=params(20),
        name="attend_back_own",
    )(pos, offsets, key_from, key_to, d_first, attended, lse, q, k, v, kt, cosine, sine, *held.flat)


def attend_back_others(d_others, att_others, lse_others, sums, q, k, v, key_from, key_to, cosine, sine, pieces,
                       offsets, pos, q_tile, k_tile):
    rows, width = sums[0].shape
    seq = q.shape[1]
    n_q = rows // q_tile
    n_own = rows // k_tile
    n_tiles = d_others.shape[0] // q_tile
    group_cols = GROUP * HD
    held = Pieces([pieces], width, slice(3 * width, 4 * width))
    n_in = len(held.flat)

    def body(pos_ref, offs_ref, from_ref, to_ref, d_ref, att_ref, lse_ref, q_ref, k_ref, v_ref, dk_in, dv_in,
             cos_ref, sin_ref, *rest):
        w_refs, rest = rest[:n_in], rest[n_in:]
        dk_ref, dv_ref, dom, delta, dk, dv, w_scr, sems = rest
        g = pl.program_id(0)

        @pl.when(g == 0)
        def _():
            held.start(0, w_refs, offs_ref, w_scr, sems)
            held.wait(0, w_refs, offs_ref, w_scr, sems)

        dk[...] = dk_in[...]
        dv[...] = dv_in[...]
        own_low = pos_ref[0] * n_own

        for i in range(n_tiles):
            true_tile = (pos_ref[0] ^ (1 + i // n_q)) * n_q + i % n_q
            low = jnp.maximum(from_ref[true_tile], own_low)
            high = jnp.minimum(to_ref[true_tile], own_low + n_own)
            here = slice(i * q_tile, (i + 1) * q_tile)

            @pl.when(high > low)
            def _(i=i, true_tile=true_tile, low=low, high=high, here=here):
                w_rows = w_scr[0, pl.ds(pl.multiple_of(g * group_cols, group_cols), group_cols), :]
                d_att = dot_nt(d_ref[here, :], w_rows).astype(BF16)
                prepare_heads(d_att, att_ref[here, :], dom, delta, 0)
                q_at = pl.multiple_of(true_tile * q_tile, q_tile)

                def one(tile, carry):
                    at = pl.ds(pl.multiple_of((tile - own_low) * k_tile, k_tile), k_tile)
                    for b in range(GROUP // 2):
                        cols = slice(b * LANES, (b + 1) * LANES)
                        dks, dvs = [], []
                        for j in (2 * b, 2 * b + 1):
                            q_head = q_ref[j, pl.ds(q_at, q_tile), :]
                            s = dot_nt(k_ref[j, at, :], q_head)
                            p = jnp.exp(s - lse_ref[0, j : j + 1, here])
                            dp = dot_nt(v_ref[at, cols], dom[j])
                            ds = (p * (dp - delta[j : j + 1, :])).astype(BF16)
                            dvs.append(dot_nn(p.astype(BF16), dom[j]))
                            dks.append(dot_nn(ds, q_head))
                        dk[at, cols] += pair_up(*dks)
                        dv[at, cols] += dvs[0] + dvs[1]
                    return carry

                lax.fori_loop(low, high, one, 0)

        for b in range(GROUP // 2):
            cols = slice(b * LANES, (b + 1) * LANES)
            dk_ref[:, cols] = unrotated(dk[:, cols], cos_ref[...], sin_ref[...])
        dv_ref[...] = dv[...].astype(BF16)

    def col_block(n):
        return pl.BlockSpec((n, group_cols), lambda g, *_: (0, g))

    table = pl.BlockSpec((rows, LANES), lambda g, p, *_: (p[0], 0))
    return pl.pallas_call(
        body,
        grid_spec=pltpu.PrefetchScalarGridSpec(
            num_scalar_prefetch=4,
            grid=(H // GROUP,),
            in_specs=[
                whole_block(d_others.shape),
                col_block(d_others.shape[0]),
                pl.BlockSpec((1, 8, d_others.shape[0]), lambda g, *_: (g, 0, 0)),
                pl.BlockSpec((GROUP, seq, LANES), lambda g, *_: (g, 0, 0)),
                pl.BlockSpec((GROUP, rows, LANES), lambda g, p, *_: (g, p[0], 0)),
                pl.BlockSpec((rows, group_cols), lambda g, p, *_: (p[0], g)),
                col_block(rows),
                col_block(rows),
                table,
                table,
            ]
            + held.in_specs,
            out_specs=[col_block(rows)] * 2,
            scratch_shapes=[
                pltpu.VMEM((GROUP, q_tile, LANES), BF16),
                pltpu.VMEM((8, q_tile), F32),
                pltpu.VMEM((rows, group_cols), F32),
                pltpu.VMEM((rows, group_cols), F32),
            ]
            + held.scratch,
        ),
        out_shape=[jax.ShapeDtypeStruct((rows, width), BF16)] * 2,
        compiler_params=params(18),
        name="attend_back_others",
    )(pos, offsets, key_from, key_to, d_others, att_others, lse_others, q, k, v, *sums, cosine, sine,
      *held.flat)


def qkv_grads(x_own, merged, out_part, offsets, groups, n_blocks, block_rows):
    rows, width = x_own.shape
    wide = 3 * width + out_part.shape[1]

    def body(offs_ref, x_ref, dq_ref, dk_ref, dv_ref, out_ref, *rest):
        group_refs, g_scr = rest[:-1], rest[-1]
        x_t = jnp.transpose(x_ref[...])
        for j, ref in enumerate((dq_ref, dk_ref, dv_ref)):
            g_scr[:, j * width : (j + 1) * width] = dot_nn(x_t, ref[...])
        g_scr[:, 3 * width :] = out_ref[...].astype(F32)
        store_groups(groups, group_refs, offs_ref, n_blocks, block_rows, g_scr)

    group_shapes = [(len(picks), n_blocks, block_rows, wide) for picks, _ in groups]
    return pl.pallas_call(
        body,
        grid_spec=pltpu.PrefetchScalarGridSpec(
            num_scalar_prefetch=1,
            grid=(1,),
            in_specs=[whole_block((rows, width))] * 4 + [whole_block(out_part.shape)],
            out_specs=[whole_block(s) for s in group_shapes],
            scratch_shapes=[pltpu.VMEM((width, wide), F32)],
        ),
        out_shape=[jax.ShapeDtypeStruct(s, dtype) for s, (_, dtype) in zip(group_shapes, groups)],
        compiler_params=params(20),
        name="qkv_grads",
    )(offsets, x_own, *merged, out_part)


def input_grads(merged, d_first, pieces, offsets):
    rows, width = d_first.shape
    tile = min(256, rows)
    held = Pieces([pieces], width, slice(0, 3 * width))
    n_in = len(held.flat)

    def body(offs_ref, dq_ref, dk_ref, dv_ref, df_ref, *rest):
        w_refs, (out_ref, w_scr, sems) = rest[:n_in], rest[n_in:]

        @pl.when(pl.program_id(0) == 0)
        def _():
            held.start(0, w_refs, offs_ref, w_scr, sems)
            held.wait(0, w_refs, offs_ref, w_scr, sems)

        total = df_ref[...]
        for j, ref in enumerate((dq_ref, dk_ref, dv_ref)):
            total = total + dot_nt(ref[...], w_scr[0, :, j * width : (j + 1) * width])
        out_ref[...] = total

    block = pl.BlockSpec((tile, width), lambda i, o: (i, 0))
    return pl.pallas_call(
        body,
        grid_spec=pltpu.PrefetchScalarGridSpec(
            num_scalar_prefetch=1,
            grid=(rows // tile,),
            in_specs=[block] * 4 + held.in_specs,
            out_specs=block,
            scratch_shapes=held.scratch,
        ),
        out_shape=jax.ShapeDtypeStruct((rows, width), F32),
        compiler_params=params(12),
        name="input_grads",
    )(offsets, *map(in_hbm, merged), in_hbm(d_first), *held.flat)


def combine(kept, got):
    _, n_blocks, block_rows, wide = kept.shape

    def body(kept_ref, got_ref, own_ref, on_ref):
        own_ref[...] = kept_ref[0].astype(F32) + got_ref[0].astype(F32)
        on_ref[...] = (kept_ref[1].astype(F32) + got_ref[1].astype(F32)).astype(BF16)

    two = pl.BlockSpec((2, 1, block_rows, wide), lambda i: (0, i, 0, 0))
    one = pl.BlockSpec((1, block_rows, wide), lambda i: (i, 0, 0))
    shape = (n_blocks, block_rows, wide)
    return pl.pallas_call(
        body,
        grid=(n_blocks,),
        in_specs=[two, two],
        out_specs=[one, one],
        out_shape=[jax.ShapeDtypeStruct(shape, F32), jax.ShapeDtypeStruct(shape, BF16)],
        compiler_params=params(6),
        name="combine",
    )(kept, got)


def make_per_device(ndp, nt):
    plane = ndp // 2

    def move(value, chip=0, core=0, flip=0):
        pairs = []
        for d in range(ndp):
            for t in range(nt):
                to_d = ((d // 2) ^ chip) * 2 + ((d % 2) ^ core)
                pairs.append((d * nt + t, to_d * nt + (t ^ flip)))
        return lax.ppermute(value, AXES, pairs)

    def after(value, *others):
        return lax.optimization_barrier((value, *others))[0]

    def per_device(inputs, segment_ids, qkv_weight, out_weight, norm_gains, norm_biases,
                   gate_weight, up_weight, down_weight, out_grad):
        rows, width = inputs.shape
        seq = segment_ids.shape[1]
        n_row = seq // rows
        q_tile = min(256, rows)
        k_tile = min(256, rows)
        shard = qkv_weight.shape[0]
        ffn_rows, ffn_cols = gate_weight.shape
        half = ffn_cols // 2
        fast = plane == 4 and nt == 4 and n_row == 2

        d_index = lax.axis_index("dp")
        core = d_index % 2
        chip = d_index // 2
        t_index = lax.axis_index("tensor")
        pos = (t_index % n_row).astype(jnp.int32)
        block_at = [((chip ^ dxy) * 2 + (core ^ other)) for dxy in range(4) for other in range(2)]

        packed = jnp.concatenate(
            [qkv_weight, out_weight, norm_gains.T, norm_biases.T,
             jnp.zeros((shard, PAD - 4), BF16)], axis=1)
        seg = lax.dynamic_index_in_dim(segment_ids, t_index // n_row, 0, keepdims=False)
        doc_from = jnp.sum((seg[None, :] < seg[:, None]).astype(jnp.int32), axis=1)
        doc_to = jnp.sum((seg[None, :] <= seg[:, None]).astype(jnp.int32), axis=1)
        place = (jnp.arange(seq, dtype=jnp.int32) - doc_from).astype(F32)
        lane = np.arange(LANES)
        frequency = rope_base ** (-jnp.asarray(lane % (HD // 2), F32) * 2.0 / HD)
        angles = place[:, None] * frequency[None, :]
        cosine = jnp.cos(angles)
        sine = jnp.sin(angles) * jnp.asarray(np.where(lane % HD < HD // 2, -1.0, 1.0), F32)[None, :]
        key_from = doc_from[::q_tile] // k_tile
        key_to = (doc_to[q_tile - 1 :: q_tile] + k_tile - 1) // k_tile
        seg_col = seg[:, None]
        seg_row = seg.reshape(seq // q_tile, 1, q_tile)
        pos_arr = pos[None]

        ffn = (gate_weight, up_weight, down_weight.T)
        mine, given = [
            jnp.concatenate([lax.dynamic_slice_in_dim(w, c * half, half, 1) for w in ffn], axis=1)
            for c in (core, 1 - core)
        ]
        if fast:
            pair = jnp.stack([mine, move(given, core=1)])
            x_others = [move(inputs, flip=1)]
            second = move(pair, flip=2)
            by_flip = [packed] + [move(packed, flip=e) for e in range(1, nt)]
            near = jnp.concatenate(
                [lax.select_n(t_index, *[by_flip[j ^ t] for t in range(nt)]) for j in range(nt)], axis=0)[None]
            far = [move(near, chip=dxy) for dxy in range(1, 4)]
            last_two = move(jnp.stack([pair, second]), flip=1)
            plane_rows = after(jnp.concatenate([near] + far, axis=0), second, *x_others,
                               cosine, sine, key_from, key_to, seg_col)
            plane_sib = move(plane_rows, core=1)

            def spread(one):
                return one, move(one, chip=1), move(one, chip=2)

            def spread_on(sides, index, along_x, *others):
                passed = after(sides[1 if along_x else 2][index], *others)
                across = move(passed, chip=2 if along_x else 1)
                return [(side, index) for side in sides] + [(across[None], 0)]

            side_0 = spread(pair[None])
            side_1 = spread(after(second, *far)[None])
            x_rel = jnp.concatenate([inputs] + x_others, axis=0)
            w_pieces = [(plane_rows[None], 0), (plane_sib[None], 0)]
            w_offsets = jnp.stack(
                [((chip ^ dxy) * 2 + (core ^ other)) * (nt * shard) for other in range(2) for dxy in range(4)]
            ).astype(jnp.int32)
            f_offsets = jnp.stack([b * ffn_rows for b in block_at]).astype(jnp.int32)
            n_blocks, block_rows = 2, ffn_rows
        else:
            x_others = [move(inputs, flip=e) for e in range(1, n_row)]
            x_rel = jnp.concatenate([inputs] + x_others, axis=0)
            w_pieces = [(lax.all_gather(packed, AXES, axis=0, tiled=True)[None, None], 0)]
            w_offsets = jnp.zeros((1,), jnp.int32)
            full = lax.all_gather(mine, "dp", axis=0, tiled=True).reshape(width, 3, half)
            full = lax.all_gather(full, "tensor", axis=2, tiled=True)
            slots = [[(full.reshape(1, 1, width, 3 * half * nt), 0)]]
            f_offsets = jnp.zeros((1,), jnp.int32)
            n_blocks, block_rows = 1, width

        q, k, v, kt, vt, norms = project(
            x_rel, w_pieces, w_offsets, cosine, sine, seg_col, pos_arr, n_row, k_tile)
        if fast:
            q = after(q, *side_0[1:], *side_1[1:])
            slots = [spread_on(side_0, 0, True, q), spread_on(side_1, 0, False, q)]
            side_2 = spread(after(last_two, q))
        attended, lse, normed1, inv_std1, mid = attend(
            inputs, q, k, vt, w_pieces, w_offsets, norms, pos_arr)
        if fast:
            slots += [spread_on(side_2, 0, True, mid), spread_on(side_2, 1, False, mid)]
        mid_sib = move(mid, core=1)

        calls = [slots[:2], slots[2:]] if fast else [slots]
        acts, partial = [], None
        for j, some in enumerate(calls):
            hid, fac_a, fac_b, *partial = feed_forward(
                mid, mid_sib, some, f_offsets, partial[0] if j else None, j == len(calls) - 1)
            acts.append((hid, fac_a, fac_b))
        part_own, part_sib = partial
        att_others = [move(attended, flip=e) for e in range(1, n_row)]
        lse_others = [move(lse, flip=e) for e in range(1, n_row)]
        part_sib = move(after(part_sib, *att_others, *lse_others), core=1)
        outputs, d_second, d_ffn, norm2 = second_norm(normed1, part_own, part_sib, out_grad, norms)
        d_ffn_sib = move(d_ffn, core=1)
        d_both, d_mid, d_mid_give = hidden_back(
            (d_ffn, d_ffn_sib), [a[1:] for a in acts], slots, f_offsets)
        d_mid_sib = move(d_mid_give, core=1)

        def groups_of(s):
            if not fast:
                return [((0,), BF16)]
            if s % 2 == 0:
                return [((2, 3), BF16), ((0, 1), BF16)]
            return [((1, 3), BF16), ((0, 2), BF16)]

        def weight_grads(j, d_both):
            first = sum(len(c) for c in calls[:j])
            return ffn_grads(
                first, (mid, mid_sib), (d_ffn, d_ffn_sib), acts[j][0], d_both, f_offsets,
                [groups_of(first + i) for i in range(len(calls[j]))], n_blocks, block_rows)

        d_first, d_first_low, norm1 = first_norm_back(
            normed1, inv_std1, d_second, d_mid, d_mid_sib, norms)
        d_others = [move(d_first_low, flip=e) for e in range(1, n_row)]
        d_both = after(d_both, d_first_low)
        if fast:
            reduced = {2 + i: r for i, r in enumerate(weight_grads(1, d_both))}
            reduced.update(enumerate(weight_grads(0, d_both)))
        else:
            reduced = dict(enumerate(weight_grads(0, d_both)))

        def turn(s):
            return (2, 1) if s % 2 == 0 else (1, 2)

        arrived, owned = {}, {}
        if fast:
            arrived = {s: move(reduced[s][0], chip=turn(s)[0]) for s in range(nt)}

        def combine_on(s):
            own, on = combine(reduced[s][1], arrived[s])
            owned[s] = (own, move(on, chip=turn(s)[1]))

        def owned_sum(s, *others):
            own, on = owned[s]
            return own + after(on, *others).astype(F32)

        dq, *sums = attend_back_own(
            after(d_first_low, *[r[-1] for r in reduced.values()]), attended, lse, q, k, v, kt, key_from, key_to,
            cosine, sine, w_pieces, w_offsets, pos_arr, k_tile)
        if fast:
            arrived[2], arrived[3] = after(arrived[2], dq), after(arrived[3], dq)
            combine_on(2)
            combine_on(3)
            sums[0] = after(sums[0], owned[2][0], owned[3][0])
        dk, dv = attend_back_others(
            jnp.concatenate(d_others, axis=0), jnp.concatenate(att_others, axis=0),
            jnp.concatenate(lse_others, axis=2), sums, q, k, v, key_from, key_to, cosine, sine,
            w_pieces, w_offsets, pos_arr, q_tile, k_tile)
        out_part = out_grads(attended, d_first_low, norm1, norm2)
        if fast:
            arrived[0], arrived[1] = after(arrived[0], dk), after(arrived[1], dk)
            combine_on(0)
            combine_on(1)
            dv = after(dv, owned[0][0], owned[1][0], owned[2][1], owned[3][1])
        merged = (dq, dk, dv)

        if fast:
            q_groups = [((1, 3, 5, 7), BF16), ((0, 2, 4, 6), BF16)]
            q_offsets = jnp.stack([b * (nt * shard) for b in block_at]).astype(jnp.int32)
            q_rows = nt * shard
        else:
            q_groups = [((0,), F32)]
            q_offsets = jnp.zeros((1,), jnp.int32)
            q_rows = width
        q_parts = qkv_grads(inputs, merged, out_part, q_offsets, q_groups, 1, q_rows)
        if fast:
            leaving = jnp.stack([owned_sum(2, q_parts[0]), owned_sum(3, q_parts[0])]).astype(BF16)
            back = move(leaving, flip=1)
            d_first = after(d_first, leaving)
        inputs_grad = input_grads(merged, d_first, w_pieces, w_offsets)

        if fast:
            q_other = after(move(q_parts[0], core=1), inputs_grad, leaving, owned[0][1], owned[1][1])
            q_sum = q_parts[1][:, 0].astype(F32) + q_other[:, 0].astype(F32)
            leaving = owned_sum(1, q_sum) + back[1].astype(F32)
            last_back = move(leaving.astype(BF16), flip=2)
            q_own = q_sum[0]
            for dxy in range(1, 4):
                q_own = q_own + move(q_sum[dxy].astype(BF16), chip=dxy).astype(F32)
            total = owned_sum(0, q_sum) + back[0].astype(F32) + after(last_back, q_own).astype(F32)
            packed_grad = None
            for e in range(nt):
                piece = lax.dynamic_slice_in_dim(q_own, (t_index ^ e) * shard, shard, 0)
                if e:
                    piece = move(piece.astype(BF16), flip=e).astype(F32)
                packed_grad = piece if packed_grad is None else packed_grad + piece
            other = move(total[1], core=1)
            mine = total[0]
            grads = []
            for m in range(3):
                part = slice(m * half, (m + 1) * half)
                grads.append(jnp.where(
                    core == 0,
                    jnp.concatenate([mine[:, part], other[:, part]], axis=1),
                    jnp.concatenate([other[:, part], mine[:, part]], axis=1)))
        else:
            summed = lax.psum_scatter(
                reduced[0][0][0, 0].reshape(width, 3, half * nt), "tensor", scatter_dimension=2, tiled=True)
            spread = jnp.zeros((width, 3, 2 * half), BF16)
            spread = lax.dynamic_update_slice_in_dim(spread, summed.astype(BF16), core * half, 2)
            spread = lax.psum_scatter(spread, "dp", scatter_dimension=0, tiled=True).astype(F32)
            grads = [spread[:, m] for m in range(3)]
            packed_grad = lax.psum_scatter(q_parts[0][0, 0], AXES, scatter_dimension=0, tiled=True)

        return (
            outputs,
            inputs_grad,
            packed_grad[:, : 3 * width],
            packed_grad[:, 3 * width : 4 * width],
            packed_grad[:, 4 * width : 4 * width + 2].T,
            packed_grad[:, 4 * width + 2 : 4 * width + 4].T,
            grads[0],
            grads[1],
            grads[2].T,
        )

    return per_device


def solution(mesh):
    tokens = P(AXES, None)
    both = P("dp", "tensor")
    return jax.shard_map(
        make_per_device(mesh.shape["dp"], mesh.shape["tensor"]),
        mesh=mesh,
        in_specs=(tokens, P("dp", None), tokens, tokens, P(None, AXES), P(None, AXES),
                  both, both, P("tensor", "dp"), tokens),
        out_specs=(tokens, tokens, tokens, tokens, P(None, AXES), P(None, AXES),
                   both, both, P("tensor", "dp")),
        check_vma=False,
    )
```
